32 devices in a mesh: fsdp: 2 (over core), ctx: 4 (over y, x), tp: 4 (over z).
Axes of the slice: x: 2, y: 2, z: 4, core: 2. Of those that a mesh axis runs over, the one named last changes fastest.
Arguments:
- tokens: bfloat16 [4096, 1024], P(('fsdp', 'ctx')), may hold values from -6 to 6
- out_grad: bfloat16 [4096, 1024], P(('fsdp', 'ctx')), may hold values from -6 to 6
- segment_ids: int32 [2, 2048], P('fsdp'), may hold values from 0 to 3, never falling along the last dimension, each value on 1 to 1024 neighbouring positions
- owner_order: int32 [2, 2048], P('fsdp'), may hold values from 0 to 2047, as said below
- attn_gain: bfloat16 [2, 1024], P(None, ('fsdp', 'ctx')), may hold values from 0.5 to 1.5
- w_query: bfloat16 [2, 1024, 1024], P(None, ('fsdp', 'ctx'), 'tp'), may hold values from -0.1875 to 0.1875
- w_key: bfloat16 [2, 1024, 1024], P(None, ('fsdp', 'ctx'), 'tp'), may hold values from -0.1875 to 0.1875
- w_value: bfloat16 [2, 1024, 1024], P(None, ('fsdp', 'ctx'), 'tp'), may hold values from -0.1875 to 0.1875
- w_out: bfloat16 [2, 1024, 1024], P(None, 'tp', ('fsdp', 'ctx')), may hold values from -0.75 to 0.75
- mlp_gain: bfloat16 [2, 1024], P(None, ('fsdp', 'ctx')), may hold values from 0.5 to 1.5
- w_gate: bfloat16 [2, 1024, 2816], P(None, ('fsdp', 'ctx'), 'tp'), may hold values from -0.1875 to 0.1875
- w_up: bfloat16 [2, 1024, 2816], P(None, ('fsdp', 'ctx'), 'tp'), may hold values from -0.1875 to 0.1875
- w_down: bfloat16 [2, 2816, 1024], P(None, 'tp', ('fsdp', 'ctx')), may hold values from -0.109375 to 0.109375
Outputs:
- outputs: bfloat16 [4096, 1024], P(('fsdp', 'ctx'))
- grad_tokens: float32 [4096, 1024], P(('fsdp', 'ctx'))
- grad_attn_gain: float32 [2, 1024], P(None, ('fsdp', 'ctx'))
- grad_w_query: float32 [2, 1024, 1024], P(None, ('fsdp', 'ctx'), 'tp')
- grad_w_key: float32 [2, 1024, 1024], P(None, ('fsdp', 'ctx'), 'tp')
- grad_w_value: float32 [2, 1024, 1024], P(None, ('fsdp', 'ctx'), 'tp')
- grad_w_out: float32 [2, 1024, 1024], P(None, 'tp', ('fsdp', 'ctx'))
- grad_mlp_gain: float32 [2, 1024], P(None, ('fsdp', 'ctx'))
- grad_w_gate: float32 [2, 1024, 2816], P(None, ('fsdp', 'ctx'), 'tp')
- grad_w_up: float32 [2, 1024, 2816], P(None, ('fsdp', 'ctx'), 'tp')
- grad_w_down: float32 [2, 2816, 1024], P(None, 'tp', ('fsdp', 'ctx'))
The draws below stay inside these ranges and needn't reach their ends.
Inputs may be any that keep to these rules, and one draw needn't show every extreme that they name: `segment_ids`: along a row the numbers never fall; each sequence holds 1 to 1024 positions and some sequence holds exactly 1024. `owner_order`: each row is a permutation of the positions of its pack. With n = 4, owner slots c * 512 + s * 512 / n + g (g below 512 / n) hold positions from s * 512 to (s + 1) * 512 - 1.
All inputs are finite; a program needn't handle non-finite values.
Results may differ from the reference program's by a relative error of at most 0.02.
Values may be sent and summed in bfloat16 or wider, within the bound.
No kernel may reach another device: no remote copies, remote signals or barrier semaphores. Data moves between devices by JAX's collectives and lax.ppermute only.
A program may use at most 320 MiB of HBM per device.

```python
import math
import jax
import jax.numpy as jnp
import numpy as np
from jax import lax

D = 1024
HEADS = 16
HEAD = 64
FF = 2816
LAYERS = 2
SEQ_MOST = 1024
TOK_DEV = 512
PACK = 2048
SEGS = 4
TOKENS = 4096
N_FSDP = 2


def draw_owner_order(key, part):
    pack_count = TOKENS // PACK
    ctx_count = PACK // TOK_DEV
    group_rows = TOK_DEV // ctx_count
    keys_list = jax.random.split(key, pack_count * ctx_count)
    shuffled = jax.vmap(lambda sub_key: jax.random.permutation(sub_key, TOK_DEV))(keys_list)
    shuffled = shuffled.astype(jnp.int32).reshape(pack_count, ctx_count, ctx_count, group_rows)
    offsets = (jnp.arange(ctx_count, dtype=jnp.int32) * TOK_DEV)[None, :, None, None]
    placed = jnp.transpose(shuffled + offsets, (0, 2, 1, 3))
    return placed.reshape(pack_count, PACK)


def block_levels(key, extent, shards, smallest, high):
    loudness = 1.0
    for position, parts in shards:
        draws = jax.random.uniform(jax.random.fold_in(jax.random.fold_in(key, 6), position), (parts,), jnp.float32, smallest / len(shards), high / len(shards))
        loudness = loudness * jnp.repeat(jnp.exp(draws), extent[position] // parts).reshape((-1,) + (1,) * (len(extent) - 1 - position))
    return loudness


def length_profile(number_of, total, bound, slope):
    weights = [(1 << 20) // math.isqrt(grade ** slope) + 1 for grade in range(2, number_of + 1)]
    rest, holding = total - bound - (number_of - 1), [1] * (number_of - 1)
    while rest > 0:
        free = [i for i in range(number_of - 1) if holding[i] < bound]
        pool, remaining = sum([weights[i] for i in free]), rest
        for i in free:
            more = min(bound - holding[i], max(1, remaining * weights[i] // pool), rest)
            holding[i] = holding[i] + more
            rest = rest - more
    return np.array([bound] + holding)


def ragged(own_key, number_of, total, limit, skew):
    if number_of == 2:
        one = jax.random.randint(own_key, (), max(1, total - limit), min(limit, total - 1) + 1)
        return jnp.stack([one, total - one])
    sizes = jnp.asarray(length_profile(number_of, total, limit, skew), jnp.int32)
    pairs = (number_of - 1) // 2
    source_of, taker = sizes[1:1 + 2 * pairs:2], sizes[2:2 + 2 * pairs:2]
    slack = jnp.minimum(source_of - 1, limit - taker)
    shifted = jax.random.randint(jax.random.fold_in(own_key, 1), (pairs,), 0, 1 << 20) % (slack + 1)
    sizes = sizes.at[1:1 + 2 * pairs:2].set(source_of - shifted).at[2:2 + 2 * pairs:2].set(taker + shifted)
    return sizes[jax.random.permutation(jax.random.fold_in(own_key, 2), number_of)]


def gaussian(own_key, dims, deviation, most, shards=(), kind=jnp.bfloat16):
    entries = deviation * jax.random.normal(own_key, dims, jnp.float32)
    if shards:
        entries = entries * block_levels(own_key, dims, shards, -0.22, 0.18)
    return jnp.clip(entries, -most, most).astype(kind)


def setup_inputs(seed: int = 0) -> dict:
    arg_keys = jax.random.split(jax.random.key(seed), 14)
    tokens = gaussian(arg_keys[0], (TOKENS, D), 1.0, 6.0, ((0, 8),))
    out_grad = gaussian(arg_keys[1], (TOKENS, D), 1.0, 6.0, ((0, 8),))
    segment_ids = jax.vmap(lambda own: jnp.searchsorted(jnp.cumsum(ragged(own, SEGS, PACK, SEQ_MOST, 1)), jnp.arange(PACK), side="right"))(jax.random.split(arg_keys[2], N_FSDP)).reshape((N_FSDP, PACK)).astype(jnp.int32)
    owner_order = draw_owner_order(jax.random.fold_in(arg_keys[13], 71), 0)
    attn_gain = jnp.clip(1.0 + 0.1 * jax.random.normal(arg_keys[4], (LAYERS, D), jnp.float32), 0.5, 1.5).astype(jnp.bfloat16)
    w_query = gaussian(arg_keys[5], (LAYERS, D, D), D ** -0.5, 0.1875, ((1, 8), (2, 4)))
    w_key = gaussian(arg_keys[6], (LAYERS, D, D), D ** -0.5, 0.1875, ((1, 8), (2, 4)))
    w_value = gaussian(arg_keys[7], (LAYERS, D, D), D ** -0.5, 0.1875, ((1, 8), (2, 4)))
    w_out = gaussian(arg_keys[8], (LAYERS, D, D), (D // 16) ** -0.5, 0.75, ((1, 4), (2, 8)))
    mlp_gain = jnp.clip(1.0 + 0.1 * jax.random.normal(arg_keys[9], (LAYERS, D), jnp.float32), 0.5, 1.5).astype(jnp.bfloat16)
    w_gate = gaussian(arg_keys[10], (LAYERS, D, FF), D ** -0.5, 0.1875, ((1, 8), (2, 4)))
    w_up = gaussian(arg_keys[11], (LAYERS, D, FF), D ** -0.5, 0.1875, ((1, 8), (2, 4)))
    w_down = gaussian(arg_keys[12], (LAYERS, FF, D), FF ** -0.5, 0.109375, ((1, 4), (2, 8)))
    return {"tokens": tokens, "out_grad": out_grad, "segment_ids": segment_ids, "owner_order": owner_order, "attn_gain": attn_gain, "w_query": w_query, "w_key": w_key, "w_value": w_value, "w_out": w_out, "mlp_gain": mlp_gain, "w_gate": w_gate, "w_up": w_up, "w_down": w_down}


EPS = 1e-05
THETA = 10000.0
NEG = -1e+30

@jax.custom_vjp
def low(v):
    return lax.optimization_barrier(v.astype(jnp.bfloat16)).astype(jnp.float32)

@jax.custom_vjp
def low_back(v):
    return v

def low_keep(v):
    return (low(v), None)

def low_pass(kept, grad):
    return (grad,)

def back_keep(v):
    return (v, None)

def back_low(kept, grad):
    return (low(grad),)
low.defvjp(low_keep, low_pass)
low_back.defvjp(back_keep, back_low)

def seq_positions(segment):
    index_all = jnp.arange(segment.shape[0], dtype=jnp.int32)
    run_start = jnp.concatenate([jnp.ones((1,), dtype=bool), segment[1:] != segment[:-1]])
    run_first = lax.cummax(jnp.where(run_start, index_all, jnp.zeros_like(index_all)), axis=0)
    return index_all - run_first

def rope_tables(positions):
    frequency = THETA ** (-(jnp.arange(HEAD // 2, dtype=jnp.float32) * 2.0 / HEAD))
    angles = positions.astype(jnp.float32)[:, None] * frequency[None, :]
    return (jnp.cos(angles), jnp.sin(angles))

def rotate(values, cos_tab, sine_tab):
    row_count = values.shape[0]
    by_head = values.reshape(row_count, -1, HEAD)
    first_half = by_head[:, :, :HEAD // 2]
    second_half = by_head[:, :, HEAD // 2:]
    cos_wide = cos_tab[:, None, :]
    sine_wide = sine_tab[:, None, :]
    turned = jnp.concatenate([first_half * cos_wide - second_half * sine_wide, second_half * cos_wide + first_half * sine_wide], axis=2)
    return turned.reshape(row_count, -1)

def rms_norm(stream, gain):
    return stream * lax.rsqrt(lax.optimization_barrier(jnp.mean(stream * stream, axis=-1, keepdims=True)) + EPS) * gain

def matmul_high(left, right):
    return jnp.dot(left, right, precision=lax.Precision.HIGHEST)

def attention(queries, keys_all, values_all, segment):
    block_rows = 512 if PACK % 512 == 0 else PACK
    key_window = min(PACK, block_rows + SEQ_MOST)
    inv_root = HEAD ** (-0.5)
    query_heads = queries.reshape(PACK, HEADS, HEAD)
    key_heads = keys_all.reshape(PACK, HEADS, HEAD)
    value_heads = values_all.reshape(PACK, HEADS, HEAD)

    def one_block(block_start):
        key_start = jnp.clip(block_start + block_rows - key_window, 0, PACK - key_window).astype(jnp.int32)
        query_rows = lax.dynamic_slice_in_dim(query_heads, block_start, block_rows, 0)
        key_rows = lax.dynamic_slice_in_dim(key_heads, key_start, key_window, 0)
        value_rows = lax.dynamic_slice_in_dim(value_heads, key_start, key_window, 0)
        scores = jnp.einsum('qhd,khd->hqk', query_rows, key_rows, precision=lax.Precision.HIGHEST) * inv_root
        scores = low_back(scores)
        query_index = block_start + jnp.arange(block_rows, dtype=jnp.int32)
        key_index = key_start + jnp.arange(key_window, dtype=jnp.int32)
        seg_query = lax.dynamic_slice_in_dim(segment, block_start, block_rows, 0)
        seg_key = lax.dynamic_slice_in_dim(segment, key_start, key_window, 0)
        allowed = (seg_query[:, None] == seg_key[None, :]) & (key_index[None, :] <= query_index[:, None])
        scores = jnp.where(allowed[None], scores, NEG)
        row_peak = lax.optimization_barrier(jnp.max(scores, axis=2, keepdims=True))
        exp_scores = jnp.exp(scores - row_peak)
        probs = low(exp_scores / lax.optimization_barrier(jnp.sum(exp_scores, axis=2, keepdims=True)))
        return jnp.einsum('hqk,khd->qhd', probs, value_rows, precision=lax.Precision.HIGHEST)
    block_starts = jnp.arange(PACK // block_rows, dtype=jnp.int32) * block_rows
    block_outs = lax.map(jax.checkpoint(one_block), block_starts)
    return block_outs.reshape(PACK, HEADS * HEAD)

def forward(stream, params, segment):
    gains_attn, wq_all, wk_all, wv_all, wo_all, gains_mlp, wg_all, wu_all, wd_all = params
    positions = seq_positions(segment)
    cos_tab, sine_tab = rope_tables(positions)
    first_values = None
    for level_idx in range(LAYERS):
        normed = low(rms_norm(stream, gains_attn[level_idx]))
        queries = low(rotate(low_back(matmul_high(normed, wq_all[level_idx])), cos_tab, sine_tab))
        keys_own = low(rotate(low_back(matmul_high(normed, wk_all[level_idx])), cos_tab, sine_tab))
        values_pre = low_back(matmul_high(normed, wv_all[level_idx]))
        if first_values is None:
            first_values = values_pre
            mixed_values = values_pre
        else:
            mixed_values = 0.5 * values_pre + 0.5 * first_values
        attended = low(low_back(attention(queries, keys_own, low(mixed_values), segment)))
        stream = stream + low_back(matmul_high(attended, wo_all[level_idx]))
        normed_mlp = low(rms_norm(stream, gains_mlp[level_idx]))
        gate_pre = low_back(matmul_high(normed_mlp, wg_all[level_idx]))
        upward = low_back(matmul_high(normed_mlp, wu_all[level_idx]))
        hidden = low(gate_pre * jax.nn.sigmoid(gate_pre) * upward)
        stream = stream + low_back(matmul_high(hidden, wd_all[level_idx]))
    return stream

def reference(tokens, out_grad, segment_ids, owner_order, attn_gain, w_query, w_key, w_value, w_out, mlp_gain, w_gate, w_up, w_down):
    params = tuple((weight.astype(jnp.float32) for weight in (attn_gain, w_query, w_key, w_value, w_out, mlp_gain, w_gate, w_up, w_down)))
    pack_count = TOKENS // PACK
    stream_packs = tokens.astype(jnp.float32).reshape(pack_count, PACK, D)
    grad_packs = out_grad.astype(jnp.float32).reshape(pack_count, PACK, D)

    def one_pack(totals, items):
        stream, grad_out, segment, order_row = items
        result, pull_back = jax.vjp(lambda stream_in, param_in: forward(stream_in, param_in, segment), stream, params)
        grad_stream, grad_params = pull_back(grad_out)
        totals = tuple((left + right for left, right in zip(totals, grad_params)))
        return (totals, (result.astype(jnp.bfloat16), grad_stream[order_row.astype(jnp.int32)]))
    zero_grads = tuple((jnp.zeros_like(weight) for weight in params))
    totals, (out_packs, grad_stream_packs) = lax.scan(one_pack, zero_grads, (stream_packs, grad_packs, segment_ids, owner_order))
    return (out_packs.reshape(TOKENS, D), grad_stream_packs.reshape(TOKENS, D), totals[0], totals[1], totals[2], totals[3], totals[4], totals[5], totals[6], totals[7], totals[8])
```

```python
import jax
import jax.numpy as jnp
from jax import lax
from jax.sharding import PartitionSpec as P

HEAD = 64
HALF = HEAD // 2
LAYERS = 2
EPS = 1e-05
THETA = 10000.0
NEG = -1e30
BF = jnp.bfloat16
F32 = jnp.float32


def dot(left, right, left_dim, right_dim):
    return lax.dot_general(
        left, right, (((left_dim,), (right_dim,)), ((), ())), preferred_element_type=F32
    )


class Plan:
    def __init__(self):
        self.fsdp = lax.axis_size("fsdp")
        self.ctx = lax.axis_size("ctx")
        self.tp = lax.axis_size("tp")
        self.high = self.fsdp // 2
        f = lax.axis_index("fsdp")
        z = lax.axis_index("tp")
        self.c = f % 2
        self.fh = f // 2
        self.x = lax.axis_index("ctx")
        self.zl = z % 2
        self.zp = z // 2
        self.ci = self.x % 4

    def core(self, value):
        return lax.ppermute(value, "fsdp", [(i, i ^ 1) for i in range(self.fsdp)])

    def near(self, value):
        return lax.ppermute(value, "tp", [(i, i ^ 1) for i in range(self.tp)])

    def far(self, value):
        return lax.ppermute(value, "tp", [(i, i ^ 2) for i in range(self.tp)])

    def side(self, value, k):
        return lax.ppermute(value, "ctx", [(i, i ^ k) for i in range(self.ctx)])

    def peer(self, value, k):
        kh, kc = divmod(k, self.ctx)
        if k == 0:
            return value
        if kh == 0:
            return self.side(value, kc)
        pairs = []
        for f in range(self.fsdp):
            for i in range(self.ctx):
                pairs.append((f * self.ctx + i, (f ^ (2 * kh)) * self.ctx + (i ^ kc)))
        return lax.ppermute(value, ("fsdp", "ctx"), pairs)

    @property
    def peers(self):
        return self.high * self.ctx


def flip_blocks(value, axis, index):
    count = value.shape[axis]
    bit = 1
    while bit < count:
        shape = value.shape
        split = value.reshape(shape[:axis] + (count // (2 * bit), 2, bit) + shape[axis + 1 :])
        turned = jnp.flip(split, axis=axis + 1).reshape(shape)
        value = jnp.where((index & bit) != 0, turned, value)
        bit *= 2
    return value


def to_peer_order(plan, rows):
    count, width = rows.shape
    grid = rows.reshape(count, plan.high, 2, plan.ctx, width // (2 * plan.peers))
    grid = jnp.swapaxes(grid, 2, 3)
    grid = flip_blocks(grid, 2, plan.x)
    grid = flip_blocks(grid, 1, plan.fh)
    return grid.reshape(count, width)


def from_peer_order(plan, rows):
    count, width = rows.shape
    grid = rows.reshape(count, plan.high, plan.ctx, 2, width // (2 * plan.peers))
    grid = flip_blocks(grid, 2, plan.x)
    grid = flip_blocks(grid, 1, plan.fh)
    grid = jnp.swapaxes(grid, 2, 3)
    return grid.reshape(count, width)


def ordered(first_is_own, own, other, axis):
    return jnp.where(
        first_is_own,
        jnp.concatenate([own, other], axis=axis),
        jnp.concatenate([other, own], axis=axis),
    )


def gather_rows(plan, rows):
    pair = ordered(plan.zl == 0, rows, plan.near(rows), 0)
    return ordered(plan.c == 0, pair, plan.core(pair), 0)


def pick(flag, value):
    half = value.shape[0] // 2
    low, high = value[:half], value[half:]
    return (jnp.where(flag == 0, low, high), jnp.where(flag == 0, high, low))


def sum_rows(plan, partial):
    mine, theirs = pick(plan.c, partial)
    pair = mine + plan.core(theirs.astype(BF)).astype(F32)
    mine, theirs = pick(plan.zl, pair)
    return mine + plan.near(theirs.astype(BF)).astype(F32)


def gather_weight(plan, halves):
    keep = jnp.where(plan.c == 0, halves[0], halves[1])
    send = jnp.where(plan.c == 0, halves[1], halves[0])
    own = ordered(plan.c == 0, keep, plan.core(send), 1)
    other = plan.far(own)
    own_parts = [plan.peer(own, k) for k in range(plan.peers)]
    other_parts = [plan.peer(other, k) for k in range(plan.peers)]
    return jnp.concatenate(
        [jnp.concatenate(own_parts, axis=1), jnp.concatenate(other_parts, axis=1)], axis=0
    )


def scatter_grad(plan, grad):
    width = grad.shape[1] // plan.peers
    total = grad[:, :width].astype(F32)
    for k in range(1, plan.peers):
        piece = grad[:, k * width : (k + 1) * width].astype(BF)
        total = total + plan.peer(piece, k).astype(F32)
    half = total.shape[0] // 2
    own = total[:half] + plan.far(total[half:].astype(BF)).astype(F32)
    left, right = own[:, : width // 2], own[:, width // 2 :]
    mine = jnp.where(plan.c == 0, left, right)
    theirs = jnp.where(plan.c == 0, right, left)
    got = plan.core(theirs.astype(BF)).astype(F32)
    return jnp.where(plan.c == 0, jnp.stack([mine, got]), jnp.stack([got, mine]))


def split_hidden(weight):
    return weight.reshape(2, weight.shape[0] // 2, weight.shape[1])


def turn(values, cos_tab, sine_tab):
    first, second = values[..., :HALF, :], values[..., HALF:, :]
    return jnp.concatenate(
        [first * cos_tab - second * sine_tab, second * cos_tab + first * sine_tab], axis=-2
    )


def to_heads(plan, values):
    got = [lax.dynamic_index_in_dim(values, plan.ci, 0, False)]
    for k in range(1, 4):
        got.append(plan.side(lax.dynamic_index_in_dim(values, plan.ci ^ k, 0, False), k))
    blocks = flip_blocks(jnp.stack(got), 0, plan.ci)
    blocks = jnp.moveaxis(blocks, 0, -2)
    return blocks.reshape(blocks.shape[:-2] + (-1,))


def from_heads(plan, values):
    blocks = jnp.moveaxis(values.reshape(values.shape[:-1] + (4, -1)), -2, 0)
    got = [lax.dynamic_index_in_dim(blocks, plan.ci, 0, False)]
    for k in range(1, 4):
        got.append(plan.side(lax.dynamic_index_in_dim(blocks, plan.ci ^ k, 0, False), k))
    return flip_blocks(jnp.stack(got), 0, plan.ci)


def far_keys(plan, values):
    width = values.shape[-1]
    parts = plan.ctx // 4
    if parts == 1:
        return values
    got = [values] + [plan.side(values, 4 * k) for k in range(1, parts)]
    blocks = flip_blocks(jnp.stack(got), 0, plan.x // 4)
    return jnp.moveaxis(blocks, 0, -2).reshape(values.shape[:-1] + (parts * width,))


def far_keys_sum(plan, values):
    parts = plan.ctx // 4
    if parts == 1:
        return values
    blocks = jnp.moveaxis(values.reshape(values.shape[:-1] + (parts, -1)), -2, 0)
    blocks = flip_blocks(blocks, 0, plan.x // 4)
    total = blocks[0]
    for k in range(1, parts):
        total = total + plan.side(blocks[k], 4 * k)
    return total


def attend(queries, keys, values, allowed):
    scores = dot(keys, queries, 0, 0) * HEAD ** (-0.5)
    scores = jnp.where(allowed, scores, NEG)
    peak = jnp.max(scores, axis=0, keepdims=True)
    exp_scores = jnp.exp(scores - peak)
    total = jnp.sum(exp_scores, axis=0, keepdims=True)
    probs = (exp_scores / total).astype(BF)
    return (dot(values, probs, 1, 0), peak + jnp.log(total))


def attend_back(queries, keys, values, allowed, log_total, grad_out):
    scores = dot(keys, queries, 0, 0) * HEAD ** (-0.5)
    scores = jnp.where(allowed, scores, NEG)
    probs = jnp.exp(scores - log_total)
    grad_probs = dot(values, grad_out, 0, 0)
    inner = jnp.sum(probs * grad_probs, axis=0, keepdims=True)
    grad_scores = (probs * (grad_probs - inner)).astype(BF)
    return (
        dot(keys, grad_scores, 1, 0) * HEAD ** (-0.5),
        dot(queries, grad_scores, 1, 1) * HEAD ** (-0.5),
        dot(grad_out, probs.astype(BF), 1, 1),
    )


def norm_scale(stream):
    return lax.rsqrt(jnp.mean(stream * stream, axis=-1, keepdims=True) + EPS)


def norm_back(stream, scale, gain, grad_normed):
    weighted = grad_normed * gain
    grad_gain = jnp.sum(grad_normed * stream * scale, axis=0, keepdims=True)
    grad_stream = scale * weighted - stream * scale**3 * jnp.mean(
        weighted * stream, axis=1, keepdims=True
    )
    return (grad_gain, grad_stream)


def local(
    tokens,
    out_grad,
    segment_ids,
    owner_order,
    attn_gain,
    w_query,
    w_key,
    w_value,
    w_out,
    mlp_gain,
    w_gate,
    w_up,
    w_down,
):
    plan = Plan()
    tok_rows = tokens.shape[0]
    part_rows = tok_rows // 4
    model = tokens.shape[1]

    gains = jnp.concatenate([attn_gain, mlp_gain], axis=0)
    gains = jnp.concatenate([gains, jnp.zeros((12, gains.shape[1]), BF)], axis=0)
    full = []
    for level in range(LAYERS):
        parts = []
        qkv = jnp.stack(
            [split_hidden(w[level].T) for w in (w_query, w_key, w_value)], axis=1
        )
        qkv = qkv.reshape(2, -1, qkv.shape[-1])
        parts.append(gather_weight(plan, qkv))
        for w in (w_out[level], w_gate[level].T, w_up[level].T, w_down[level]):
            parts.append(gather_weight(plan, split_hidden(w)))
        full.append(parts)
    gain_pair = ordered(plan.c == 0, gains, plan.core(gains), 1)
    gain_full = jnp.concatenate(
        [plan.peer(gain_pair, k) for k in range(plan.peers)], axis=1
    ).astype(F32)

    part = plan.c * 2 + plan.zl
    other_part = (1 - plan.c) * 2 + plan.zl

    def own_rows(array):
        mine = lax.dynamic_slice_in_dim(array, part * part_rows, part_rows, 0)
        sent = lax.dynamic_slice_in_dim(array, other_part * part_rows, part_rows, 0)
        got = plan.core(sent)
        return to_peer_order(plan, jnp.where(plan.c == plan.zp, mine, got))

    stream = own_rows(tokens).astype(F32)
    grad_stream = own_rows(out_grad).astype(F32)

    segment = segment_ids
    segment = jnp.where(plan.c == plan.zp, segment, plan.core(segment))[0]
    pack = segment.shape[0]
    index_all = jnp.arange(pack, dtype=jnp.int32)
    run_start = jnp.concatenate([jnp.ones((1,), dtype=bool), segment[1:] != segment[:-1]])
    run_first = lax.cummax(jnp.where(run_start, index_all, jnp.zeros_like(index_all)), axis=0)
    positions = (index_all - run_first).astype(F32)
    frequency = THETA ** (-(jnp.arange(HALF, dtype=F32) * 2.0 / HEAD))
    angles = frequency[:, None] * positions[None, :]
    cos_all, sine_all = jnp.cos(angles), jnp.sin(angles)
    cos_own = lax.dynamic_slice_in_dim(cos_all, plan.x * tok_rows, tok_rows, 1)
    sine_own = lax.dynamic_slice_in_dim(sine_all, plan.x * tok_rows, tok_rows, 1)
    first_query = (plan.x // 4) * (4 * tok_rows)
    cos_query = lax.dynamic_slice_in_dim(cos_all, first_query, 4 * tok_rows, 1)
    sine_query = lax.dynamic_slice_in_dim(sine_all, first_query, 4 * tok_rows, 1)
    query_index = lax.dynamic_slice_in_dim(index_all, first_query, 4 * tok_rows, 0)
    query_first = lax.dynamic_slice_in_dim(run_first, first_query, 4 * tok_rows, 0)
    allowed = (index_all[:, None] <= query_index[None, :]) & (
        index_all[:, None] >= query_first[None, :]
    )

    kept = []
    first_values = None
    for level in range(LAYERS):
        w_qkv, w_o, w_g, w_u, w_d = full[level]
        scale_attn = norm_scale(stream)
        normed = (stream * scale_attn * gain_full[level : level + 1]).astype(BF)
        normed_all = gather_rows(plan, normed)
        qkv = dot(w_qkv, normed_all, 1, 1).reshape(2, 3, 2, HEAD, tok_rows)
        query = turn(qkv[:, 0], cos_own, sine_own).astype(BF)
        key = turn(qkv[:, 1], cos_own, sine_own).astype(BF)
        if level == 0:
            first_values = qkv[:, 2]
            mixed = first_values
        else:
            mixed = 0.5 * qkv[:, 2] + 0.5 * first_values
        heads = jnp.stack([query, key, mixed.astype(BF)], axis=2)
        heads = heads.reshape(4, 3, HEAD, tok_rows)
        heads = to_heads(plan, heads)
        keys_values = far_keys(plan, heads[1:])
        out, log_total = attend(heads[0], keys_values[0], keys_values[1], allowed)
        attended = from_heads(plan, out.astype(BF)).reshape(4 * HEAD, tok_rows)
        middle = stream + sum_rows(plan, dot(attended, w_o, 0, 0))
        scale_mlp = norm_scale(middle)
        normed_mlp = (middle * scale_mlp * gain_full[2 + level : 3 + level]).astype(BF)
        normed_mlp_all = gather_rows(plan, normed_mlp)
        gate = dot(normed_mlp_all, w_g, 1, 1)
        upward = dot(normed_mlp_all, w_u, 1, 1)
        hidden = (gate * jax.nn.sigmoid(gate) * upward).astype(BF)
        result = middle + sum_rows(plan, dot(hidden, w_d, 1, 0))
        kept.append(
            (
                stream,
                scale_attn,
                normed_all,
                heads[0],
                keys_values,
                log_total,
                attended,
                middle,
                scale_mlp,
                normed_mlp_all,
                gate,
                upward,
                hidden,
            )
        )
        stream = result

    def to_pack(rows):
        block = gather_rows(plan, rows)
        pairs = []
        for f in range(plan.fsdp):
            for z in range(plan.tp):
                if f % 2 == z // 2:
                    pairs.append((f * plan.tp + z, f * plan.tp + (z ^ 2)))
        got = lax.ppermute(block, ("fsdp", "tp"), pairs)
        return jnp.where(plan.c == plan.zp, block, got)

    outputs = to_pack(from_peer_order(plan, stream.astype(BF)))

    grads = [None] * LAYERS
    gain_rows = [None] * (2 * LAYERS)
    carried = None
    for level in reversed(range(LAYERS)):
        (
            stream,
            scale_attn,
            normed_all,
            query,
            keys_values,
            log_total,
            attended,
            middle,
            scale_mlp,
            normed_mlp_all,
            gate,
            upward,
            hidden,
        ) = kept[level]
        w_qkv, w_o, w_g, w_u, w_d = full[level]
        branch = gather_rows(plan, grad_stream.astype(BF))
        grad_hidden = dot(branch, w_d, 1, 1)
        sigma = jax.nn.sigmoid(gate)
        grad_gate = (grad_hidden * upward * sigma * (1.0 + gate * (1.0 - sigma))).astype(BF)
        grad_up = (grad_hidden * gate * sigma).astype(BF)
        grad_normed = sum_rows(plan, dot(grad_gate, w_g, 1, 0) + dot(grad_up, w_u, 1, 0))
        grad_down = scatter_grad(plan, dot(hidden, branch, 0, 0))
        grad_wg = scatter_grad(plan, dot(grad_gate, normed_mlp_all, 0, 0))
        grad_wu = scatter_grad(plan, dot(grad_up, normed_mlp_all, 0, 0))
        gain_rows[2 + level], through = norm_back(
            middle, scale_mlp, gain_full[2 + level : 3 + level], grad_normed
        )
        grad_middle = grad_stream + through
        branch = gather_rows(plan, grad_middle.astype(BF))
        grad_wo = scatter_grad(plan, dot(attended, branch, 1, 0))
        grad_attended = dot(w_o, branch, 1, 1).astype(BF)
        grad_attended = to_heads(plan, grad_attended.reshape(4, HEAD, tok_rows))
        grad_q, grad_k, grad_v = attend_back(
            query, keys_values[0], keys_values[1], allowed, log_total, grad_attended
        )
        grad_k = far_keys_sum(plan, grad_k)
        grad_v = far_keys_sum(plan, grad_v)
        grad_q = turn(grad_q, cos_query, -sine_query).astype(BF)
        grad_k = turn(grad_k, cos_query, -sine_query).astype(BF)
        if level > 0:
            half = 0.5 * grad_v
            carried = half if carried is None else carried + half
            grad_v = half.astype(BF)
        else:
            grad_v = (grad_v + carried).astype(BF)
        grad_heads = from_heads(plan, jnp.stack([grad_q, grad_k, grad_v]))
        grad_qkv = grad_heads.reshape(2, 2, 3, HEAD, tok_rows)
        grad_qkv = jnp.swapaxes(grad_qkv, 1, 2).reshape(-1, tok_rows)
        grad_wqkv = scatter_grad(plan, dot(grad_qkv, normed_all, 1, 0))
        grad_normed = sum_rows(plan, dot(grad_qkv, w_qkv, 0, 0))
        gain_rows[level], through = norm_back(
            stream, scale_attn, gain_full[level : level + 1], grad_normed
        )
        grad_stream = grad_middle + through
        hidden_half = grad_wqkv.shape[1] // 3
        qkv_split = grad_wqkv.reshape(2, 3, hidden_half, -1)
        qkv_split = [qkv_split[:, i].reshape(2 * hidden_half, -1).T for i in range(3)]

        def whole(halves):
            return halves.reshape(-1, halves.shape[-1])

        grads[level] = (
            qkv_split[0],
            qkv_split[1],
            qkv_split[2],
            whole(grad_wo),
            whole(grad_wg).T,
            whole(grad_wu).T,
            whole(grad_down),
        )

    gain_sum = jnp.concatenate(gain_rows + [jnp.zeros((4, model), F32)], axis=0)
    width = model // plan.peers
    total = gain_sum[:, :width]
    for k in range(1, plan.peers):
        total = total + plan.peer(gain_sum[:, k * width : (k + 1) * width], k)
    total = total + plan.far(total)
    total = total + plan.near(total)
    left, right = total[:, : width // 2], total[:, width // 2 :]
    mine = jnp.where(plan.c == 0, left, right)
    theirs = jnp.where(plan.c == 0, right, left)
    total = mine + plan.core(theirs)

    grad_block = to_pack(from_peer_order(plan, grad_stream.astype(BF)))
    group_rows = tok_rows // plan.ctx
    owner_grid = owner_order[0].reshape(plan.ctx, plan.ctx, group_rows)
    local_rows = (
        lax.dynamic_index_in_dim(owner_grid, plan.x, 1, False) - plan.x * tok_rows
    ).reshape(tok_rows)
    grad_tokens = lax.all_to_all(
        grad_block[local_rows], "ctx", split_axis=0, concat_axis=0, tiled=True
    ).astype(F32)

    stacked = [jnp.stack([grads[level][i] for level in range(LAYERS)]) for i in range(7)]
    return (
        outputs,
        grad_tokens,
        total[:2],
        stacked[0],
        stacked[1],
        stacked[2],
        stacked[3],
        total[2:4],
        stacked[4],
        stacked[5],
        stacked[6],
    )


def solution(mesh):
    columns = P(None, ("fsdp", "ctx"), "tp")
    rows = P(None, "tp", ("fsdp", "ctx"))
    gain = P(None, ("fsdp", "ctx"))
    tokens = P(("fsdp", "ctx"), None)
    return jax.shard_map(
        local,
        mesh=mesh,
        in_specs=(
            tokens,
            tokens,
            P("fsdp", None),
            P("fsdp", None),
            gain,
            columns,
            columns,
            columns,
            rows,
            gain,
            columns,
            columns,
            rows,
        ),
        out_specs=(
            tokens,
            tokens,
            gain,
            columns,
            columns,
            columns,
            rows,
            gain,
            columns,
            columns,
            rows,
        ),
        check_vma=False,
    )
```

```python
import functools

import jax
import jax.numpy as jnp
from jax import lax
from jax.experimental import pallas as pl
from jax.experimental.pallas import tpu as pltpu
from jax.sharding import PartitionSpec as P

HEAD = 64
HALF = HEAD // 2
LAYERS = 2
EPS = 1e-05
THETA = 10000.0
NEG = -1e30
BF = jnp.bfloat16
F32 = jnp.float32
IN_VMEM = pl.BlockSpec(memory_space=pltpu.VMEM)
IN_SMEM = pl.BlockSpec(memory_space=pltpu.SMEM)


def dot(left, right, left_dim, right_dim):
    return lax.dot_general(
        left, right, (((left_dim,), (right_dim,)), ((), ())), preferred_element_type=F32
    )


def mm(left, right):
    return jnp.dot(left, right, preferred_element_type=F32)


class Plan:
    def __init__(self):
        self.fsdp = lax.axis_size("fsdp")
        self.ctx = lax.axis_size("ctx")
        self.tp = lax.axis_size("tp")
        self.high = self.fsdp // 2
        f = lax.axis_index("fsdp")
        z = lax.axis_index("tp")
        self.c = f % 2
        self.fh = f // 2
        self.x = lax.axis_index("ctx")
        self.zl = z % 2
        self.zp = z // 2
        self.ci = self.x % 4
        self.part = self.c * 2 + self.zl
        self.peers = self.high * self.ctx

    def core(self, value):
        return lax.ppermute(value, "fsdp", [(i, i ^ 1) for i in range(self.fsdp)])

    def near(self, value):
        return lax.ppermute(value, "tp", [(i, i ^ 1) for i in range(self.tp)])

    def far(self, value):
        return lax.ppermute(value, "tp", [(i, i ^ 2) for i in range(self.tp)])

    def side(self, value, k):
        return lax.ppermute(value, "ctx", [(i, i ^ k) for i in range(self.ctx)])

    def high_fsdp(self, value, k):
        return lax.ppermute(value, "fsdp", [(i, i ^ (2 * k)) for i in range(self.fsdp)])


def flip_list(blocks, index):
    bit = 1
    while bit < len(blocks):
        on = (index & bit) != 0
        blocks = [jnp.where(on, blocks[i ^ bit], blocks[i]) for i in range(len(blocks))]
        bit *= 2
    return blocks


def place(blocks, index, axis):
    width = blocks[0].shape[axis]
    shape = list(blocks[0].shape)
    shape[axis] = width * len(blocks)
    full = jnp.zeros(shape, blocks[0].dtype)
    for i, block in enumerate(blocks):
        full = lax.dynamic_update_slice_in_dim(full, block, (index ^ i) * width, axis)
    return full


def to_block_order(plan, rows):
    width = rows.shape[1] // (2 * plan.peers)
    parts = []
    for h in range(plan.high):
        for x in range(plan.ctx):
            for c in range(2):
                start = ((h * 2 + c) * plan.ctx + x) * width
                parts.append(rows[:, start : start + width])
    return jnp.concatenate(parts, axis=1)


def from_block_order(plan, rows):
    width = rows.shape[1] // (2 * plan.peers)
    parts = []
    for h in range(plan.high):
        for c in range(2):
            for x in range(plan.ctx):
                start = ((h * plan.ctx + x) * 2 + c) * width
                parts.append(rows[:, start : start + width])
    return jnp.concatenate(parts, axis=1)


def gather_rows(plan, rows):
    pair = jnp.concatenate([rows, plan.near(rows)], axis=0)
    return jnp.concatenate([pair, plan.core(pair)], axis=0)


def sum_rows(plan, partial):
    half = partial.shape[0] // 2
    pair = partial[:half] + plan.core(partial[half:].astype(BF)).astype(F32)
    half = half // 2
    return pair[:half] + plan.near(pair[half:].astype(BF)).astype(F32)


def natural_rows(plan, rows):
    count = rows.shape[0] // 4
    parts = [
        lax.dynamic_slice_in_dim(rows, (plan.part ^ i) * count, count, 0) for i in range(4)
    ]
    return jnp.concatenate(parts, axis=0)


def own_columns(plan, halves):
    keep = lax.dynamic_index_in_dim(halves, plan.c, 0, False)
    got = plan.core(lax.dynamic_index_in_dim(halves, 1 - plan.c, 0, False))
    return jnp.where(
        plan.c == 0,
        jnp.concatenate([keep, got], axis=1),
        jnp.concatenate([got, keep], axis=1),
    )


def all_columns(plan, rows, direct):
    if direct and plan.peers == 4:
        return place([rows] + [plan.side(rows, k) for k in range(1, 4)], plan.x, 1)
    full = lax.all_gather(rows, "ctx", axis=1, tiled=True)
    if plan.high > 1:
        parts = [full] + [plan.high_fsdp(full, k) for k in range(1, plan.high)]
        full = place(parts, plan.fh, 1)
    return full


def columns_sum(plan, grad, direct):
    if plan.high > 1:
        width = grad.shape[1] // plan.high
        parts = [
            lax.dynamic_slice_in_dim(grad, (plan.fh ^ k) * width, width, 1)
            for k in range(plan.high)
        ]
        grad = parts[0]
        for k in range(1, plan.high):
            grad = grad + plan.high_fsdp(parts[k], k)
    if direct and plan.ctx == 4:
        width = grad.shape[1] // 4
        parts = [
            lax.dynamic_slice_in_dim(grad, (plan.x ^ k) * width, width, 1) for k in range(4)
        ]
        total = parts[0].astype(F32)
        for k in range(1, 4):
            total = total + plan.side(parts[k], k).astype(F32)
        return total
    return lax.psum_scatter(grad, "ctx", scatter_dimension=1, tiled=True).astype(F32)


def gather_weights(plan, groups, direct):
    own = own_columns(plan, jnp.concatenate(groups, axis=1))
    far = plan.far(own)
    parts = []
    start = 0
    for group in groups:
        rows = group.shape[1]
        parts += [own[start : start + rows], far[start : start + rows]]
        start += rows
    return all_columns(plan, jnp.concatenate(parts, axis=0), direct)


def scatter_grads(plan, grads, direct):
    total = columns_sum(plan, jnp.concatenate(grads, axis=0), direct)
    mine, far = [], []
    start = 0
    for grad in grads:
        rows = grad.shape[0] // 2
        mine.append(total[start : start + rows])
        far.append(total[start + rows : start + 2 * rows])
        start += 2 * rows
    got = plan.far(jnp.concatenate(far, axis=0).astype(BF)).astype(F32)
    own = jnp.concatenate(mine, axis=0) + got
    width = own.shape[1]
    left, right = own[:, : width // 2], own[:, width // 2 :]
    kept = jnp.where(plan.c == 0, left, right)
    got = plan.core(jnp.where(plan.c == 0, right, left).astype(BF)).astype(F32)
    low = jnp.where(plan.c == 0, kept, got)
    high = jnp.where(plan.c == 0, got, kept)
    out = []
    start = 0
    for grad in grads:
        rows = grad.shape[0] // 2
        out.append((low[start : start + rows], high[start : start + rows]))
        start += rows
    return out


def split_hidden(weight):
    return weight.reshape(2, weight.shape[0] // 2, weight.shape[1])


def turn(values, cos_tab, sine_tab):
    first, second = values[..., :HALF, :], values[..., HALF:, :]
    return jnp.concatenate(
        [first * cos_tab - second * sine_tab, second * cos_tab + first * sine_tab], axis=-2
    )


def to_heads(plan, values):
    got = [lax.dynamic_index_in_dim(values, plan.ci, 0, False)]
    for k in range(1, 4):
        got.append(plan.side(lax.dynamic_index_in_dim(values, plan.ci ^ k, 0, False), k))
    return got


def from_heads(plan, blocks):
    got = [blocks[0]] + [plan.side(blocks[k], k) for k in range(1, 4)]
    return place([block[None] for block in got], plan.ci, 0)


def more_keys(plan, blocks):
    full = list(blocks)
    for m in range(1, plan.ctx // 4):
        full += [plan.side(block, 4 * m) for block in blocks]
    return full


def more_keys_sum(plan, blocks):
    total = list(blocks[:4])
    for m in range(1, plan.ctx // 4):
        total = [total[k] + plan.side(blocks[4 * m + k], 4 * m) for k in range(4)]
    return total


def seen(first_row, part, key_block, query_block, size):
    turned = part * (size // 4)
    key = key_block * size + (lax.broadcasted_iota(jnp.int32, (size, 1), 0) ^ turned)
    query = query_block * size + (lax.broadcasted_iota(jnp.int32, (1, size), 1) ^ turned)
    return (key <= query) & (key >= first_row)


def attend_kernel(count, place_ref, first_ref, *refs):
    blocks, (out_ref, low_ref, lse_ref, kt_ref, v_ref) = refs[:count], refs[count:]
    size = blocks[0].shape[2]
    x, part = place_ref[0], place_ref[1]
    for k in range(count):
        kt_ref[x ^ k] = blocks[k][1].T
        v_ref[x ^ k] = blocks[k][2]
    for k in range(4):
        block = x ^ k
        query = blocks[k][0] * BF(HEAD ** (-0.5))
        first_row = first_ref[k]

        def step(kb, carry):
            peak, total, acc = carry
            s = mm(kt_ref[kb], query)
            s = jnp.where(seen(first_row, part, kb, block, size), s, NEG)
            top = jnp.maximum(peak, jnp.max(s, axis=0, keepdims=True))
            p = jnp.exp(s - top)
            fade = jnp.exp(peak - top)
            total = fade * total + jnp.sum(p, axis=0, keepdims=True)
            return top, total, fade * acc + mm(v_ref[kb], p.astype(BF))

        start = (
            jnp.full((1, size), NEG, F32),
            jnp.zeros((1, size), F32),
            jnp.zeros((HEAD, size), F32),
        )
        peak, total, acc = lax.fori_loop(place_ref[2 + block], block + 1, step, start)
        acc = acc / total
        out_ref[k] = acc
        low_ref[k] = acc.astype(BF)
        lse_ref[k] = peak + jnp.log(total)


def attend(where_all, first_query, blocks):
    count = len(blocks)
    size = blocks[0].shape[2]
    return pl.pallas_call(
        functools.partial(attend_kernel, count),
        out_shape=(
            jax.ShapeDtypeStruct((4, HEAD, size), F32),
            jax.ShapeDtypeStruct((4, HEAD, size), BF),
            jax.ShapeDtypeStruct((4, 1, size), F32),
        ),
        in_specs=[IN_SMEM] + [IN_VMEM] * (1 + count),
        out_specs=(IN_VMEM,) * 3,
        scratch_shapes=[
            pltpu.VMEM((count, size, HEAD), BF),
            pltpu.VMEM((count, HEAD, size), BF),
        ],
        name="attend",
    )(where_all, first_query, *blocks)


def back_kernel(count, place_ref, first_ref, out_ref, lse_ref, *refs):
    blocks, grads = refs[:count], refs[count : count + 4]
    dq_ref, dk_ref, dv_ref, kt_ref, vt_ref, k_ref, dks_ref, dvs_ref = refs[count + 4 :]
    size = blocks[0].shape[2]
    x, part = place_ref[0], place_ref[1]
    for k in range(count):
        kt_ref[x ^ k] = blocks[k][1].T
        vt_ref[x ^ k] = blocks[k][2].T
        k_ref[x ^ k] = blocks[k][1]
    dks_ref[...] = jnp.zeros_like(dks_ref)
    dvs_ref[...] = jnp.zeros_like(dvs_ref)
    for k in range(4):
        block = x ^ k
        query = blocks[k][0] * BF(HEAD ** (-0.5))
        query_t = query.T
        grad = grads[k][...]
        grad_t = grad.T
        delta = jnp.sum(grad.astype(F32) * out_ref[k], axis=0, keepdims=True)
        lse = lse_ref[k]
        first_row = first_ref[k]

        def step(kb, dq):
            s = mm(kt_ref[kb], query)
            p = jnp.where(seen(first_row, part, kb, block, size), jnp.exp(s - lse), 0.0)
            dp = mm(vt_ref[kb], grad)
            ds = (p * (dp - delta)).astype(BF)
            dvs_ref[kb] += mm(p.astype(BF), grad_t)
            dks_ref[kb] += mm(ds, query_t)
            return dq + mm(k_ref[kb], ds)

        dq = lax.fori_loop(
            place_ref[2 + block], block + 1, step, jnp.zeros((HEAD, size), F32)
        )
        dq_ref[k] = dq * HEAD ** (-0.5)
    for k in range(count):
        dk_ref[k] = dks_ref[x ^ k].T
        dv_ref[k] = dvs_ref[x ^ k].T


def attend_back(where_all, first_query, blocks, grads, out, log_total):
    count = len(blocks)
    size = blocks[0].shape[2]
    return pl.pallas_call(
        functools.partial(back_kernel, count),
        out_shape=(
            jax.ShapeDtypeStruct((4, HEAD, size), F32),
            jax.ShapeDtypeStruct((count, HEAD, size), F32),
            jax.ShapeDtypeStruct((count, HEAD, size), F32),
        ),
        in_specs=[IN_SMEM] + [IN_VMEM] * (3 + count + 4),
        out_specs=(IN_VMEM,) * 3,
        scratch_shapes=[
            pltpu.VMEM((count, size, HEAD), BF),
            pltpu.VMEM((count, size, HEAD), BF),
            pltpu.VMEM((count, HEAD, size), BF),
            pltpu.VMEM((count, size, HEAD), F32),
            pltpu.VMEM((count, size, HEAD), F32),
        ],
        name="attend_back",
    )(where_all, first_query, out, log_total, *blocks, *grads)


def norm_scale(stream):
    return lax.rsqrt(jnp.mean(stream * stream, axis=-1, keepdims=True) + EPS)


def norm_back(stream, scale, gain, grad_normed):
    weighted = grad_normed * gain
    grad_gain = jnp.sum(grad_normed * stream * scale, axis=0, keepdims=True)
    grad_stream = scale * weighted - stream * scale**3 * jnp.mean(
        weighted * stream, axis=1, keepdims=True
    )
    return (grad_gain, grad_stream)


def local(
    tokens,
    out_grad,
    segment_ids,
    owner_order,
    attn_gain,
    w_query,
    w_key,
    w_value,
    w_out,
    mlp_gain,
    w_gate,
    w_up,
    w_down,
):
    plan = Plan()
    tok_rows = tokens.shape[0]
    part_rows = tok_rows // 4
    model = tokens.shape[1]

    gains = jnp.concatenate([attn_gain, mlp_gain], axis=0)
    gains = jnp.concatenate([gains, jnp.zeros((12, gains.shape[1]), BF)], axis=0)
    full = []
    for level in range(LAYERS):
        qkv = jnp.concatenate(
            [split_hidden(w[level].T) for w in (w_query, w_key, w_value)], axis=1
        )
        w_attn = gather_weights(plan, [qkv, split_hidden(w_out[level])], level == 0)
        w_mlp = gather_weights(
            plan,
            [split_hidden(w) for w in (w_gate[level].T, w_up[level].T, w_down[level])],
            False,
        )
        cut = 2 * qkv.shape[1]
        gated = 2 * w_gate.shape[2]
        full.append((w_attn[:cut], w_attn[cut:], w_mlp[:gated], w_mlp[gated:]))
    got = plan.core(gains)
    gain_pair = jnp.where(
        plan.c == 0,
        jnp.concatenate([gains, got], axis=1),
        jnp.concatenate([got, gains], axis=1),
    )
    gain_full = all_columns(plan, gain_pair, True).astype(F32)

    def own_rows(array):
        mine = lax.dynamic_slice_in_dim(array, plan.part * part_rows, part_rows, 0)
        got = plan.core(
            lax.dynamic_slice_in_dim(array, (plan.part ^ 2) * part_rows, part_rows, 0)
        )
        return to_block_order(plan, jnp.where(plan.c == plan.zp, mine, got))

    stream = own_rows(tokens).astype(F32)
    grad_stream = own_rows(out_grad).astype(F32)

    segment = jnp.where(plan.c == plan.zp, segment_ids, plan.core(segment_ids))[0]
    pack = segment.shape[0]
    index_all = jnp.arange(pack, dtype=jnp.int32)
    run_start = jnp.concatenate([jnp.ones((1,), dtype=bool), segment[1:] != segment[:-1]])
    run_first = lax.cummax(jnp.where(run_start, index_all, jnp.zeros_like(index_all)), axis=0)
    where_all = jnp.concatenate(
        [jnp.stack([plan.x, plan.part]).astype(jnp.int32), run_first[::tok_rows] // tok_rows]
    )

    def by_peer(row):
        grid = row.reshape(plan.ctx, 4, part_rows)
        blocks = [lax.dynamic_index_in_dim(grid, plan.x ^ k, 0, False) for k in range(4)]
        grid = jnp.stack(blocks)
        return jnp.concatenate(flip_list([grid[:, i] for i in range(4)], plan.part), axis=1)

    positions = by_peer((index_all - run_first).astype(F32))
    first_query = by_peer(run_first)[:, None, :]
    frequency = THETA ** (-(jnp.arange(HALF, dtype=F32) * 2.0 / HEAD))
    angles = frequency[None, :, None] * positions[:, None, :]
    cos_all, sine_all = jnp.cos(angles), jnp.sin(angles)
    cos_own, sine_own = cos_all[0], sine_all[0]

    kept = []
    first_values = None
    for level in range(LAYERS):
        w_qkv, w_o, w_gu, w_d = full[level]
        width = w_d.shape[0]
        scale_attn = norm_scale(stream)
        normed = (stream * scale_attn * gain_full[level : level + 1]).astype(BF)
        normed_all = gather_rows(plan, normed)
        qkv = dot(w_qkv, normed_all, 1, 1).reshape(2, 3, 2, HEAD, tok_rows)
        query = turn(qkv[:, 0], cos_own, sine_own).astype(BF)
        key = turn(qkv[:, 1], cos_own, sine_own).astype(BF)
        if level == 0:
            first_values = qkv[:, 2]
            mixed = first_values
        else:
            mixed = 0.5 * qkv[:, 2] + 0.5 * first_values
        heads = jnp.stack([query, key, mixed.astype(BF)], axis=2)
        heads = more_keys(plan, to_heads(plan, heads.reshape(4, 3, HEAD, tok_rows)))
        out, out_low, log_total = attend(where_all, first_query, heads)
        attended = from_heads(plan, [out_low[k] for k in range(4)])
        attended = attended.reshape(4 * HEAD, tok_rows)
        middle = stream + sum_rows(plan, dot(attended, w_o, 0, 0))
        scale_mlp = norm_scale(middle)
        normed_mlp = (middle * scale_mlp * gain_full[2 + level : 3 + level]).astype(BF)
        normed_mlp_all = gather_rows(plan, normed_mlp)
        gate_up = dot(normed_mlp_all, w_gu, 1, 1)
        gate, upward = gate_up[:, :width], gate_up[:, width:]
        hidden = (gate * jax.nn.sigmoid(gate) * upward).astype(BF)
        result = middle + sum_rows(plan, dot(hidden, w_d, 1, 0))
        kept.append(
            (
                stream,
                scale_attn,
                normed_all,
                heads,
                out,
                log_total,
                attended,
                middle,
                scale_mlp,
                normed_mlp_all,
                gate_up,
                hidden,
            )
        )
        stream = result

    def to_pack(rows):
        block = gather_rows(plan, rows)
        pairs = []
        for f in range(plan.fsdp):
            for z in range(plan.tp):
                if f % 2 == z // 2:
                    pairs.append((f * plan.tp + z, f * plan.tp + (z ^ 2)))
        got = lax.ppermute(block, ("fsdp", "tp"), pairs)
        return jnp.where(plan.c == plan.zp, block, got)

    outputs = natural_rows(plan, to_pack(from_block_order(plan, stream.astype(BF))))

    grads = [None] * LAYERS
    gain_rows = [None] * (2 * LAYERS)
    carried = None
    for level in reversed(range(LAYERS)):
        (
            stream,
            scale_attn,
            normed_all,
            heads,
            out,
            log_total,
            attended,
            middle,
            scale_mlp,
            normed_mlp_all,
            gate_up,
            hidden,
        ) = kept[level]
        w_qkv, w_o, w_gu, w_d = full[level]
        width = w_d.shape[0]
        branch = gather_rows(plan, grad_stream.astype(BF))
        grad_hidden = dot(branch, w_d, 1, 1)
        gate, upward = gate_up[:, :width], gate_up[:, width:]
        sigma = jax.nn.sigmoid(gate)
        grad_gate = (grad_hidden * upward * sigma * (1.0 + gate * (1.0 - sigma))).astype(BF)
        grad_up = (grad_hidden * gate * sigma).astype(BF)
        grad_gu = jnp.concatenate([grad_gate, grad_up], axis=1)
        grad_normed = sum_rows(plan, dot(grad_gu, w_gu, 1, 0))
        grad_wgu = dot(grad_gu, normed_mlp_all, 0, 0).astype(BF)
        grad_wd = dot(hidden, branch, 0, 0).astype(BF)
        grad_wg, grad_wu, grad_wd = scatter_grads(
            plan, [grad_wgu[:width], grad_wgu[width:], grad_wd], False
        )
        gain_rows[2 + level], through = norm_back(
            middle, scale_mlp, gain_full[2 + level : 3 + level], grad_normed
        )
        grad_middle = grad_stream + through
        branch = gather_rows(plan, grad_middle.astype(BF))
        grad_wo = dot(attended, branch, 1, 0).astype(BF)
        grad_attended = dot(w_o, branch, 1, 1).astype(BF)
        grad_attended = to_heads(plan, grad_attended.reshape(4, HEAD, tok_rows))
        grad_q, grad_k, grad_v = attend_back(
            where_all, first_query, heads, grad_attended, out, log_total
        )
        grad_k = more_keys_sum(plan, grad_k)
        grad_v = more_keys_sum(plan, grad_v)
        if level > 0:
            grad_v = [0.5 * block for block in grad_v]
            if carried is None:
                carried = grad_v
            else:
                carried = [left + right for left, right in zip(carried, grad_v)]
        else:
            grad_v = [left + right for left, right in zip(grad_v, carried)]
        grad_heads = [
            jnp.stack(
                [
                    turn(grad_q[k], cos_all[k], -sine_all[k]).astype(BF),
                    turn(grad_k[k], cos_all[k], -sine_all[k]).astype(BF),
                    grad_v[k].astype(BF),
                ]
            )
            for k in range(4)
        ]
        grad_qkv = from_heads(plan, grad_heads).reshape(2, 2, 3, HEAD, tok_rows)
        grad_qkv = jnp.swapaxes(grad_qkv, 1, 2).reshape(-1, tok_rows)
        grad_wqkv = dot(grad_qkv, normed_all, 1, 0).astype(BF)
        grad_wqkv, grad_wo = scatter_grads(plan, [grad_wqkv, grad_wo], level == 0)
        grad_normed = sum_rows(plan, dot(grad_qkv, w_qkv, 0, 0))
        gain_rows[level], through = norm_back(
            stream, scale_attn, gain_full[level : level + 1], grad_normed
        )
        grad_stream = grad_middle + through
        third = grad_wqkv[0].shape[0] // 3

        def member(i):
            rows = [half[i * third : (i + 1) * third] for half in grad_wqkv]
            return jnp.concatenate(rows, axis=0).T

        grads[level] = (
            member(0),
            member(1),
            member(2),
            jnp.concatenate(grad_wo, axis=0),
            jnp.concatenate(grad_wg, axis=0).T,
            jnp.concatenate(grad_wu, axis=0).T,
            jnp.concatenate(grad_wd, axis=0),
        )

    gain_sum = jnp.concatenate(gain_rows + [jnp.zeros((4, model), F32)], axis=0)
    total = columns_sum(plan, gain_sum, True)
    width = total.shape[1]
    total = total + plan.far(total)
    total = total + plan.near(total)
    left, right = total[:, : width // 2], total[:, width // 2 :]
    mine = jnp.where(plan.c == 0, left, right)
    theirs = jnp.where(plan.c == 0, right, left)
    total = mine + plan.core(theirs)

    grad_block = to_pack(from_block_order(plan, grad_stream.astype(BF)))
    group_rows = tok_rows // plan.ctx
    owner_grid = owner_order[0].reshape(plan.ctx, plan.ctx, group_rows)
    local_rows = (
        lax.dynamic_index_in_dim(owner_grid, plan.x, 1, False) - plan.x * tok_rows
    ).reshape(tok_rows)
    local_rows = local_rows ^ (plan.part * part_rows)
    grad_tokens = lax.all_to_all(
        grad_block[local_rows], "ctx", split_axis=0, concat_axis=0, tiled=True
    ).astype(F32)

    stacked = [jnp.stack([grads[level][i] for level in range(LAYERS)]) for i in range(7)]
    return (
        outputs,
        grad_tokens,
        total[:2],
        stacked[0],
        stacked[1],
        stacked[2],
        stacked[3],
        total[2:4],
        stacked[4],
        stacked[5],
        stacked[6],
    )


def solution(mesh):
    columns = P(None, ("fsdp", "ctx"), "tp")
    rows = P(None, "tp", ("fsdp", "ctx"))
    gain = P(None, ("fsdp", "ctx"))
    tokens = P(("fsdp", "ctx"), None)
    return jax.shard_map(
        local,
        mesh=mesh,
        in_specs=(
            tokens,
            tokens,
            P("fsdp", None),
            P("fsdp", None),
            gain,
            columns,
            columns,
            columns,
            rows,
            gain,
            columns,
            columns,
            rows,
        ),
        out_specs=(
            tokens,
            tokens,
            gain,
            columns,
            columns,
            columns,
            rows,
            gain,
            columns,
            columns,
            rows,
        ),
        check_vma=False,
    )
```

```python
import functools

import jax
import jax.numpy as jnp
from jax import lax
from jax.experimental import pallas as pl
from jax.experimental.pallas import tpu as pltpu
from jax.sharding import PartitionSpec as P

HEAD = 64
HALF = HEAD // 2
LAYERS = 2
EPS = 1e-05
THETA = 10000.0
NEG = -1e30
BF = jnp.bfloat16
F32 = jnp.float32
IN_VMEM = pl.BlockSpec(memory_space=pltpu.VMEM)
IN_SMEM = pl.BlockSpec(memory_space=pltpu.SMEM)


def dot(left, right, left_dim, right_dim):
    return lax.dot_general(
        left, right, (((left_dim,), (right_dim,)), ((), ())), preferred_element_type=F32
    )


def mm(left, right):
    return jnp.dot(left, right, preferred_element_type=F32)


class Plan:
    def __init__(self):
        self.fsdp = lax.axis_size("fsdp")
        self.ctx = lax.axis_size("ctx")
        self.tp = lax.axis_size("tp")
        self.high = self.fsdp // 2
        f = lax.axis_index("fsdp")
        z = lax.axis_index("tp")
        self.c = f % 2
        self.fh = f // 2
        self.x = lax.axis_index("ctx")
        self.zl = z % 2
        self.zp = z // 2
        self.ci = self.x % 4
        self.part = self.c * 2 + self.zl
        self.peers = self.high * self.ctx

    def core(self, value):
        return lax.ppermute(value, "fsdp", [(i, i ^ 1) for i in range(self.fsdp)])

    def near(self, value):
        return lax.ppermute(value, "tp", [(i, i ^ 1) for i in range(self.tp)])

    def far(self, value):
        return lax.ppermute(value, "tp", [(i, i ^ 2) for i in range(self.tp)])

    def side(self, value, k):
        return lax.ppermute(value, "ctx", [(i, i ^ k) for i in range(self.ctx)])

    def high_fsdp(self, value, k):
        return lax.ppermute(value, "fsdp", [(i, i ^ (2 * k)) for i in range(self.fsdp)])


def flip_list(blocks, index):
    bit = 1
    while bit < len(blocks):
        on = (index & bit) != 0
        blocks = [jnp.where(on, blocks[i ^ bit], blocks[i]) for i in range(len(blocks))]
        bit *= 2
    return blocks


def place(blocks, index, axis):
    width = blocks[0].shape[axis]
    shape = list(blocks[0].shape)
    shape[axis] = width * len(blocks)
    full = jnp.zeros(shape, blocks[0].dtype)
    for i, block in enumerate(blocks):
        full = lax.dynamic_update_slice_in_dim(full, block, (index ^ i) * width, axis)
    return full


def to_block_order(plan, rows):
    width = rows.shape[1] // (2 * plan.peers)
    parts = []
    for h in range(plan.high):
        for x in range(plan.ctx):
            for c in range(2):
                start = ((h * 2 + c) * plan.ctx + x) * width
                parts.append(rows[:, start : start + width])
    return jnp.concatenate(parts, axis=1)


def from_block_order(plan, rows):
    width = rows.shape[1] // (2 * plan.peers)
    parts = []
    for h in range(plan.high):
        for c in range(2):
            for x in range(plan.ctx):
                start = ((h * plan.ctx + x) * 2 + c) * width
                parts.append(rows[:, start : start + width])
    return jnp.concatenate(parts, axis=1)


def gather_rows(plan, rows):
    pair = jnp.concatenate([rows, plan.near(rows)], axis=0)
    return jnp.concatenate([pair, plan.core(pair)], axis=0)


def sum_rows(plan, partial):
    half = partial.shape[0] // 2
    pair = partial[:half] + plan.core(partial[half:].astype(BF)).astype(F32)
    half = half // 2
    return pair[:half] + plan.near(pair[half:].astype(BF)).astype(F32)


def natural_rows(plan, rows):
    count = rows.shape[0] // 4
    parts = [
        lax.dynamic_slice_in_dim(rows, (plan.part ^ i) * count, count, 0) for i in range(4)
    ]
    return jnp.concatenate(parts, axis=0)


def own_columns(plan, halves):
    keep = lax.dynamic_index_in_dim(halves, plan.c, 0, False)
    got = plan.core(lax.dynamic_index_in_dim(halves, 1 - plan.c, 0, False))
    return jnp.where(
        plan.c == 0,
        jnp.concatenate([keep, got], axis=1),
        jnp.concatenate([got, keep], axis=1),
    )


def all_columns(plan, rows, direct):
    if direct and plan.peers == 4:
        return place([rows] + [plan.side(rows, k) for k in range(1, 4)], plan.x, 1)
    full = lax.all_gather(rows, "ctx", axis=1, tiled=True)
    if plan.high > 1:
        parts = [full] + [plan.high_fsdp(full, k) for k in range(1, plan.high)]
        full = place(parts, plan.fh, 1)
    return full


def columns_sum(plan, grad, direct):
    if plan.high > 1:
        width = grad.shape[1] // plan.high
        parts = [
            lax.dynamic_slice_in_dim(grad, (plan.fh ^ k) * width, width, 1)
            for k in range(plan.high)
        ]
        grad = parts[0]
        for k in range(1, plan.high):
            grad = grad + plan.high_fsdp(parts[k], k)
    if direct and plan.ctx == 4:
        width = grad.shape[1] // 4
        parts = [
            lax.dynamic_slice_in_dim(grad, (plan.x ^ k) * width, width, 1) for k in range(4)
        ]
        total = parts[0].astype(F32)
        for k in range(1, 4):
            total = total + plan.side(parts[k], k).astype(F32)
        return total
    return lax.psum_scatter(grad, "ctx", scatter_dimension=1, tiled=True).astype(F32)


def tie(value, *others):
    return lax.optimization_barrier((value, *others))[0]


def with_far(own, far, counts):
    parts = []
    start = 0
    for rows in counts:
        parts += [own[start : start + rows], far[start : start + rows]]
        start += rows
    return jnp.concatenate(parts, axis=0)


def far_halves(total, counts):
    mine, far = [], []
    start = 0
    for rows in counts:
        mine.append(total[start : start + rows])
        far.append(total[start + rows : start + 2 * rows])
        start += 2 * rows
    return jnp.concatenate(mine, axis=0), jnp.concatenate(far, axis=0).astype(BF)


def core_halves(plan, own, counts):
    width = own.shape[1]
    left, right = own[:, : width // 2], own[:, width // 2 :]
    kept = jnp.where(plan.c == 0, left, right)
    got = plan.core(jnp.where(plan.c == 0, right, left).astype(BF)).astype(F32)
    low = jnp.where(plan.c == 0, kept, got)
    high = jnp.where(plan.c == 0, got, kept)
    out = []
    start = 0
    for rows in counts:
        out.append((low[start : start + rows], high[start : start + rows]))
        start += rows
    return out


def split_hidden(weight):
    return weight.reshape(2, weight.shape[0] // 2, weight.shape[1])


def turn(values, cos_tab, sine_tab):
    first, second = values[..., :HALF, :], values[..., HALF:, :]
    return jnp.concatenate(
        [first * cos_tab - second * sine_tab, second * cos_tab + first * sine_tab], axis=-2
    )


def to_heads(plan, values):
    got = [lax.dynamic_index_in_dim(values, plan.ci, 0, False)]
    for k in range(1, 4):
        got.append(plan.side(lax.dynamic_index_in_dim(values, plan.ci ^ k, 0, False), k))
    return got


def from_heads(plan, blocks):
    got = [blocks[0]] + [plan.side(blocks[k], k) for k in range(1, 4)]
    return place([block[None] for block in got], plan.ci, 0)


def more_keys(plan, blocks):
    full = list(blocks)
    for m in range(1, plan.ctx // 4):
        full += [plan.side(block, 4 * m) for block in blocks]
    return full


def more_keys_sum(plan, blocks):
    total = list(blocks[:4])
    for m in range(1, plan.ctx // 4):
        total = [total[k] + plan.side(blocks[4 * m + k], 4 * m) for k in range(4)]
    return total


def seen(first_row, part, key_block, query_block, size):
    turned = part * (size // 4)
    key = key_block * size + (lax.broadcasted_iota(jnp.int32, (size, 1), 0) ^ turned)
    query = query_block * size + (lax.broadcasted_iota(jnp.int32, (1, size), 1) ^ turned)
    return (key <= query) & (key >= first_row)


def attend_kernel(count, place_ref, first_ref, *refs):
    blocks, (out_ref, low_ref, lse_ref, kt_ref, v_ref) = refs[:count], refs[count:]
    size = blocks[0].shape[2]
    x, part = place_ref[0], place_ref[1]
    for k in range(count):
        kt_ref[x ^ k] = blocks[k][1].T
        v_ref[x ^ k] = blocks[k][2]
    for k in range(4):
        block = x ^ k
        query = blocks[k][0] * BF(HEAD ** (-0.5))
        first_row = first_ref[k]

        def step(kb, carry):
            peak, total, acc = carry
            s = mm(kt_ref[kb], query)
            s = jnp.where(seen(first_row, part, kb, block, size), s, NEG)
            top = jnp.maximum(peak, jnp.max(s, axis=0, keepdims=True))
            p = jnp.exp(s - top)
            fade = jnp.exp(peak - top)
            total = fade * total + jnp.sum(p, axis=0, keepdims=True)
            return top, total, fade * acc + mm(v_ref[kb], p.astype(BF))

        start = (
            jnp.full((1, size), NEG, F32),
            jnp.zeros((1, size), F32),
            jnp.zeros((HEAD, size), F32),
        )
        peak, total, acc = lax.fori_loop(place_ref[2 + block], block + 1, step, start)
        acc = acc / total
        out_ref[k] = acc
        low_ref[k] = acc.astype(BF)
        lse_ref[k] = peak + jnp.log(total)


def attend(where_all, first_query, blocks):
    count = len(blocks)
    size = blocks[0].shape[2]
    return pl.pallas_call(
        functools.partial(attend_kernel, count),
        out_shape=(
            jax.ShapeDtypeStruct((4, HEAD, size), F32),
            jax.ShapeDtypeStruct((4, HEAD, size), BF),
            jax.ShapeDtypeStruct((4, 1, size), F32),
        ),
        in_specs=[IN_SMEM] + [IN_VMEM] * (1 + count),
        out_specs=(IN_VMEM,) * 3,
        scratch_shapes=[
            pltpu.VMEM((count, size, HEAD), BF),
            pltpu.VMEM((count, HEAD, size), BF),
        ],
        name="attend",
    )(where_all, first_query, *blocks)


def back_kernel(count, place_ref, first_ref, out_ref, lse_ref, *refs):
    blocks, grads = refs[:count], refs[count : count + 4]
    dq_ref, dk_ref, dv_ref, kt_ref, vt_ref, k_ref, dks_ref, dvs_ref = refs[count + 4 :]
    size = blocks[0].shape[2]
    x, part = place_ref[0], place_ref[1]
    for k in range(count):
        kt_ref[x ^ k] = blocks[k][1].T
        vt_ref[x ^ k] = blocks[k][2].T
        k_ref[x ^ k] = blocks[k][1]
    dks_ref[...] = jnp.zeros_like(dks_ref)
    dvs_ref[...] = jnp.zeros_like(dvs_ref)
    for k in range(4):
        block = x ^ k
        query = blocks[k][0] * BF(HEAD ** (-0.5))
        query_t = query.T
        grad = grads[k][...]
        grad_t = grad.T
        delta = jnp.sum(grad.astype(F32) * out_ref[k], axis=0, keepdims=True)
        lse = lse_ref[k]
        first_row = first_ref[k]

        def step(kb, dq):
            s = mm(kt_ref[kb], query)
            p = jnp.where(seen(first_row, part, kb, block, size), jnp.exp(s - lse), 0.0)
            dp = mm(vt_ref[kb], grad)
            ds = (p * (dp - delta)).astype(BF)
            dvs_ref[kb] += mm(p.astype(BF), grad_t)
            dks_ref[kb] += mm(ds, query_t)
            return dq + mm(k_ref[kb], ds)

        dq = lax.fori_loop(
            place_ref[2 + block], block + 1, step, jnp.zeros((HEAD, size), F32)
        )
        dq_ref[k] = dq * HEAD ** (-0.5)
    for k in range(count):
        dk_ref[k] = dks_ref[x ^ k].T
        dv_ref[k] = dvs_ref[x ^ k].T


def attend_back(where_all, first_query, blocks, grads, out, log_total):
    count = len(blocks)
    size = blocks[0].shape[2]
    return pl.pallas_call(
        functools.partial(back_kernel, count),
        out_shape=(
            jax.ShapeDtypeStruct((4, HEAD, size), F32),
            jax.ShapeDtypeStruct((count, HEAD, size), F32),
            jax.ShapeDtypeStruct((count, HEAD, size), F32),
        ),
        in_specs=[IN_SMEM] + [IN_VMEM] * (3 + count + 4),
        out_specs=(IN_VMEM,) * 3,
        scratch_shapes=[
            pltpu.VMEM((count, size, HEAD), BF),
            pltpu.VMEM((count, size, HEAD), BF),
            pltpu.VMEM((count, HEAD, size), BF),
            pltpu.VMEM((count, size, HEAD), F32),
            pltpu.VMEM((count, size, HEAD), F32),
        ],
        name="attend_back",
    )(where_all, first_query, out, log_total, *blocks, *grads)


def norm_scale(stream):
    return lax.rsqrt(jnp.mean(stream * stream, axis=-1, keepdims=True) + EPS)


def norm_back(stream, scale, gain, grad_normed):
    weighted = grad_normed * gain
    grad_gain = jnp.sum(grad_normed * stream * scale, axis=0, keepdims=True)
    grad_stream = scale * weighted - stream * scale**3 * jnp.mean(
        weighted * stream, axis=1, keepdims=True
    )
    return (grad_gain, grad_stream)


def local(
    tokens,
    out_grad,
    segment_ids,
    owner_order,
    attn_gain,
    w_query,
    w_key,
    w_value,
    w_out,
    mlp_gain,
    w_gate,
    w_up,
    w_down,
):
    plan = Plan()
    tok_rows = tokens.shape[0]
    part_rows = tok_rows // 4
    model = tokens.shape[1]

    gains = jnp.concatenate([attn_gain, mlp_gain], axis=0)
    gains = jnp.concatenate([gains, jnp.zeros((12, gains.shape[1]), BF)], axis=0)
    qkv_rows = 3 * w_query.shape[2] // 2
    out_rows = w_out.shape[1] // 2
    mlp_rows = w_down.shape[1] // 2
    counts = [qkv_rows, out_rows] + [mlp_rows] * 3

    def own_weights(level):
        qkv = [split_hidden(w[level].T) for w in (w_query, w_key, w_value)]
        return [
            jnp.concatenate(qkv, axis=1),
            split_hidden(w_out[level]),
            split_hidden(w_gate[level].T),
            split_hidden(w_up[level].T),
            split_hidden(w_down[level]),
        ]

    groups = own_weights(0)
    own = own_columns(plan, groups[0])
    far_first = plan.far(own)
    w_qkv = all_columns(plan, with_far(own, far_first, counts[:1]), True)
    own = tie(own_columns(plan, jnp.concatenate(groups[1:], axis=1)), far_first)
    far_rest = plan.far(own)
    rest = with_far(own, far_rest, counts[1:])
    w_o = all_columns(plan, tie(rest[: 2 * out_rows], w_qkv), True)
    w_mlp = all_columns(plan, tie(rest[2 * out_rows :], w_qkv), False)
    full = [(w_qkv, w_o, w_mlp)]
    far_later = []
    for level in range(1, LAYERS):
        own = own_columns(plan, jnp.concatenate(own_weights(level), axis=1))
        far_rest = plan.far(tie(own, far_rest))
        far_later.append(far_rest)
        rest = with_far(own, far_rest, counts)
        cut = 2 * (qkv_rows + out_rows)
        w_attn = all_columns(plan, rest[:cut], False)
        w_mlp = all_columns(plan, rest[cut:], False)
        full.append((w_attn[: 2 * qkv_rows], w_attn[2 * qkv_rows :], w_mlp))
    got = plan.core(gains)
    gain_pair = jnp.where(
        plan.c == 0,
        jnp.concatenate([gains, got], axis=1),
        jnp.concatenate([got, gains], axis=1),
    )
    gain_full = all_columns(plan, gain_pair, True).astype(F32)

    def own_rows(array):
        mine = lax.dynamic_slice_in_dim(array, plan.part * part_rows, part_rows, 0)
        got = plan.core(
            lax.dynamic_slice_in_dim(array, (plan.part ^ 2) * part_rows, part_rows, 0)
        )
        return to_block_order(plan, jnp.where(plan.c == plan.zp, mine, got))

    stream = own_rows(tokens).astype(F32)
    grad_stream = own_rows(out_grad).astype(F32)

    segment = jnp.where(plan.c == plan.zp, segment_ids, plan.core(segment_ids))[0]
    pack = segment.shape[0]
    index_all = jnp.arange(pack, dtype=jnp.int32)
    run_start = jnp.concatenate([jnp.ones((1,), dtype=bool), segment[1:] != segment[:-1]])
    run_first = lax.cummax(jnp.where(run_start, index_all, jnp.zeros_like(index_all)), axis=0)
    where_all = jnp.concatenate(
        [jnp.stack([plan.x, plan.part]).astype(jnp.int32), run_first[::tok_rows] // tok_rows]
    )

    def by_peer(row):
        grid = row.reshape(plan.ctx, 4, part_rows)
        blocks = [lax.dynamic_index_in_dim(grid, plan.x ^ k, 0, False) for k in range(4)]
        grid = jnp.stack(blocks)
        return jnp.concatenate(flip_list([grid[:, i] for i in range(4)], plan.part), axis=1)

    positions = by_peer((index_all - run_first).astype(F32))
    first_query = by_peer(run_first)[:, None, :]
    frequency = THETA ** (-(jnp.arange(HALF, dtype=F32) * 2.0 / HEAD))
    angles = frequency[None, :, None] * positions[:, None, :]
    cos_all, sine_all = jnp.cos(angles), jnp.sin(angles)
    cos_own, sine_own = cos_all[0], sine_all[0]

    kept = []
    first_values = None
    for level in range(LAYERS):
        w_qkv, w_o, w_mlp = full[level]
        width = 2 * mlp_rows
        w_gu, w_d = w_mlp[: 2 * width], w_mlp[2 * width :]
        scale_attn = norm_scale(stream)
        normed = (stream * scale_attn * gain_full[level : level + 1]).astype(BF)
        normed_all = gather_rows(plan, normed)
        qkv = dot(w_qkv, normed_all, 1, 1).reshape(2, 3, 2, HEAD, tok_rows)
        query = turn(qkv[:, 0], cos_own, sine_own).astype(BF)
        key = turn(qkv[:, 1], cos_own, sine_own).astype(BF)
        if level == 0:
            first_values = qkv[:, 2]
            mixed = first_values
        else:
            mixed = 0.5 * qkv[:, 2] + 0.5 * first_values
        heads = jnp.stack([query, key, mixed.astype(BF)], axis=2)
        heads = more_keys(plan, to_heads(plan, heads.reshape(4, 3, HEAD, tok_rows)))
        out, out_low, log_total = attend(where_all, first_query, heads)
        attended = from_heads(plan, [out_low[k] for k in range(4)])
        attended = attended.reshape(4 * HEAD, tok_rows)
        branch = sum_rows(plan, dot(attended, w_o, 0, 0))
        if level < len(far_later):
            branch = tie(branch, far_later[level])
        middle = stream + branch
        scale_mlp = norm_scale(middle)
        normed_mlp = (middle * scale_mlp * gain_full[2 + level : 3 + level]).astype(BF)
        normed_mlp_all = gather_rows(plan, normed_mlp)
        gate_up = dot(normed_mlp_all, w_gu, 1, 1)
        gate, upward = gate_up[:, :width], gate_up[:, width:]
        hidden = (gate * jax.nn.sigmoid(gate) * upward).astype(BF)
        result = middle + sum_rows(plan, dot(hidden, w_d, 1, 0))
        kept.append(
            (
                stream,
                scale_attn,
                normed_all,
                heads,
                out,
                log_total,
                attended,
                middle,
                scale_mlp,
                normed_mlp_all,
                gate_up,
                hidden,
            )
        )
        stream = result

    def to_pack(rows):
        other = plan.far(rows)
        mine = jnp.where(plan.c == plan.zp, rows, other)
        got = plan.core(jnp.where(plan.c == plan.zp, other, rows))
        count = rows.shape[0]
        near = plan.near(jnp.concatenate([mine, got], axis=0))
        return jnp.concatenate([mine, near[:count], got, near[count:]], axis=0)

    last = from_block_order(plan, stream.astype(BF))

    grads = [None] * LAYERS
    gain_rows = [None] * (2 * LAYERS)
    carried = None
    later_sums = []
    for level in reversed(range(LAYERS)):
        (
            stream,
            scale_attn,
            normed_all,
            heads,
            out,
            log_total,
            attended,
            middle,
            scale_mlp,
            normed_mlp_all,
            gate_up,
            hidden,
        ) = kept[level]
        w_qkv, w_o, w_mlp = full[level]
        width = 2 * mlp_rows
        w_gu, w_d = w_mlp[: 2 * width], w_mlp[2 * width :]
        branch = gather_rows(plan, grad_stream.astype(BF))
        grad_hidden = dot(branch, w_d, 1, 1)
        gate, upward = gate_up[:, :width], gate_up[:, width:]
        sigma = jax.nn.sigmoid(gate)
        grad_gate = (grad_hidden * upward * sigma * (1.0 + gate * (1.0 - sigma))).astype(BF)
        grad_up = (grad_hidden * gate * sigma).astype(BF)
        grad_gu = jnp.concatenate([grad_gate, grad_up], axis=1)
        grad_normed = sum_rows(plan, dot(grad_gu, w_gu, 1, 0))
        grad_wd = dot(hidden, branch, 0, 0).astype(BF)
        grad_wgu = dot(grad_gu, normed_mlp_all, 0, 0).astype(BF)
        if level > 0:
            grad_mlp = jnp.concatenate([grad_wgu, grad_wd], axis=0)
            grad_normed = tie(grad_normed, grad_mlp)
            sum_mlp = columns_sum(plan, grad_mlp, False)
        else:
            sum_wd = columns_sum(plan, grad_wd, False)
        gain_rows[2 + level], through = norm_back(
            middle, scale_mlp, gain_full[2 + level : 3 + level], grad_normed
        )
        grad_middle = grad_stream + through
        branch = gather_rows(plan, grad_middle.astype(BF))
        if level == 0:
            branch, *sums = lax.optimization_barrier((branch, *later_sums))
            mine, far = far_halves(jnp.concatenate(sums, axis=0), counts * (LAYERS - 1))
            far_sums = plan.far(far)
        grad_wo = dot(attended, branch, 1, 0).astype(BF)
        grad_attended = dot(w_o, branch, 1, 1).astype(BF)
        if level == 0:
            grad_out = jnp.concatenate([grad_wgu, grad_wo], axis=0)
            grad_attended = tie(grad_attended, grad_out, outputs)
            sum_gu = columns_sum(plan, grad_out, False)
        elif level == LAYERS - 1:
            outputs = natural_rows(plan, to_pack(tie(last, grad_attended)))
        grad_attended = to_heads(plan, grad_attended.reshape(4, HEAD, tok_rows))
        grad_q, grad_k, grad_v = attend_back(
            where_all, first_query, heads, grad_attended, out, log_total
        )
        grad_k = more_keys_sum(plan, grad_k)
        grad_v = more_keys_sum(plan, grad_v)
        if level > 0:
            grad_v = [0.5 * block for block in grad_v]
            if carried is None:
                carried = grad_v
            else:
                carried = [left + right for left, right in zip(carried, grad_v)]
        else:
            grad_v = [left + right for left, right in zip(grad_v, carried)]
        grad_heads = [
            jnp.stack(
                [
                    turn(grad_q[k], cos_all[k], -sine_all[k]).astype(BF),
                    turn(grad_k[k], cos_all[k], -sine_all[k]).astype(BF),
                    grad_v[k].astype(BF),
                ]
            )
            for k in range(4)
        ]
        grad_qkv = from_heads(plan, grad_heads).reshape(2, 2, 3, HEAD, tok_rows)
        grad_qkv = jnp.swapaxes(grad_qkv, 1, 2).reshape(-1, tok_rows)
        if level == 0:
            grad_qkv, far_sums = lax.optimization_barrier((grad_qkv, far_sums))
            later = core_halves(plan, mine + far_sums.astype(F32), counts * (LAYERS - 1))
        grad_wqkv = dot(grad_qkv, normed_all, 1, 0).astype(BF)
        if level > 0:
            sum_attn = columns_sum(plan, jnp.concatenate([grad_wqkv, grad_wo], axis=0), False)
            later_sums += [sum_attn, sum_mlp]
        else:
            sum_qkv = columns_sum(plan, grad_wqkv, True)
        grad_normed = sum_rows(plan, dot(grad_qkv, w_qkv, 0, 0))
        gain_rows[level], through = norm_back(
            stream, scale_attn, gain_full[level : level + 1], grad_normed
        )
        grad_stream = grad_middle + through

    def weight_grads(grad_qkv, grad_wo, grad_wg, grad_wu, grad_wd):
        third = qkv_rows // 3

        def member(i):
            rows = [half[i * third : (i + 1) * third] for half in grad_qkv]
            return jnp.concatenate(rows, axis=0).T

        return (
            member(0),
            member(1),
            member(2),
            jnp.concatenate(grad_wo, axis=0),
            jnp.concatenate(grad_wg, axis=0).T,
            jnp.concatenate(grad_wu, axis=0).T,
            jnp.concatenate(grad_wd, axis=0),
        )

    for i, level in enumerate(reversed(range(1, LAYERS))):
        grads[level] = weight_grads(*later[5 * i : 5 * i + 5])

    grad_block = to_pack(from_block_order(plan, grad_stream.astype(BF)))
    group_rows = tok_rows // plan.ctx
    owner_grid = owner_order[0].reshape(plan.ctx, plan.ctx, group_rows)
    local_rows = (
        lax.dynamic_index_in_dim(owner_grid, plan.x, 1, False) - plan.x * tok_rows
    ).reshape(tok_rows)
    local_rows = local_rows ^ (plan.part * part_rows)
    grad_tokens = lax.all_to_all(
        grad_block[local_rows], "ctx", split_axis=0, concat_axis=0, tiled=True
    ).astype(F32)

    mlp_counts = [mlp_rows, mlp_rows, out_rows, mlp_rows]
    mine, far = far_halves(jnp.concatenate([sum_gu, sum_wd], axis=0), mlp_counts)
    rest = core_halves(plan, mine + plan.far(far).astype(F32), mlp_counts)
    mine, far = far_halves(sum_qkv, [qkv_rows])
    first = core_halves(plan, mine + plan.far(far).astype(F32), [qkv_rows])
    grads[0] = weight_grads(first[0], rest[2], rest[0], rest[1], rest[3])

    gain_sum = jnp.concatenate(gain_rows + [jnp.zeros((4, model), F32)], axis=0)
    total = columns_sum(plan, tie(gain_sum, grad_block), True)
    width = total.shape[1]
    total = total + plan.far(total)
    total = total + plan.near(total)
    left, right = total[:, : width // 2], total[:, width // 2 :]
    mine = jnp.where(plan.c == 0, left, right)
    theirs = jnp.where(plan.c == 0, right, left)
    total = mine + plan.core(theirs)

    stacked = [jnp.stack([grads[level][i] for level in range(LAYERS)]) for i in range(7)]
    return (
        outputs,
        grad_tokens,
        total[:2],
        stacked[0],
        stacked[1],
        stacked[2],
        stacked[3],
        total[2:4],
        stacked[4],
        stacked[5],
        stacked[6],
    )


def solution(mesh):
    columns = P(None, ("fsdp", "ctx"), "tp")
    rows = P(None, "tp", ("fsdp", "ctx"))
    gain = P(None, ("fsdp", "ctx"))
    tokens = P(("fsdp", "ctx"), None)
    return jax.shard_map(
        local,
        mesh=mesh,
        in_specs=(
            tokens,
            tokens,
            P("fsdp", None),
            P("fsdp", None),
            gain,
            columns,
            columns,
            columns,
            rows,
            gain,
            columns,
            columns,
            rows,
        ),
        out_specs=(
            tokens,
            tokens,
            gain,
            columns,
            columns,
            columns,
            rows,
            gain,
            columns,
            columns,
            rows,
        ),
        check_vma=False,
    )
```

```python
import functools

import jax
import jax.numpy as jnp
from jax import lax
from jax.experimental import pallas as pl
from jax.experimental.pallas import tpu as pltpu
from jax.sharding import PartitionSpec as P

HEAD = 64
HALF = HEAD // 2
LAYERS = 2
EPS = 1e-05
THETA = 10000.0
NEG = -1e30
BF = jnp.bfloat16
F32 = jnp.float32
IN_VMEM = pl.BlockSpec(memory_space=pltpu.VMEM)
IN_SMEM = pl.BlockSpec(memory_space=pltpu.SMEM)


def dot(left, right, left_dim, right_dim):
    return lax.dot_general(
        left, right, (((left_dim,), (right_dim,)), ((), ())), preferred_element_type=F32
    )


def mm(left, right):
    return jnp.dot(left, right, preferred_element_type=F32)


class Plan:
    def __init__(self):
        self.fsdp = lax.axis_size("fsdp")
        self.ctx = lax.axis_size("ctx")
        self.tp = lax.axis_size("tp")
        self.high = self.fsdp // 2
        f = lax.axis_index("fsdp")
        z = lax.axis_index("tp")
        self.c = f % 2
        self.fh = f // 2
        self.x = lax.axis_index("ctx")
        self.zl = z % 2
        self.zp = z // 2
        self.ci = self.x % 4
        self.part = self.c * 2 + self.zl
        self.peers = self.high * self.ctx

    def core(self, value):
        return lax.ppermute(value, "fsdp", [(i, i ^ 1) for i in range(self.fsdp)])

    def near(self, value):
        return lax.ppermute(value, "tp", [(i, i ^ 1) for i in range(self.tp)])

    def far(self, value):
        return lax.ppermute(value, "tp", [(i, i ^ 2) for i in range(self.tp)])

    def side(self, value, k):
        return lax.ppermute(value, "ctx", [(i, i ^ k) for i in range(self.ctx)])

    def high_fsdp(self, value, k):
        return lax.ppermute(value, "fsdp", [(i, i ^ (2 * k)) for i in range(self.fsdp)])


def flip_list(blocks, index):
    bit = 1
    while bit < len(blocks):
        on = (index & bit) != 0
        blocks = [jnp.where(on, blocks[i ^ bit], blocks[i]) for i in range(len(blocks))]
        bit *= 2
    return blocks


def place(blocks, index, axis):
    width = blocks[0].shape[axis]
    shape = list(blocks[0].shape)
    shape[axis] = width * len(blocks)
    full = jnp.zeros(shape, blocks[0].dtype)
    for i, block in enumerate(blocks):
        full = lax.dynamic_update_slice_in_dim(full, block, (index ^ i) * width, axis)
    return full


def to_block_order(plan, rows):
    width = rows.shape[1] // (2 * plan.peers)
    parts = []
    for h in range(plan.high):
        for x in range(plan.ctx):
            for c in range(2):
                start = ((h * 2 + c) * plan.ctx + x) * width
                parts.append(rows[:, start : start + width])
    return jnp.concatenate(parts, axis=1)


def from_block_order(plan, rows):
    width = rows.shape[1] // (2 * plan.peers)
    parts = []
    for h in range(plan.high):
        for c in range(2):
            for x in range(plan.ctx):
                start = ((h * plan.ctx + x) * 2 + c) * width
                parts.append(rows[:, start : start + width])
    return jnp.concatenate(parts, axis=1)


def gather_rows(plan, rows):
    pair = jnp.concatenate([rows, plan.near(rows)], axis=0)
    return jnp.concatenate([pair, plan.core(pair)], axis=0)


def sum_rows(plan, partial):
    half = partial.shape[0] // 2
    pair = partial[:half] + plan.core(partial[half:].astype(BF)).astype(F32)
    half = half // 2
    return pair[:half] + plan.near(pair[half:].astype(BF)).astype(F32)


def natural_rows(plan, rows):
    count = rows.shape[0] // 4
    parts = [
        lax.dynamic_slice_in_dim(rows, (plan.part ^ i) * count, count, 0) for i in range(4)
    ]
    return jnp.concatenate(parts, axis=0)


def own_columns(plan, halves):
    keep = lax.dynamic_index_in_dim(halves, plan.c, 0, False)
    got = plan.core(lax.dynamic_index_in_dim(halves, 1 - plan.c, 0, False))
    return jnp.where(
        plan.c == 0,
        jnp.concatenate([keep, got], axis=1),
        jnp.concatenate([got, keep], axis=1),
    )


def all_columns(plan, rows, direct):
    if direct and plan.peers == 4:
        return place([rows] + [plan.side(rows, k) for k in range(1, 4)], plan.x, 1)
    full = lax.all_gather(rows, "ctx", axis=1, tiled=True)
    if plan.high > 1:
        parts = [full] + [plan.high_fsdp(full, k) for k in range(1, plan.high)]
        full = place(parts, plan.fh, 1)
    return full


def columns_sum(plan, grad, direct):
    if plan.high > 1:
        width = grad.shape[1] // plan.high
        parts = [
            lax.dynamic_slice_in_dim(grad, (plan.fh ^ k) * width, width, 1)
            for k in range(plan.high)
        ]
        grad = parts[0]
        for k in range(1, plan.high):
            grad = grad + plan.high_fsdp(parts[k], k)
    if direct and plan.ctx == 4:
        width = grad.shape[1] // 4
        parts = [
            lax.dynamic_slice_in_dim(grad, (plan.x ^ k) * width, width, 1) for k in range(4)
        ]
        total = parts[0].astype(F32)
        for k in range(1, 4):
            total = total + plan.side(parts[k], k).astype(F32)
        return total
    return lax.psum_scatter(grad, "ctx", scatter_dimension=1, tiled=True).astype(F32)


def tie(value, *others):
    return lax.optimization_barrier((value, *others))[0]


def together(value, *others):
    many = isinstance(value, list)
    got = lax.optimization_barrier((*value, *others) if many else (value, *others))
    count = len(value) if many else 1
    first = list(got[:count]) if many else got[0]
    return (first, *got[count:])


def with_far(own, far, counts):
    parts = []
    start = 0
    for rows in counts:
        parts += [own[start : start + rows], far[start : start + rows]]
        start += rows
    return jnp.concatenate(parts, axis=0)


def far_halves(total, counts):
    mine, far = [], []
    start = 0
    for rows in counts:
        mine.append(total[start : start + rows])
        far.append(total[start + rows : start + 2 * rows])
        start += 2 * rows
    return jnp.concatenate(mine, axis=0), jnp.concatenate(far, axis=0).astype(BF)


def core_halves(plan, own, counts):
    width = own.shape[1]
    left, right = own[:, : width // 2], own[:, width // 2 :]
    kept = jnp.where(plan.c == 0, left, right)
    got = plan.core(jnp.where(plan.c == 0, right, left).astype(BF)).astype(F32)
    low = jnp.where(plan.c == 0, kept, got)
    high = jnp.where(plan.c == 0, got, kept)
    out = []
    start = 0
    for rows in counts:
        out.append((low[start : start + rows], high[start : start + rows]))
        start += rows
    return out


def split_hidden(weight):
    return weight.reshape(2, weight.shape[0] // 2, weight.shape[1])


def turn(values, cos_tab, sine_tab):
    first, second = values[..., :HALF, :], values[..., HALF:, :]
    return jnp.concatenate(
        [first * cos_tab - second * sine_tab, second * cos_tab + first * sine_tab], axis=-2
    )


def to_heads(plan, values):
    got = [lax.dynamic_index_in_dim(values, plan.ci, 0, False)]
    for k in range(1, 4):
        got.append(plan.side(lax.dynamic_index_in_dim(values, plan.ci ^ k, 0, False), k))
    return got


def from_heads(plan, blocks):
    got = [blocks[0]] + [plan.side(blocks[k], k) for k in range(1, 4)]
    return place([block[None] for block in got], plan.ci, 0)


def more_keys(plan, blocks):
    full = list(blocks)
    for m in range(1, plan.ctx // 4):
        full += [plan.side(block, 4 * m) for block in blocks]
    return full


def more_keys_sum(plan, blocks):
    total = list(blocks[:4])
    for m in range(1, plan.ctx // 4):
        total = [total[k] + plan.side(blocks[4 * m + k], 4 * m) for k in range(4)]
    return total


def seen(first_row, part, key_block, query_block, size):
    turned = part * (size // 4)
    key = key_block * size + (lax.broadcasted_iota(jnp.int32, (size, 1), 0) ^ turned)
    query = query_block * size + (lax.broadcasted_iota(jnp.int32, (1, size), 1) ^ turned)
    return (key <= query) & (key >= first_row)


def attend_kernel(count, place_ref, first_ref, *refs):
    blocks, (out_ref, low_ref, lse_ref, kt_ref, v_ref) = refs[:count], refs[count:]
    size = blocks[0].shape[2]
    x, part = place_ref[0], place_ref[1]
    for k in range(count):
        kt_ref[x ^ k] = blocks[k][1].T
        v_ref[x ^ k] = blocks[k][2]
    for k in range(4):
        block = x ^ k
        query = blocks[k][0] * BF(HEAD ** (-0.5))
        first_row = first_ref[k]

        def step(kb, carry):
            peak, total, acc = carry
            s = mm(kt_ref[kb], query)
            s = jnp.where(seen(first_row, part, kb, block, size), s, NEG)
            top = jnp.maximum(peak, jnp.max(s, axis=0, keepdims=True))
            p = jnp.exp(s - top)
            fade = jnp.exp(peak - top)
            total = fade * total + jnp.sum(p, axis=0, keepdims=True)
            return top, total, fade * acc + mm(v_ref[kb], p.astype(BF))

        start = (
            jnp.full((1, size), NEG, F32),
            jnp.zeros((1, size), F32),
            jnp.zeros((HEAD, size), F32),
        )
        peak, total, acc = lax.fori_loop(place_ref[2 + block], block + 1, step, start)
        acc = acc / total
        out_ref[k] = acc
        low_ref[k] = acc.astype(BF)
        lse_ref[k] = peak + jnp.log(total)


def attend(where_all, first_query, blocks):
    count = len(blocks)
    size = blocks[0].shape[2]
    return pl.pallas_call(
        functools.partial(attend_kernel, count),
        out_shape=(
            jax.ShapeDtypeStruct((4, HEAD, size), F32),
            jax.ShapeDtypeStruct((4, HEAD, size), BF),
            jax.ShapeDtypeStruct((4, 1, size), F32),
        ),
        in_specs=[IN_SMEM] + [IN_VMEM] * (1 + count),
        out_specs=(IN_VMEM,) * 3,
        scratch_shapes=[
            pltpu.VMEM((count, size, HEAD), BF),
            pltpu.VMEM((count, HEAD, size), BF),
        ],
        name="attend",
    )(where_all, first_query, *blocks)


def back_kernel(count, place_ref, first_ref, out_ref, lse_ref, *refs):
    blocks, grads = refs[:count], refs[count : count + 4]
    dq_ref, dk_ref, dv_ref, kt_ref, vt_ref, k_ref, dks_ref, dvs_ref = refs[count + 4 :]
    size = blocks[0].shape[2]
    x, part = place_ref[0], place_ref[1]
    for k in range(count):
        kt_ref[x ^ k] = blocks[k][1].T
        vt_ref[x ^ k] = blocks[k][2].T
        k_ref[x ^ k] = blocks[k][1]
    dks_ref[...] = jnp.zeros_like(dks_ref)
    dvs_ref[...] = jnp.zeros_like(dvs_ref)
    for k in range(4):
        block = x ^ k
        query = blocks[k][0] * BF(HEAD ** (-0.5))
        query_t = query.T
        grad = grads[k][...]
        grad_t = grad.T
        delta = jnp.sum(grad.astype(F32) * out_ref[k], axis=0, keepdims=True)
        lse = lse_ref[k]
        first_row = first_ref[k]

        def step(kb, dq):
            s = mm(kt_ref[kb], query)
            p = jnp.where(seen(first_row, part, kb, block, size), jnp.exp(s - lse), 0.0)
            dp = mm(vt_ref[kb], grad)
            ds = (p * (dp - delta)).astype(BF)
            dvs_ref[kb] += mm(p.astype(BF), grad_t)
            dks_ref[kb] += mm(ds, query_t)
            return dq + mm(k_ref[kb], ds)

        dq = lax.fori_loop(
            place_ref[2 + block], block + 1, step, jnp.zeros((HEAD, size), F32)
        )
        dq_ref[k] = dq * HEAD ** (-0.5)
    for k in range(count):
        dk_ref[k] = dks_ref[x ^ k].T
        dv_ref[k] = dvs_ref[x ^ k].T


def attend_back(where_all, first_query, blocks, grads, out, log_total):
    count = len(blocks)
    size = blocks[0].shape[2]
    return pl.pallas_call(
        functools.partial(back_kernel, count),
        out_shape=(
            jax.ShapeDtypeStruct((4, HEAD, size), F32),
            jax.ShapeDtypeStruct((count, HEAD, size), F32),
            jax.ShapeDtypeStruct((count, HEAD, size), F32),
        ),
        in_specs=[IN_SMEM] + [IN_VMEM] * (3 + count + 4),
        out_specs=(IN_VMEM,) * 3,
        scratch_shapes=[
            pltpu.VMEM((count, size, HEAD), BF),
            pltpu.VMEM((count, size, HEAD), BF),
            pltpu.VMEM((count, HEAD, size), BF),
            pltpu.VMEM((count, size, HEAD), F32),
            pltpu.VMEM((count, size, HEAD), F32),
        ],
        name="attend_back",
    )(where_all, first_query, out, log_total, *blocks, *grads)


def norm_scale(stream):
    return lax.rsqrt(jnp.mean(stream * stream, axis=-1, keepdims=True) + EPS)


def norm_back(stream, scale, gain, grad_normed):
    weighted = grad_normed * gain
    grad_gain = jnp.sum(grad_normed * stream * scale, axis=0, keepdims=True)
    grad_stream = scale * weighted - stream * scale**3 * jnp.mean(
        weighted * stream, axis=1, keepdims=True
    )
    return (grad_gain, grad_stream)


def local(
    tokens,
    out_grad,
    segment_ids,
    owner_order,
    attn_gain,
    w_query,
    w_key,
    w_value,
    w_out,
    mlp_gain,
    w_gate,
    w_up,
    w_down,
):
    plan = Plan()
    tok_rows = tokens.shape[0]
    part_rows = tok_rows // 4
    model = tokens.shape[1]

    gains = jnp.concatenate([attn_gain, mlp_gain], axis=0)
    gains = jnp.concatenate([gains, jnp.zeros((12, gains.shape[1]), BF)], axis=0)
    qkv_rows = 3 * w_query.shape[2] // 2
    out_rows = w_out.shape[1] // 2
    mlp_rows = w_down.shape[1] // 2
    counts = [qkv_rows, out_rows] + [mlp_rows] * 3

    def own_weights(level):
        qkv = [split_hidden(w[level].T) for w in (w_query, w_key, w_value)]
        return [
            jnp.concatenate(qkv, axis=1),
            split_hidden(w_out[level]),
            split_hidden(w_gate[level].T),
            split_hidden(w_up[level].T),
            split_hidden(w_down[level]),
        ]

    groups = own_weights(0)
    own = own_columns(plan, groups[0])
    far_first = plan.far(own)
    w_qkv = all_columns(plan, with_far(own, far_first, counts[:1]), True)
    own = own_columns(plan, jnp.concatenate(groups[2:4] + [groups[1], groups[4]], axis=1))
    far_gu = plan.far(tie(own[: 2 * mlp_rows], far_first))
    rest_gu = with_far(own[: 2 * mlp_rows], far_gu, counts[2:4])
    own_rest = own[2 * mlp_rows :]
    last_far = plan.far(tie(own_rest, far_gu))
    own_later = []
    for level in range(1, LAYERS):
        own = own_columns(plan, jnp.concatenate(own_weights(level), axis=1))
        own_later.append(own)
    cuts = [0, qkv_rows + out_rows]
    for _ in range(3):
        cuts.append(cuts[-1] + mlp_rows)
    full = [(w_qkv, None, None)]
    got = plan.core(gains)
    gain_pair = jnp.where(
        plan.c == 0,
        jnp.concatenate([gains, got], axis=1),
        jnp.concatenate([got, gains], axis=1),
    )
    gain_full = all_columns(plan, gain_pair, True).astype(F32)

    def own_rows(array):
        mine = lax.dynamic_slice_in_dim(array, plan.part * part_rows, part_rows, 0)
        got = plan.core(
            lax.dynamic_slice_in_dim(array, (plan.part ^ 2) * part_rows, part_rows, 0)
        )
        return to_block_order(plan, jnp.where(plan.c == plan.zp, mine, got))

    stream = own_rows(tokens).astype(F32)
    grad_stream = own_rows(out_grad).astype(F32)

    segment = jnp.where(plan.c == plan.zp, segment_ids, plan.core(segment_ids))[0]
    pack = segment.shape[0]
    index_all = jnp.arange(pack, dtype=jnp.int32)
    run_start = jnp.concatenate([jnp.ones((1,), dtype=bool), segment[1:] != segment[:-1]])
    run_first = lax.cummax(jnp.where(run_start, index_all, jnp.zeros_like(index_all)), axis=0)
    where_all = jnp.concatenate(
        [jnp.stack([plan.x, plan.part]).astype(jnp.int32), run_first[::tok_rows] // tok_rows]
    )

    def by_peer(row):
        grid = row.reshape(plan.ctx, 4, part_rows)
        blocks = [lax.dynamic_index_in_dim(grid, plan.x ^ k, 0, False) for k in range(4)]
        grid = jnp.stack(blocks)
        return jnp.concatenate(flip_list([grid[:, i] for i in range(4)], plan.part), axis=1)

    positions = by_peer((index_all - run_first).astype(F32))
    first_query = by_peer(run_first)[:, None, :]
    frequency = THETA ** (-(jnp.arange(HALF, dtype=F32) * 2.0 / HEAD))
    angles = frequency[None, :, None] * positions[:, None, :]
    cos_all, sine_all = jnp.cos(angles), jnp.sin(angles)
    cos_own, sine_own = cos_all[0], sine_all[0]

    kept = []
    first_values = None
    for level in range(LAYERS):
        w_qkv, w_o, w_mlp = full[level]
        width = 2 * mlp_rows
        scale_attn = norm_scale(stream)
        normed = (stream * scale_attn * gain_full[level : level + 1]).astype(BF)
        normed_all = gather_rows(plan, normed)
        qkv = dot(w_qkv, normed_all, 1, 1)
        if level == 0:
            w_gu = all_columns(plan, tie(rest_gu, qkv), False)
        qkv = qkv.reshape(2, 3, 2, HEAD, tok_rows)
        query = turn(qkv[:, 0], cos_own, sine_own).astype(BF)
        key = turn(qkv[:, 1], cos_own, sine_own).astype(BF)
        if level == 0:
            first_values = qkv[:, 2]
            mixed = first_values
        else:
            mixed = 0.5 * qkv[:, 2] + 0.5 * first_values
        heads = jnp.stack([query, key, mixed.astype(BF)], axis=2)
        heads = more_keys(plan, to_heads(plan, heads.reshape(4, 3, HEAD, tok_rows)))
        ahead = level + 1 < LAYERS
        far_next = []

        def next_far():
            i = len(far_next)
            piece = own_later[level][cuts[i] : cuts[i + 1]]
            return plan.far(tie(piece, far_next[-1] if far_next else last_far))

        if level == 0:
            heads, last_far = together(heads, last_far)
            rest = with_far(own_rest, last_far, [out_rows, mlp_rows])
            w_o = all_columns(plan, tie(rest[: 2 * out_rows], heads[0]), True)
            w_d = all_columns(plan, rest[2 * out_rows :], False)
            w_mlp = (w_gu, w_d)
        out, out_low, log_total = attend(where_all, first_query, heads)
        if ahead:
            out_low, got = together(out_low, next_far())
            far_next.append(got)
        attended = from_heads(plan, [out_low[k] for k in range(4)])
        attended = attended.reshape(4 * HEAD, tok_rows)
        if ahead:
            attended, got = together(attended, next_far())
            far_next.append(got)
        branch = sum_rows(plan, dot(attended, w_o, 0, 0))
        if ahead:
            branch, got = together(branch, next_far())
            far_next.append(got)
        middle = stream + branch
        scale_mlp = norm_scale(middle)
        normed_mlp = (middle * scale_mlp * gain_full[2 + level : 3 + level]).astype(BF)
        normed_mlp_all = gather_rows(plan, normed_mlp)
        w_gu, w_d = w_mlp
        full[level] = (w_qkv, w_o, w_gu, w_d)
        gate_up = dot(normed_mlp_all, w_gu, 1, 1)
        gate, upward = gate_up[:, :width], gate_up[:, width:]
        hidden = (gate * jax.nn.sigmoid(gate) * upward).astype(BF)
        if ahead:
            hidden, got = together(hidden, next_far())
            far_next.append(got)
            last_far = got
            own = own_later[level]
            w_attn = with_far(own[: cuts[1]], far_next[0], counts[:2])
            w_attn = all_columns(plan, w_attn, False)
            rest = with_far(own[cuts[1] :], jnp.concatenate(far_next[1:], axis=0), counts[2:])
            rest = all_columns(plan, rest, False)
            w_mlp = (rest[: 2 * width], rest[2 * width :])
            full.append((w_attn[: 2 * qkv_rows], w_attn[2 * qkv_rows :], w_mlp))
        result = middle + sum_rows(plan, dot(hidden, w_d, 1, 0))
        kept.append(
            (
                stream,
                scale_attn,
                normed_all,
                heads,
                out,
                log_total,
                attended,
                middle,
                scale_mlp,
                normed_mlp_all,
                gate_up,
                hidden,
            )
        )
        stream = result

    def to_pack(rows, other):
        mine = jnp.where(plan.c == plan.zp, rows, other)
        got = plan.core(jnp.where(plan.c == plan.zp, other, rows))
        count = rows.shape[0]
        near = plan.near(jnp.concatenate([mine, got], axis=0))
        return jnp.concatenate([mine, near[:count], got, near[count:]], axis=0)

    last = from_block_order(plan, stream.astype(BF))

    def weight_grads(grad_qkv, grad_wo, grad_wg, grad_wu, grad_wd):
        third = qkv_rows // 3

        def member(i):
            rows = [half[i * third : (i + 1) * third] for half in grad_qkv]
            return jnp.concatenate(rows, axis=0).T

        return (
            member(0),
            member(1),
            member(2),
            jnp.concatenate(grad_wo, axis=0),
            jnp.concatenate(grad_wg, axis=0).T,
            jnp.concatenate(grad_wu, axis=0).T,
            jnp.concatenate(grad_wd, axis=0),
        )

    grads = [None] * LAYERS
    gain_rows = [None] * (2 * LAYERS)
    carried = None
    for level in reversed(range(LAYERS)):
        (
            stream,
            scale_attn,
            normed_all,
            heads,
            out,
            log_total,
            attended,
            middle,
            scale_mlp,
            normed_mlp_all,
            gate_up,
            hidden,
        ) = kept[level]
        w_qkv, w_o, w_gu, w_d = full[level]
        width = 2 * mlp_rows
        branch = gather_rows(plan, grad_stream.astype(BF))
        grad_hidden = dot(branch, w_d, 1, 1)
        gate, upward = gate_up[:, :width], gate_up[:, width:]
        sigma = jax.nn.sigmoid(gate)
        grad_gate = (grad_hidden * upward * sigma * (1.0 + gate * (1.0 - sigma))).astype(BF)
        grad_up = (grad_hidden * gate * sigma).astype(BF)
        grad_gu = jnp.concatenate([grad_gate, grad_up], axis=1)
        if level == 0:
            grad_gu, sum_attn = together(grad_gu, sum_attn)
        grad_normed = sum_rows(plan, dot(grad_gu, w_gu, 1, 0))
        grad_wd = dot(hidden, branch, 0, 0).astype(BF)
        grad_wgu = dot(grad_gu, normed_mlp_all, 0, 0).astype(BF)
        grad_mlp = jnp.concatenate([grad_wgu, grad_wd], axis=0)
        grad_normed = tie(grad_normed, grad_mlp)
        sum_mlp = columns_sum(plan, grad_mlp, False)
        gain_rows[2 + level], through = norm_back(
            middle, scale_mlp, gain_full[2 + level : 3 + level], grad_normed
        )
        grad_middle = grad_stream + through
        branch = gather_rows(plan, grad_middle.astype(BF))
        if level == 0:
            mine_mlp, far = far_halves(tie(later_mlp, branch), counts[2:])
            mine_attn, far_attn = far_halves(sum_attn, counts[:2])
            far_a = plan.far(far[:mlp_rows])
        grad_wo = dot(attended, branch, 1, 0).astype(BF)
        grad_attended = dot(w_o, branch, 1, 1).astype(BF)
        if level == LAYERS - 1:
            last = tie(last, branch)
            other = plan.far(last)
        grad_attended = to_heads(plan, grad_attended.reshape(4, HEAD, tok_rows))
        if level == 0:
            grad_attended, far_a = together(grad_attended, far_a)
            far_b = plan.far(tie(far[mlp_rows : 2 * mlp_rows], far_a))
        elif level == LAYERS - 1:
            grad_attended, other = together(grad_attended, other)
            last = to_pack(last, other)
        grad_q, grad_k, grad_v = attend_back(
            where_all, first_query, heads, grad_attended, out, log_total
        )
        if level == 0:
            grad_q, far_b = together(grad_q, far_b)
            far_c = plan.far(tie(far[2 * mlp_rows :], far_b))
        grad_k = more_keys_sum(plan, grad_k)
        grad_v = more_keys_sum(plan, grad_v)
        if level > 0:
            grad_v = [0.5 * block for block in grad_v]
            if carried is None:
                carried = grad_v
            else:
                carried = [left + right for left, right in zip(carried, grad_v)]
        else:
            grad_v = [left + right for left, right in zip(grad_v, carried)]
        grad_heads = [
            jnp.stack(
                [
                    turn(grad_q[k], cos_all[k], -sine_all[k]).astype(BF),
                    turn(grad_k[k], cos_all[k], -sine_all[k]).astype(BF),
                    grad_v[k].astype(BF),
                ]
            )
            for k in range(4)
        ]
        grad_qkv = from_heads(plan, grad_heads).reshape(2, 2, 3, HEAD, tok_rows)
        grad_qkv = jnp.swapaxes(grad_qkv, 1, 2).reshape(-1, tok_rows)
        if level == 0:
            grad_qkv, far_c = together(grad_qkv, far_c)
            far_d = plan.far(tie(far_attn, far_c))
        elif level == LAYERS - 1:
            grad_qkv, last = together(grad_qkv, last)
            outputs = natural_rows(plan, last)
        grad_wqkv = dot(grad_qkv, normed_all, 1, 0).astype(BF)
        grad_attn = jnp.concatenate([grad_wqkv, grad_wo], axis=0)
        sum_attn = columns_sum(plan, grad_attn, level == 0)
        grad_normed = sum_rows(plan, dot(grad_qkv, w_qkv, 0, 0))
        if level == 0:
            grad_normed, far_d, sum_mlp = together(grad_normed, far_d, sum_mlp)
            got = jnp.concatenate([far_d, far_a, far_b, far_c], axis=0).astype(F32)
            mine = jnp.concatenate([mine_attn, mine_mlp], axis=0)
            grads[1] = weight_grads(*core_halves(plan, mine + got, counts))
        else:
            grad_normed, later_mlp = together(grad_normed, sum_mlp)
        gain_rows[level], through = norm_back(
            stream, scale_attn, gain_full[level : level + 1], grad_normed
        )
        grad_stream = grad_middle + through

    rows = from_block_order(plan, grad_stream.astype(BF))
    other = plan.far(rows)
    mine_mlp, far_mlp = far_halves(sum_mlp, counts[2:])
    far_mlp = plan.far(tie(far_mlp, other))
    grad_block = to_pack(rows, other)
    group_rows = tok_rows // plan.ctx
    owner_grid = owner_order[0].reshape(plan.ctx, plan.ctx, group_rows)
    local_rows = (
        lax.dynamic_index_in_dim(owner_grid, plan.x, 1, False) - plan.x * tok_rows
    ).reshape(tok_rows)
    local_rows = local_rows ^ (plan.part * part_rows)
    slots, far_mlp = together(grad_block[local_rows], far_mlp)
    grad_tokens = lax.all_to_all(slots, "ctx", split_axis=0, concat_axis=0, tiled=True)

    rest = core_halves(plan, mine_mlp + far_mlp.astype(F32), counts[2:])
    gain_sum = jnp.concatenate(gain_rows + [jnp.zeros((12, model), F32)], axis=0)
    gain_sum = gain_sum + plan.near(gain_sum)
    gain_sum = columns_sum(plan, gain_sum, True)
    mine, far = far_halves(sum_attn, counts[:2])
    far = jnp.concatenate([far, gain_sum.astype(BF)], axis=0)
    far = plan.far(tie(far, far_mlp))
    grad_tokens, far = together(grad_tokens, far)
    grad_tokens = grad_tokens.astype(F32)
    total = jnp.concatenate([mine, gain_sum], axis=0) + far.astype(F32)
    first = core_halves(plan, total, [qkv_rows, out_rows, gain_sum.shape[0]])
    total = first[2][0] + first[2][1]
    grads[0] = weight_grads(first[0], first[1], *rest)

    stacked = [jnp.stack([grads[level][i] for level in range(LAYERS)]) for i in range(7)]
    return (
        outputs,
        grad_tokens,
        total[:2],
        stacked[0],
        stacked[1],
        stacked[2],
        stacked[3],
        total[2:4],
        stacked[4],
        stacked[5],
        stacked[6],
    )


def solution(mesh):
    columns = P(None, ("fsdp", "ctx"), "tp")
    rows = P(None, "tp", ("fsdp", "ctx"))
    gain = P(None, ("fsdp", "ctx"))
    tokens = P(("fsdp", "ctx"), None)
    return jax.shard_map(
        local,
        mesh=mesh,
        in_specs=(
            tokens,
            tokens,
            P("fsdp", None),
            P("fsdp", None),
            gain,
            columns,
            columns,
            columns,
            rows,
            gain,
            columns,
            columns,
            rows,
        ),
        out_specs=(
            tokens,
            tokens,
            gain,
            columns,
            columns,
            columns,
            rows,
            gain,
            columns,
            columns,
            rows,
        ),
        check_vma=False,
    )
```

```python
import functools

import jax
import jax.numpy as jnp
from jax import lax
from jax.experimental import pallas as pl
from jax.experimental.pallas import tpu as pltpu
from jax.sharding import PartitionSpec as P

HEAD = 64
HALF = HEAD // 2
LAYERS = 2
EPS = 1e-05
THETA = 10000.0
NEG = -1e30
BF = jnp.bfloat16
F32 = jnp.float32
IN_VMEM = pl.BlockSpec(memory_space=pltpu.VMEM)
IN_SMEM = pl.BlockSpec(memory_space=pltpu.SMEM)


def dot(left, right, left_dim, right_dim):
    return lax.dot_general(
        left, right, (((left_dim,), (right_dim,)), ((), ())), preferred_element_type=F32
    )


def mm(left, right):
    return jnp.dot(left, right, preferred_element_type=F32)


class Plan:
    def __init__(self):
        self.fsdp = lax.axis_size("fsdp")
        self.ctx = lax.axis_size("ctx")
        self.tp = lax.axis_size("tp")
        self.high = self.fsdp // 2
        f = lax.axis_index("fsdp")
        z = lax.axis_index("tp")
        self.c = f % 2
        self.fh = f // 2
        self.x = lax.axis_index("ctx")
        self.zl = z % 2
        self.zp = z // 2
        self.ci = self.x % 4
        self.part = self.c * 2 + self.zl
        self.peers = self.high * self.ctx

    def core(self, value):
        return lax.ppermute(value, "fsdp", [(i, i ^ 1) for i in range(self.fsdp)])

    def near(self, value):
        return lax.ppermute(value, "tp", [(i, i ^ 1) for i in range(self.tp)])

    def far(self, value):
        return lax.ppermute(value, "tp", [(i, i ^ 2) for i in range(self.tp)])

    def side(self, value, k):
        return lax.ppermute(value, "ctx", [(i, i ^ k) for i in range(self.ctx)])

    def high_fsdp(self, value, k):
        return lax.ppermute(value, "fsdp", [(i, i ^ (2 * k)) for i in range(self.fsdp)])


def flip_list(blocks, index):
    bit = 1
    while bit < len(blocks):
        on = (index & bit) != 0
        blocks = [jnp.where(on, blocks[i ^ bit], blocks[i]) for i in range(len(blocks))]
        bit *= 2
    return blocks


def place(blocks, index, axis):
    width = blocks[0].shape[axis]
    shape = list(blocks[0].shape)
    shape[axis] = width * len(blocks)
    full = jnp.zeros(shape, blocks[0].dtype)
    for i, block in enumerate(blocks):
        full = lax.dynamic_update_slice_in_dim(full, block, (index ^ i) * width, axis)
    return full


def to_block_order(plan, rows):
    width = rows.shape[1] // (2 * plan.peers)
    parts = []
    for h in range(plan.high):
        for x in range(plan.ctx):
            for c in range(2):
                start = ((h * 2 + c) * plan.ctx + x) * width
                parts.append(rows[:, start : start + width])
    return jnp.concatenate(parts, axis=1)


def from_block_order(plan, rows):
    width = rows.shape[1] // (2 * plan.peers)
    parts = []
    for h in range(plan.high):
        for c in range(2):
            for x in range(plan.ctx):
                start = ((h * plan.ctx + x) * 2 + c) * width
                parts.append(rows[:, start : start + width])
    return jnp.concatenate(parts, axis=1)


def gather_rows(plan, rows):
    pair = jnp.concatenate([rows, plan.near(rows)], axis=0)
    return jnp.concatenate([pair, plan.core(pair)], axis=0)


def sum_rows(plan, partial):
    half = partial.shape[0] // 2
    pair = partial[:half] + plan.core(partial[half:].astype(BF)).astype(F32)
    half = half // 2
    return pair[:half] + plan.near(pair[half:].astype(BF)).astype(F32)


def natural_rows(plan, rows):
    count = rows.shape[0] // 4
    parts = [
        lax.dynamic_slice_in_dim(rows, (plan.part ^ i) * count, count, 0) for i in range(4)
    ]
    return jnp.concatenate(parts, axis=0)


def own_columns(plan, halves):
    keep = lax.dynamic_index_in_dim(halves, plan.c, 0, False)
    got = plan.core(lax.dynamic_index_in_dim(halves, 1 - plan.c, 0, False))
    return jnp.where(
        plan.c == 0,
        jnp.concatenate([keep, got], axis=1),
        jnp.concatenate([got, keep], axis=1),
    )


def all_columns(plan, rows, direct):
    if direct and plan.peers == 4:
        return place([rows] + [plan.side(rows, k) for k in range(1, 4)], plan.x, 1)
    full = lax.all_gather(rows, "ctx", axis=1, tiled=True)
    if plan.high > 1:
        parts = [full] + [plan.high_fsdp(full, k) for k in range(1, plan.high)]
        full = place(parts, plan.fh, 1)
    return full


def columns_sum(plan, grad, direct):
    if plan.high > 1:
        width = grad.shape[1] // plan.high
        parts = [
            lax.dynamic_slice_in_dim(grad, (plan.fh ^ k) * width, width, 1)
            for k in range(plan.high)
        ]
        grad = parts[0]
        for k in range(1, plan.high):
            grad = grad + plan.high_fsdp(parts[k], k)
    if direct and plan.ctx == 4:
        width = grad.shape[1] // 4
        parts = [
            lax.dynamic_slice_in_dim(grad, (plan.x ^ k) * width, width, 1) for k in range(4)
        ]
        total = parts[0].astype(F32)
        for k in range(1, 4):
            total = total + plan.side(parts[k], k).astype(F32)
        return total
    return lax.psum_scatter(grad, "ctx", scatter_dimension=1, tiled=True)


def together(value, *others):
    many = isinstance(value, list)
    got = lax.optimization_barrier((*value, *others) if many else (value, *others))
    count = len(value) if many else 1
    first = list(got[:count]) if many else got[0]
    return (first, *got[count:])


def with_far(own, far, counts):
    parts = []
    start = 0
    for rows in counts:
        parts += [own[start : start + rows], far[start : start + rows]]
        start += rows
    return jnp.concatenate(parts, axis=0)


def far_halves(total, counts):
    mine, far = [], []
    start = 0
    for rows in counts:
        mine.append(total[start : start + rows])
        far.append(total[start + rows : start + 2 * rows])
        start += 2 * rows
    return jnp.concatenate(mine, axis=0).astype(F32), jnp.concatenate(far, axis=0).astype(BF)


def core_halves(plan, own, counts):
    width = own.shape[1]
    left, right = own[:, : width // 2], own[:, width // 2 :]
    kept = jnp.where(plan.c == 0, left, right)
    got = plan.core(jnp.where(plan.c == 0, right, left).astype(BF)).astype(F32)
    low = jnp.where(plan.c == 0, kept, got)
    high = jnp.where(plan.c == 0, got, kept)
    out = []
    start = 0
    for rows in counts:
        out.append((low[start : start + rows], high[start : start + rows]))
        start += rows
    return out


def split_hidden(weight):
    return weight.reshape(2, weight.shape[0] // 2, weight.shape[1])


def turn(values, cos_tab, sine_tab):
    first, second = values[..., :HALF, :], values[..., HALF:, :]
    return jnp.concatenate(
        [first * cos_tab - second * sine_tab, second * cos_tab + first * sine_tab], axis=-2
    )


def to_heads(plan, values):
    got = [lax.dynamic_index_in_dim(values, plan.ci, 0, False)]
    for k in range(1, 4):
        got.append(plan.side(lax.dynamic_index_in_dim(values, plan.ci ^ k, 0, False), k))
    return got


def from_heads(plan, blocks):
    got = [blocks[0]] + [plan.side(blocks[k], k) for k in range(1, 4)]
    return place([block[None] for block in got], plan.ci, 0)


def more_keys(plan, blocks):
    full = list(blocks)
    for m in range(1, plan.ctx // 4):
        full += [plan.side(block, 4 * m) for block in blocks]
    return full


def more_keys_sum(plan, blocks):
    total = list(blocks[:4])
    for m in range(1, plan.ctx // 4):
        total = [total[k] + plan.side(blocks[4 * m + k], 4 * m) for k in range(4)]
    return total


def seen(first_row, part, key_block, query_block, size):
    turned = part * (size // 4)
    key = key_block * size + (lax.broadcasted_iota(jnp.int32, (size, 1), 0) ^ turned)
    query = query_block * size + (lax.broadcasted_iota(jnp.int32, (1, size), 1) ^ turned)
    return (key <= query) & (key >= first_row)


def attend_kernel(count, place_ref, first_ref, *refs):
    blocks, (out_ref, low_ref, lse_ref, kt_ref, v_ref) = refs[:count], refs[count:]
    size = blocks[0].shape[2]
    x, part = place_ref[0], place_ref[1]
    for k in range(count):
        kt_ref[x ^ k] = blocks[k][1].T
        v_ref[x ^ k] = blocks[k][2]
    for k in range(4):
        block = x ^ k
        query = blocks[k][0] * BF(HEAD ** (-0.5))
        first_row = first_ref[k]

        def step(kb, carry):
            peak, total, acc = carry
            s = mm(kt_ref[kb], query)
            s = jnp.where(seen(first_row, part, kb, block, size), s, NEG)
            top = jnp.maximum(peak, jnp.max(s, axis=0, keepdims=True))
            p = jnp.exp(s - top)
            fade = jnp.exp(peak - top)
            total = fade * total + jnp.sum(p, axis=0, keepdims=True)
            return top, total, fade * acc + mm(v_ref[kb], p.astype(BF))

        start = (
            jnp.full((1, size), NEG, F32),
            jnp.zeros((1, size), F32),
            jnp.zeros((HEAD, size), F32),
        )
        peak, total, acc = lax.fori_loop(place_ref[2 + block], block + 1, step, start)
        acc = acc / total
        out_ref[k] = acc
        low_ref[k] = acc.astype(BF)
        lse_ref[k] = peak + jnp.log(total)


def attend(where_all, first_query, blocks):
    count = len(blocks)
    size = blocks[0].shape[2]
    return pl.pallas_call(
        functools.partial(attend_kernel, count),
        out_shape=(
            jax.ShapeDtypeStruct((4, HEAD, size), F32),
            jax.ShapeDtypeStruct((4, HEAD, size), BF),
            jax.ShapeDtypeStruct((4, 1, size), F32),
        ),
        in_specs=[IN_SMEM] + [IN_VMEM] * (1 + count),
        out_specs=(IN_VMEM,) * 3,
        scratch_shapes=[
            pltpu.VMEM((count, size, HEAD), BF),
            pltpu.VMEM((count, HEAD, size), BF),
        ],
        name="attend",
    )(where_all, first_query, *blocks)


def back_kernel(count, place_ref, first_ref, out_ref, lse_ref, *refs):
    blocks, grads = refs[:count], refs[count : count + 4]
    dq_ref, dk_ref, dv_ref, kt_ref, vt_ref, k_ref, dks_ref, dvs_ref = refs[count + 4 :]
    size = blocks[0].shape[2]
    x, part = place_ref[0], place_ref[1]
    for k in range(count):
        kt_ref[x ^ k] = blocks[k][1].T
        vt_ref[x ^ k] = blocks[k][2].T
        k_ref[x ^ k] = blocks[k][1]
    dks_ref[...] = jnp.zeros_like(dks_ref)
    dvs_ref[...] = jnp.zeros_like(dvs_ref)
    for k in range(4):
        block = x ^ k
        query = blocks[k][0] * BF(HEAD ** (-0.5))
        query_t = query.T
        grad = grads[k][...]
        grad_t = grad.T
        delta = jnp.sum(grad.astype(F32) * out_ref[k], axis=0, keepdims=True)
        lse = lse_ref[k]
        first_row = first_ref[k]

        def step(kb, dq):
            s = mm(kt_ref[kb], query)
            p = jnp.where(seen(first_row, part, kb, block, size), jnp.exp(s - lse), 0.0)
            dp = mm(vt_ref[kb], grad)
            ds = (p * (dp - delta)).astype(BF)
            dvs_ref[kb] += mm(p.astype(BF), grad_t)
            dks_ref[kb] += mm(ds, query_t)
            return dq + mm(k_ref[kb], ds)

        dq = lax.fori_loop(
            place_ref[2 + block], block + 1, step, jnp.zeros((HEAD, size), F32)
        )
        dq_ref[k] = dq * HEAD ** (-0.5)
    for k in range(count):
        dk_ref[k] = dks_ref[x ^ k].T
        dv_ref[k] = dvs_ref[x ^ k].T


def attend_back(where_all, first_query, blocks, grads, out, log_total):
    count = len(blocks)
    size = blocks[0].shape[2]
    return pl.pallas_call(
        functools.partial(back_kernel, count),
        out_shape=(
            jax.ShapeDtypeStruct((4, HEAD, size), F32),
            jax.ShapeDtypeStruct((count, HEAD, size), F32),
            jax.ShapeDtypeStruct((count, HEAD, size), F32),
        ),
        in_specs=[IN_SMEM] + [IN_VMEM] * (3 + count + 4),
        out_specs=(IN_VMEM,) * 3,
        scratch_shapes=[
            pltpu.VMEM((count, size, HEAD), BF),
            pltpu.VMEM((count, size, HEAD), BF),
            pltpu.VMEM((count, HEAD, size), BF),
            pltpu.VMEM((count, size, HEAD), F32),
            pltpu.VMEM((count, size, HEAD), F32),
        ],
        name="attend_back",
    )(where_all, first_query, out, log_total, *blocks, *grads)


def norm_scale(stream):
    return lax.rsqrt(jnp.mean(stream * stream, axis=-1, keepdims=True) + EPS)


def norm_back(stream, scale, gain, grad_normed):
    weighted = grad_normed * gain
    grad_gain = jnp.sum(grad_normed * stream * scale, axis=0, keepdims=True)
    grad_stream = scale * weighted - stream * scale**3 * jnp.mean(
        weighted * stream, axis=1, keepdims=True
    )
    return (grad_gain, grad_stream)


def local(
    tokens,
    out_grad,
    segment_ids,
    owner_order,
    attn_gain,
    w_query,
    w_key,
    w_value,
    w_out,
    mlp_gain,
    w_gate,
    w_up,
    w_down,
):
    plan = Plan()
    tok_rows = tokens.shape[0]
    part_rows = tok_rows // 4
    model = tokens.shape[1]

    gains = jnp.concatenate([attn_gain, mlp_gain], axis=0)
    gains = jnp.concatenate([gains, jnp.zeros((12, gains.shape[1]), BF)], axis=0)
    qkv_rows = 3 * w_query.shape[2] // 2
    out_rows = w_out.shape[1] // 2
    mlp_rows = w_down.shape[1] // 2
    counts = [qkv_rows, out_rows] + [mlp_rows] * 3

    def own_weights(level):
        qkv = [split_hidden(w[level].T) for w in (w_query, w_key, w_value)]
        return [
            jnp.concatenate(qkv, axis=1),
            split_hidden(w_out[level]),
            split_hidden(w_gate[level].T),
            split_hidden(w_up[level].T),
            split_hidden(w_down[level]),
        ]

    groups = own_weights(0)
    own = own_columns(plan, groups[0])
    far_first = plan.far(own)
    own_rest = own_columns(plan, jnp.concatenate(groups[1:], axis=1))
    got = plan.core(gains)
    gain_pair = jnp.where(
        plan.c == 0,
        jnp.concatenate([gains, got], axis=1),
        jnp.concatenate([got, gains], axis=1),
    )
    own_rest, far_first = together(own_rest, far_first)
    first = jnp.concatenate([own, far_first, gain_pair], axis=0)
    first = all_columns(plan, first, True)
    w_qkv, gain_full = first[: 2 * qkv_rows], first[2 * qkv_rows :].astype(F32)
    last_far = plan.far(own_rest)
    own_later = []
    for level in range(1, LAYERS):
        own = own_columns(plan, jnp.concatenate(own_weights(level), axis=1))
        own_later.append(own)
    cuts = [0, qkv_rows + out_rows]
    for _ in range(3):
        cuts.append(cuts[-1] + mlp_rows)
    full = [(w_qkv, None, None)]
    def own_rows(array):
        mine = lax.dynamic_slice_in_dim(array, plan.part * part_rows, part_rows, 0)
        got = plan.core(
            lax.dynamic_slice_in_dim(array, (plan.part ^ 2) * part_rows, part_rows, 0)
        )
        return to_block_order(plan, jnp.where(plan.c == plan.zp, mine, got))

    token_rows = own_rows(tokens)
    tokens_all = gather_rows(plan, token_rows).astype(F32)
    stream = token_rows.astype(F32)
    grad_stream = own_rows(out_grad).astype(F32)

    segment = jnp.where(plan.c == plan.zp, segment_ids, plan.core(segment_ids))[0]
    pack = segment.shape[0]
    index_all = jnp.arange(pack, dtype=jnp.int32)
    run_start = jnp.concatenate([jnp.ones((1,), dtype=bool), segment[1:] != segment[:-1]])
    run_first = lax.cummax(jnp.where(run_start, index_all, jnp.zeros_like(index_all)), axis=0)
    where_all = jnp.concatenate(
        [jnp.stack([plan.x, plan.part]).astype(jnp.int32), run_first[::tok_rows] // tok_rows]
    )

    def by_peer(row):
        grid = row.reshape(plan.ctx, 4, part_rows)
        blocks = [lax.dynamic_index_in_dim(grid, plan.x ^ k, 0, False) for k in range(4)]
        grid = jnp.stack(blocks)
        return jnp.concatenate(flip_list([grid[:, i] for i in range(4)], plan.part), axis=1)

    positions = by_peer((index_all - run_first).astype(F32))
    first_query = by_peer(run_first)[:, None, :]
    frequency = THETA ** (-(jnp.arange(HALF, dtype=F32) * 2.0 / HEAD))
    angles = frequency[None, :, None] * positions[:, None, :]
    cos_all, sine_all = jnp.cos(angles), jnp.sin(angles)
    cos_own, sine_own = cos_all[0], sine_all[0]

    kept = []
    first_values = None
    out_branch = None
    for level in range(LAYERS):
        w_qkv, w_o, w_mlp = full[level]
        width = 2 * mlp_rows
        if level == 0:
            scale_all = norm_scale(tokens_all)
            scale_attn = scale_all[:part_rows]
            normed_all = (tokens_all * scale_all * gain_full[:1]).astype(BF)
        else:
            scale_attn = norm_scale(stream)
            normed = (stream * scale_attn * gain_full[level : level + 1]).astype(BF)
            normed_all = gather_rows(plan, normed)
        qkv = dot(w_qkv, normed_all, 1, 1)
        if level == 0:
            rest = with_far(own_rest, last_far, counts[1:])
            rest, w_o = rest[2 * out_rows :], rest[: 2 * out_rows]
            rest, qkv = together(rest, qkv)
            rest = all_columns(plan, rest, False)
            w_mlp = (rest[: 2 * width], rest[2 * width :])
        qkv = qkv.reshape(2, 3, 2, HEAD, tok_rows)
        query = turn(qkv[:, 0], cos_own, sine_own).astype(BF)
        key = turn(qkv[:, 1], cos_own, sine_own).astype(BF)
        if level == 0:
            first_values = qkv[:, 2]
            mixed = first_values
        else:
            mixed = 0.5 * qkv[:, 2] + 0.5 * first_values
        heads = jnp.stack([query, key, mixed.astype(BF)], axis=2)
        heads = more_keys(plan, to_heads(plan, heads.reshape(4, 3, HEAD, tok_rows)))
        ahead = level + 1 < LAYERS
        far_next = []

        def next_far():
            i = len(far_next)
            piece = own_later[level][cuts[i] : cuts[i + 1]]
            if far_next:
                piece, far_next[-1] = together(piece, far_next[-1])
            return plan.far(piece)

        if ahead:
            heads, got = together(heads, next_far())
            far_next.append(got)
        if level == 0:
            heads, w_o = together(heads, w_o)
            w_o = all_columns(plan, w_o, True)
        out, out_low, log_total = attend(where_all, first_query, heads)
        if ahead:
            out_low, got = together(out_low, next_far())
            far_next.append(got)
        if level == LAYERS - 1:
            out_low, out_branch = together(out_low, gather_rows(plan, grad_stream.astype(BF)))
        attended = from_heads(plan, [out_low[k] for k in range(4)])
        attended = attended.reshape(4 * HEAD, tok_rows)
        if ahead:
            attended, got = together(attended, next_far())
            far_next.append(got)
        branch = sum_rows(plan, dot(attended, w_o, 0, 0))
        if ahead:
            branch, got = together(branch, next_far())
            far_next.append(got)
            own = own_later[level]
            w_attn = with_far(own[: cuts[1]], far_next[0], counts[:2])
            w_attn = all_columns(plan, w_attn, False)
            rest = with_far(own[cuts[1] :], jnp.concatenate(far_next[1:], axis=0), counts[2:])
            rest = all_columns(plan, rest, False)
            later = (rest[: 2 * width], rest[2 * width :])
            full.append((w_attn[: 2 * qkv_rows], w_attn[2 * qkv_rows :], later))
        middle = stream + branch
        scale_mlp = norm_scale(middle)
        normed_mlp = (middle * scale_mlp * gain_full[2 + level : 3 + level]).astype(BF)
        normed_mlp_all = gather_rows(plan, normed_mlp)
        w_gu, w_d = w_mlp
        full[level] = (w_qkv, w_o, w_gu, w_d)
        gate_up = dot(normed_mlp_all, w_gu, 1, 1)
        gate, upward = gate_up[:, :width], gate_up[:, width:]
        hidden = (gate * jax.nn.sigmoid(gate) * upward).astype(BF)
        if level < LAYERS - 1:
            result = middle + sum_rows(plan, dot(hidden, w_d, 1, 0))
        kept.append(
            (
                stream,
                scale_attn,
                normed_all,
                heads,
                out,
                log_total,
                attended,
                middle,
                scale_mlp,
                normed_mlp_all,
                gate_up,
                hidden,
            )
        )
        if level < LAYERS - 1:
            stream = result

    def to_pack(rows, other):
        mine = jnp.where(plan.c == plan.zp, rows, other)
        got = plan.core(jnp.where(plan.c == plan.zp, other, rows))
        count = rows.shape[0]
        near = plan.near(jnp.concatenate([mine, got], axis=0))
        return jnp.concatenate([mine, near[:count], got, near[count:]], axis=0)


    def weight_grads(grad_qkv, grad_wo, grad_wg, grad_wu, grad_wd):
        third = qkv_rows // 3

        def member(i):
            rows = [half[i * third : (i + 1) * third] for half in grad_qkv]
            return jnp.concatenate(rows, axis=0).T

        return (
            member(0),
            member(1),
            member(2),
            jnp.concatenate(grad_wo, axis=0),
            jnp.concatenate(grad_wg, axis=0).T,
            jnp.concatenate(grad_wu, axis=0).T,
            jnp.concatenate(grad_wd, axis=0),
        )

    grads = [None] * LAYERS
    gain_rows = [None] * (2 * LAYERS)
    carried = None
    for level in reversed(range(LAYERS)):
        (
            stream,
            scale_attn,
            normed_all,
            heads,
            out,
            log_total,
            attended,
            middle,
            scale_mlp,
            normed_mlp_all,
            gate_up,
            hidden,
        ) = kept[level]
        w_qkv, w_o, w_gu, w_d = full[level]
        width = 2 * mlp_rows
        if level == LAYERS - 1:
            branch = out_branch
        else:
            branch = gather_rows(plan, grad_stream.astype(BF))
        grad_hidden = dot(branch, w_d, 1, 1)
        gate, upward = gate_up[:, :width], gate_up[:, width:]
        sigma = jax.nn.sigmoid(gate)
        grad_gate = (grad_hidden * upward * sigma * (1.0 + gate * (1.0 - sigma))).astype(BF)
        grad_up = (grad_hidden * gate * sigma).astype(BF)
        grad_gu = jnp.concatenate([grad_gate, grad_up], axis=1)
        partial, grad_gu = together(dot(grad_gu, w_gu, 1, 0), grad_gu)
        grad_normed = sum_rows(plan, partial)
        grad_wd = dot(hidden, branch, 0, 0).astype(BF)
        grad_wgu = dot(grad_gu, normed_mlp_all, 0, 0).astype(BF)
        grad_mlp = jnp.concatenate([grad_wgu, grad_wd], axis=0)
        if level == 0:
            grad_normed, grad_mlp, sum_attn = together(grad_normed, grad_mlp, sum_attn)
        else:
            grad_normed, grad_mlp = together(grad_normed, grad_mlp)
        sum_mlp = columns_sum(plan, grad_mlp, False)
        gain_rows[2 + level], through = norm_back(
            middle, scale_mlp, gain_full[2 + level : 3 + level], grad_normed
        )
        grad_middle = grad_stream + through
        branch = gather_rows(plan, grad_middle.astype(BF))
        if level == 0:
            later_mlp, branch = together(later_mlp, branch)
            mine_mlp, far = far_halves(later_mlp, counts[2:])
            mine_attn, far_attn = far_halves(sum_attn, counts[:2])
            far_a = plan.far(far[: 2 * mlp_rows])
        if level == LAYERS - 1:
            partial, branch = together(dot(hidden, w_d, 1, 0), branch)
            last = sum_rows(plan, partial)
        grad_wo = dot(attended, branch, 1, 0).astype(BF)
        grad_attended = dot(w_o, branch, 1, 1).astype(BF)
        grad_attended = to_heads(plan, grad_attended.reshape(4, HEAD, tok_rows))
        if level == 0:
            far_b, far_a = together(far[2 * mlp_rows :], far_a)
            far_b = plan.far(far_b)
            grad_attended, far_a, grad_wo = together(grad_attended, far_a, grad_wo)
            sum_wo = columns_sum(plan, grad_wo, True)
        elif level == LAYERS - 1:
            grad_attended, last = together(grad_attended, last)
            last = from_block_order(plan, (middle + last).astype(BF))
            other = plan.far(last)
        grad_q, grad_k, grad_v = attend_back(
            where_all, first_query, heads, grad_attended, out, log_total
        )
        if level == 0:
            far_attn, far_b = together(far_attn, far_b)
            far_c = plan.far(far_attn)
            grad_q, far_b, sum_wo = together(grad_q, far_b, sum_wo)
        elif level == LAYERS - 1:
            grad_q, other = together(grad_q, other)
            last = to_pack(last, other)
        grad_k = more_keys_sum(plan, grad_k)
        grad_v = more_keys_sum(plan, grad_v)
        if level > 0:
            grad_v = [0.5 * block for block in grad_v]
            if carried is None:
                carried = grad_v
            else:
                carried = [left + right for left, right in zip(carried, grad_v)]
        else:
            grad_v = [left + right for left, right in zip(grad_v, carried)]
        grad_heads = [
            jnp.stack(
                [
                    turn(grad_q[k], cos_all[k], -sine_all[k]).astype(BF),
                    turn(grad_k[k], cos_all[k], -sine_all[k]).astype(BF),
                    grad_v[k].astype(BF),
                ]
            )
            for k in range(4)
        ]
        grad_qkv = from_heads(plan, grad_heads).reshape(2, 2, 3, HEAD, tok_rows)
        grad_qkv = jnp.swapaxes(grad_qkv, 1, 2).reshape(-1, tok_rows)
        if level == 0:
            mine_first, far = far_halves(sum_mlp, counts[2:])
            far_d, far_c = together(far[: 2 * mlp_rows], far_c)
            far_d = plan.far(far_d)
            grad_qkv, far_c = together(grad_qkv, far_c)
        elif level == LAYERS - 1:
            grad_qkv, last = together(grad_qkv, last)
            outputs = natural_rows(plan, last)
        grad_wqkv = dot(grad_qkv, normed_all, 1, 0).astype(BF)
        grad_normed = sum_rows(plan, dot(grad_qkv, w_qkv, 0, 0))
        if level == 0:
            far_e = far[2 * mlp_rows :]
            grad_normed, far_d, far_e, grad_wqkv = together(
                grad_normed, far_d, far_e, grad_wqkv
            )
            far_e = plan.far(far_e)
            sum_qkv = columns_sum(plan, grad_wqkv, True)
            got = jnp.concatenate([far_c, far_a, far_b], axis=0).astype(F32)
            mine = jnp.concatenate([mine_attn, mine_mlp], axis=0)
            grads[1] = weight_grads(*core_halves(plan, mine + got, counts))
        else:
            grad_normed, later_mlp = together(grad_normed, sum_mlp)
            grad_attn = jnp.concatenate([grad_wqkv, grad_wo], axis=0)
            sum_attn = columns_sum(plan, grad_attn, False)
        gain_rows[level], through = norm_back(
            stream, scale_attn, gain_full[level : level + 1], grad_normed
        )
        grad_stream = grad_middle + through

    rows = from_block_order(plan, grad_stream.astype(BF))
    other, sum_qkv = together(plan.far(rows), sum_qkv)
    group_rows = tok_rows // plan.ctx
    owner_grid = owner_order[0].reshape(plan.ctx, plan.ctx, group_rows)
    local_rows = (
        lax.dynamic_index_in_dim(owner_grid, plan.x, 1, False) - plan.x * tok_rows
    ).reshape(tok_rows)
    local_rows = local_rows ^ (plan.part * part_rows)
    slots, far_e = together(to_pack(rows, other)[local_rows], far_e)
    grad_tokens = lax.all_to_all(slots, "ctx", split_axis=0, concat_axis=0, tiled=True)

    got = jnp.concatenate([far_d, far_e], axis=0).astype(F32)
    rest = core_halves(plan, mine_first + got, counts[2:])
    gain_sum = jnp.concatenate(gain_rows + [jnp.zeros((12, model), F32)], axis=0)
    gain_sum = gain_sum + plan.near(gain_sum)
    gain_sum = columns_sum(plan, gain_sum, True)
    mine, far = far_halves(jnp.concatenate([sum_qkv, sum_wo], axis=0), counts[:2])
    far = jnp.concatenate([far, gain_sum.astype(BF)], axis=0)
    far = plan.far(far)
    grad_tokens, far = together(grad_tokens, far)
    grad_tokens = grad_tokens.astype(F32)
    total = jnp.concatenate([mine, gain_sum], axis=0) + far.astype(F32)
    first = core_halves(plan, total, [qkv_rows, out_rows, gain_sum.shape[0]])
    total = first[2][0] + first[2][1]
    grads[0] = weight_grads(first[0], first[1], *rest)

    stacked = [jnp.stack([grads[level][i] for level in range(LAYERS)]) for i in range(7)]
    return (
        outputs,
        grad_tokens,
        total[:2],
        stacked[0],
        stacked[1],
        stacked[2],
        stacked[3],
        total[2:4],
        stacked[4],
        stacked[5],
        stacked[6],
    )


def solution(mesh):
    columns = P(None, ("fsdp", "ctx"), "tp")
    rows = P(None, "tp", ("fsdp", "ctx"))
    gain = P(None, ("fsdp", "ctx"))
    tokens = P(("fsdp", "ctx"), None)
    return jax.shard_map(
        local,
        mesh=mesh,
        in_specs=(
            tokens,
            tokens,
            P("fsdp", None),
            P("fsdp", None),
            gain,
            columns,
            columns,
            columns,
            rows,
            gain,
            columns,
            columns,
            rows,
        ),
        out_specs=(
            tokens,
            tokens,
            gain,
            columns,
            columns,
            columns,
            rows,
            gain,
            columns,
            columns,
            rows,
        ),
        check_vma=False,
    )
```

```python
import functools

import jax
import jax.numpy as jnp
from jax import lax
from jax.experimental import pallas as pl
from jax.experimental.pallas import tpu as pltpu
from jax.sharding import PartitionSpec as P

HEAD = 64
HALF = HEAD // 2
LAYERS = 2
EPS = 1e-05
THETA = 10000.0
NEG = -1e30
BF = jnp.bfloat16
F32 = jnp.float32
IN_VMEM = pl.BlockSpec(memory_space=pltpu.VMEM)
IN_SMEM = pl.BlockSpec(memory_space=pltpu.SMEM)


def dot(left, right, left_dim, right_dim):
    return lax.dot_general(
        left, right, (((left_dim,), (right_dim,)), ((), ())), preferred_element_type=F32
    )


def mm(left, right):
    return jnp.dot(left, right, preferred_element_type=F32)


class Plan:
    def __init__(self):
        self.fsdp = lax.axis_size("fsdp")
        self.ctx = lax.axis_size("ctx")
        self.tp = lax.axis_size("tp")
        self.high = self.fsdp // 2
        f = lax.axis_index("fsdp")
        z = lax.axis_index("tp")
        self.c = f % 2
        self.fh = f // 2
        self.x = lax.axis_index("ctx")
        self.zl = z % 2
        self.zp = z // 2
        self.ci = self.x % 4
        self.part = self.c * 2 + self.zl
        self.peers = self.high * self.ctx

    def core(self, value):
        return lax.ppermute(value, "fsdp", [(i, i ^ 1) for i in range(self.fsdp)])

    def near(self, value):
        return lax.ppermute(value, "tp", [(i, i ^ 1) for i in range(self.tp)])

    def far(self, value):
        return lax.ppermute(value, "tp", [(i, i ^ 2) for i in range(self.tp)])

    def side(self, value, k):
        return lax.ppermute(value, "ctx", [(i, i ^ k) for i in range(self.ctx)])

    def high_fsdp(self, value, k):
        return lax.ppermute(value, "fsdp", [(i, i ^ (2 * k)) for i in range(self.fsdp)])


def flip_list(blocks, index):
    bit = 1
    while bit < len(blocks):
        on = (index & bit) != 0
        blocks = [jnp.where(on, blocks[i ^ bit], blocks[i]) for i in range(len(blocks))]
        bit *= 2
    return blocks


def place(blocks, index, axis):
    width = blocks[0].shape[axis]
    shape = list(blocks[0].shape)
    shape[axis] = width * len(blocks)
    full = jnp.zeros(shape, blocks[0].dtype)
    for i, block in enumerate(blocks):
        full = lax.dynamic_update_slice_in_dim(full, block, (index ^ i) * width, axis)
    return full


def to_block_order(plan, rows):
    width = rows.shape[1] // (2 * plan.peers)
    parts = []
    for h in range(plan.high):
        for x in range(plan.ctx):
            for c in range(2):
                start = ((h * 2 + c) * plan.ctx + x) * width
                parts.append(rows[:, start : start + width])
    return jnp.concatenate(parts, axis=1)


def from_block_order(plan, rows):
    width = rows.shape[1] // (2 * plan.peers)
    parts = []
    for h in range(plan.high):
        for c in range(2):
            for x in range(plan.ctx):
                start = ((h * plan.ctx + x) * 2 + c) * width
                parts.append(rows[:, start : start + width])
    return jnp.concatenate(parts, axis=1)


def gather_rows(plan, rows):
    pair = jnp.concatenate([rows, plan.near(rows)], axis=0)
    return jnp.concatenate([pair, plan.core(pair)], axis=0)


def sum_rows(plan, partial):
    half = partial.shape[0] // 2
    pair = partial[:half] + plan.core(partial[half:].astype(BF)).astype(F32)
    half = half // 2
    return pair[:half] + plan.near(pair[half:].astype(BF)).astype(F32)


def natural_rows(plan, rows):
    count = rows.shape[0] // 4
    parts = [
        lax.dynamic_slice_in_dim(rows, (plan.part ^ i) * count, count, 0) for i in range(4)
    ]
    return jnp.concatenate(parts, axis=0)


def own_columns(plan, halves):
    keep = lax.dynamic_index_in_dim(halves, plan.c, 0, False)
    got = plan.core(lax.dynamic_index_in_dim(halves, 1 - plan.c, 0, False))
    return jnp.where(
        plan.c == 0,
        jnp.concatenate([keep, got], axis=1),
        jnp.concatenate([got, keep], axis=1),
    )


def all_columns(plan, rows, direct):
    if direct and plan.peers == 4:
        return place([rows] + [plan.side(rows, k) for k in range(1, 4)], plan.x, 1)
    full = lax.all_gather(rows, "ctx", axis=1, tiled=True)
    if plan.high > 1:
        parts = [full] + [plan.high_fsdp(full, k) for k in range(1, plan.high)]
        full = place(parts, plan.fh, 1)
    return full


def columns_sum(plan, grad, direct):
    if plan.high > 1:
        width = grad.shape[1] // plan.high
        parts = [
            lax.dynamic_slice_in_dim(grad, (plan.fh ^ k) * width, width, 1)
            for k in range(plan.high)
        ]
        grad = parts[0]
        for k in range(1, plan.high):
            grad = grad + plan.high_fsdp(parts[k], k)
    if direct and plan.ctx == 4:
        width = grad.shape[1] // 4
        parts = [
            lax.dynamic_slice_in_dim(grad, (plan.x ^ k) * width, width, 1) for k in range(4)
        ]
        total = parts[0].astype(F32)
        for k in range(1, 4):
            total = total + plan.side(parts[k], k).astype(F32)
        return total
    return lax.psum_scatter(grad, "ctx", scatter_dimension=1, tiled=True)


def together(value, *others):
    many = isinstance(value, list)
    got = lax.optimization_barrier((*value, *others) if many else (value, *others))
    count = len(value) if many else 1
    first = list(got[:count]) if many else got[0]
    return (first, *got[count:])


def with_far(own, far, counts):
    parts = []
    start = 0
    for rows in counts:
        parts += [own[start : start + rows], far[start : start + rows]]
        start += rows
    return jnp.concatenate(parts, axis=0)


def far_halves(total, counts):
    mine, far = [], []
    start = 0
    for rows in counts:
        mine.append(total[start : start + rows])
        far.append(total[start + rows : start + 2 * rows])
        start += 2 * rows
    return jnp.concatenate(mine, axis=0).astype(F32), jnp.concatenate(far, axis=0).astype(BF)


def core_halves(plan, own, counts):
    width = own.shape[1]
    left, right = own[:, : width // 2], own[:, width // 2 :]
    kept = jnp.where(plan.c == 0, left, right)
    got = plan.core(jnp.where(plan.c == 0, right, left).astype(BF)).astype(F32)
    low = jnp.where(plan.c == 0, kept, got)
    high = jnp.where(plan.c == 0, got, kept)
    out = []
    start = 0
    for rows in counts:
        out.append((low[start : start + rows], high[start : start + rows]))
        start += rows
    return out


def split_hidden(weight):
    return weight.reshape(2, weight.shape[0] // 2, weight.shape[1])


def turn(values, cos_tab, sine_tab):
    first, second = values[..., :HALF, :], values[..., HALF:, :]
    return jnp.concatenate(
        [first * cos_tab - second * sine_tab, second * cos_tab + first * sine_tab], axis=-2
    )


def to_heads(plan, values):
    got = [lax.dynamic_index_in_dim(values, plan.ci, 0, False)]
    for k in range(1, 4):
        got.append(plan.side(lax.dynamic_index_in_dim(values, plan.ci ^ k, 0, False), k))
    return got


def from_heads(plan, blocks):
    got = [blocks[0]] + [plan.side(blocks[k], k) for k in range(1, 4)]
    return place([block[None] for block in got], plan.ci, 0)


def more_keys(plan, blocks):
    full = list(blocks)
    for m in range(1, plan.ctx // 4):
        full += [plan.side(block, 4 * m) for block in blocks]
    return full


def more_keys_sum(plan, blocks):
    total = list(blocks[:4])
    for m in range(1, plan.ctx // 4):
        total = [total[k] + plan.side(blocks[4 * m + k], 4 * m) for k in range(4)]
    return total


def seen(first_row, part, key_block, query_block, size):
    turned = part * (size // 4)
    key = key_block * size + (lax.broadcasted_iota(jnp.int32, (size, 1), 0) ^ turned)
    query = query_block * size + (lax.broadcasted_iota(jnp.int32, (1, size), 1) ^ turned)
    return (key <= query) & (key >= first_row)


def attend_kernel(count, place_ref, first_ref, *refs):
    blocks, (out_ref, low_ref, lse_ref, kt_ref, v_ref) = refs[:count], refs[count:]
    size = blocks[0].shape[2]
    x, part = place_ref[0], place_ref[1]
    for k in range(count):
        kt_ref[x ^ k] = blocks[k][1].T
        v_ref[x ^ k] = blocks[k][2]
    for k in range(4):
        block = x ^ k
        query = blocks[k][0] * BF(HEAD ** (-0.5))
        first_row = first_ref[k]

        def step(kb, carry):
            peak, total, acc = carry
            s = mm(kt_ref[kb], query)
            s = jnp.where(seen(first_row, part, kb, block, size), s, NEG)
            top = jnp.maximum(peak, jnp.max(s, axis=0, keepdims=True))
            p = jnp.exp(s - top)
            fade = jnp.exp(peak - top)
            total = fade * total + jnp.sum(p, axis=0, keepdims=True)
            return top, total, fade * acc + mm(v_ref[kb], p.astype(BF))

        start = (
            jnp.full((1, size), NEG, F32),
            jnp.zeros((1, size), F32),
            jnp.zeros((HEAD, size), F32),
        )
        peak, total, acc = lax.fori_loop(place_ref[2 + block], block + 1, step, start)
        acc = acc / total
        out_ref[k] = acc
        low_ref[k] = acc.astype(BF)
        lse_ref[k] = peak + jnp.log(total)


def attend(where_all, first_query, blocks):
    count = len(blocks)
    size = blocks[0].shape[2]
    return pl.pallas_call(
        functools.partial(attend_kernel, count),
        out_shape=(
            jax.ShapeDtypeStruct((4, HEAD, size), F32),
            jax.ShapeDtypeStruct((4, HEAD, size), BF),
            jax.ShapeDtypeStruct((4, 1, size), F32),
        ),
        in_specs=[IN_SMEM] + [IN_VMEM] * (1 + count),
        out_specs=(IN_VMEM,) * 3,
        scratch_shapes=[
            pltpu.VMEM((count, size, HEAD), BF),
            pltpu.VMEM((count, HEAD, size), BF),
        ],
        name="attend",
    )(where_all, first_query, *blocks)


def back_kernel(count, place_ref, first_ref, out_ref, lse_ref, *refs):
    blocks, grads = refs[:count], refs[count : count + 4]
    dq_ref, dk_ref, dv_ref, kt_ref, vt_ref, k_ref, dks_ref, dvs_ref = refs[count + 4 :]
    size = blocks[0].shape[2]
    x, part = place_ref[0], place_ref[1]
    for k in range(count):
        kt_ref[x ^ k] = blocks[k][1].T
        vt_ref[x ^ k] = blocks[k][2].T
        k_ref[x ^ k] = blocks[k][1]
    dks_ref[...] = jnp.zeros_like(dks_ref)
    dvs_ref[...] = jnp.zeros_like(dvs_ref)
    for k in range(4):
        block = x ^ k
        query = blocks[k][0] * BF(HEAD ** (-0.5))
        query_t = query.T
        grad = grads[k][...]
        grad_t = grad.T
        delta = jnp.sum(grad.astype(F32) * out_ref[k], axis=0, keepdims=True)
        lse = lse_ref[k]
        first_row = first_ref[k]

        def step(kb, dq):
            s = mm(kt_ref[kb], query)
            p = jnp.where(seen(first_row, part, kb, block, size), jnp.exp(s - lse), 0.0)
            dp = mm(vt_ref[kb], grad)
            ds = (p * (dp - delta)).astype(BF)
            dvs_ref[kb] += mm(p.astype(BF), grad_t)
            dks_ref[kb] += mm(ds, query_t)
            return dq + mm(k_ref[kb], ds)

        dq = lax.fori_loop(
            place_ref[2 + block], block + 1, step, jnp.zeros((HEAD, size), F32)
        )
        dq_ref[k] = dq * HEAD ** (-0.5)
    for k in range(count):
        dk_ref[k] = dks_ref[x ^ k].T
        dv_ref[k] = dvs_ref[x ^ k].T


def attend_back(where_all, first_query, blocks, grads, out, log_total):
    count = len(blocks)
    size = blocks[0].shape[2]
    return pl.pallas_call(
        functools.partial(back_kernel, count),
        out_shape=(
            jax.ShapeDtypeStruct((4, HEAD, size), F32),
            jax.ShapeDtypeStruct((count, HEAD, size), F32),
            jax.ShapeDtypeStruct((count, HEAD, size), F32),
        ),
        in_specs=[IN_SMEM] + [IN_VMEM] * (3 + count + 4),
        out_specs=(IN_VMEM,) * 3,
        scratch_shapes=[
            pltpu.VMEM((count, size, HEAD), BF),
            pltpu.VMEM((count, size, HEAD), BF),
            pltpu.VMEM((count, HEAD, size), BF),
            pltpu.VMEM((count, size, HEAD), F32),
            pltpu.VMEM((count, size, HEAD), F32),
        ],
        name="attend_back",
    )(where_all, first_query, out, log_total, *blocks, *grads)


def norm_scale(stream):
    return lax.rsqrt(jnp.mean(stream * stream, axis=-1, keepdims=True) + EPS)


def norm_back(stream, scale, gain, grad_normed):
    weighted = grad_normed * gain
    grad_gain = jnp.sum(grad_normed * stream * scale, axis=0, keepdims=True)
    grad_stream = scale * weighted - stream * scale**3 * jnp.mean(
        weighted * stream, axis=1, keepdims=True
    )
    return (grad_gain, grad_stream)


def local(
    tokens,
    out_grad,
    segment_ids,
    owner_order,
    attn_gain,
    w_query,
    w_key,
    w_value,
    w_out,
    mlp_gain,
    w_gate,
    w_up,
    w_down,
):
    plan = Plan()
    tok_rows = tokens.shape[0]
    part_rows = tok_rows // 4
    model = tokens.shape[1]

    gains = jnp.concatenate([attn_gain, mlp_gain], axis=0)
    gains = jnp.concatenate([gains, jnp.zeros((12, gains.shape[1]), BF)], axis=0)
    qkv_rows = 3 * w_query.shape[2] // 2
    out_rows = w_out.shape[1] // 2
    mlp_rows = w_down.shape[1] // 2
    counts = [qkv_rows, out_rows] + [mlp_rows] * 3

    def own_weights(level):
        qkv = [split_hidden(w[level].T) for w in (w_query, w_key, w_value)]
        return [
            jnp.concatenate(qkv, axis=1),
            split_hidden(w_out[level]),
            split_hidden(w_gate[level].T),
            split_hidden(w_up[level].T),
            split_hidden(w_down[level]),
        ]

    groups = own_weights(0)
    own_later = []
    for level in range(1, LAYERS):
        own = own_columns(plan, jnp.concatenate(own_weights(level), axis=1))
        own_later.append(own)
    cuts = [0, qkv_rows + out_rows]
    for _ in range(3):
        cuts.append(cuts[-1] + mlp_rows)
    def own_rows(array):
        mine = lax.dynamic_slice_in_dim(array, plan.part * part_rows, part_rows, 0)
        got = plan.core(
            lax.dynamic_slice_in_dim(array, (plan.part ^ 2) * part_rows, part_rows, 0)
        )
        return to_block_order(plan, jnp.where(plan.c == plan.zp, mine, got))

    token_rows = own_rows(tokens)
    tokens_all = gather_rows(plan, token_rows).astype(F32)
    stream = token_rows.astype(F32)
    grad_rows = own_rows(out_grad)
    grad_stream = grad_rows.astype(F32)

    own = own_columns(plan, groups[0])
    far_first = plan.far(own)
    own_rest = own_columns(plan, jnp.concatenate(groups[1:], axis=1))
    got = plan.core(gains)
    gain_pair = jnp.where(
        plan.c == 0,
        jnp.concatenate([gains, got], axis=1),
        jnp.concatenate([got, gains], axis=1),
    )
    own_rest, far_first, grad_rows = together(own_rest, far_first, grad_rows)
    out_branch = gather_rows(plan, grad_rows)
    first = jnp.concatenate([own, far_first, gain_pair], axis=0)
    first, out_branch = together(all_columns(plan, first, True), out_branch)
    w_qkv, gain_full = first[: 2 * qkv_rows], first[2 * qkv_rows :].astype(F32)
    last_far = plan.far(own_rest)

    segment = jnp.where(plan.c == plan.zp, segment_ids, plan.core(segment_ids))[0]
    pack = segment.shape[0]
    index_all = jnp.arange(pack, dtype=jnp.int32)
    run_start = jnp.concatenate([jnp.ones((1,), dtype=bool), segment[1:] != segment[:-1]])
    run_first = lax.cummax(jnp.where(run_start, index_all, jnp.zeros_like(index_all)), axis=0)
    where_all = jnp.concatenate(
        [jnp.stack([plan.x, plan.part]).astype(jnp.int32), run_first[::tok_rows] // tok_rows]
    )

    def by_peer(row):
        grid = row.reshape(plan.ctx, 4, part_rows)
        blocks = [lax.dynamic_index_in_dim(grid, plan.x ^ k, 0, False) for k in range(4)]
        grid = jnp.stack(blocks)
        return jnp.concatenate(flip_list([grid[:, i] for i in range(4)], plan.part), axis=1)

    positions = by_peer((index_all - run_first).astype(F32))
    first_query = by_peer(run_first)[:, None, :]
    frequency = THETA ** (-(jnp.arange(HALF, dtype=F32) * 2.0 / HEAD))
    angles = frequency[None, :, None] * positions[:, None, :]
    cos_all, sine_all = jnp.cos(angles), jnp.sin(angles)
    cos_own, sine_own = cos_all[0], sine_all[0]

    full = [(w_qkv, None, None)]
    kept = []
    first_values = None
    for level in range(LAYERS):
        w_qkv, w_o, w_mlp = full[level]
        width = 2 * mlp_rows
        if level == 0:
            scale_all = norm_scale(tokens_all)
            scale_attn = scale_all[:part_rows]
            normed_all = (tokens_all * scale_all * gain_full[:1]).astype(BF)
        else:
            scale_attn = norm_scale(stream)
            normed = (stream * scale_attn * gain_full[level : level + 1]).astype(BF)
            normed_all = gather_rows(plan, normed)
        qkv = dot(w_qkv, normed_all, 1, 1)
        qkv = qkv.reshape(2, 3, 2, HEAD, tok_rows)
        query = turn(qkv[:, 0], cos_own, sine_own).astype(BF)
        key = turn(qkv[:, 1], cos_own, sine_own).astype(BF)
        if level == 0:
            first_values = qkv[:, 2]
            mixed = first_values
        else:
            mixed = 0.5 * qkv[:, 2] + 0.5 * first_values
        heads = jnp.stack([query, key, mixed.astype(BF)], axis=2)
        heads = more_keys(plan, to_heads(plan, heads.reshape(4, 3, HEAD, tok_rows)))
        ahead = level + 1 < LAYERS
        far_next = []

        def next_far():
            i = len(far_next)
            piece = own_later[level][cuts[i] : cuts[i + 1]]
            if far_next:
                piece, far_next[-1] = together(piece, far_next[-1])
            return plan.far(piece)

        if level == 0:
            heads, last_far = together(heads, last_far)
            rest = with_far(own_rest, last_far, counts[1:])
            w_o = all_columns(plan, rest[: 2 * out_rows], True)
            rest = all_columns(plan, rest[2 * out_rows :], False)
            w_mlp = (rest[: 2 * width], rest[2 * width :])
        out, out_low, log_total = attend(where_all, first_query, heads)
        if ahead:
            out_low, got = together(out_low, next_far())
            far_next.append(got)
        attended = from_heads(plan, [out_low[k] for k in range(4)])
        attended = attended.reshape(4 * HEAD, tok_rows)
        if ahead:
            attended, got = together(attended, next_far())
            far_next.append(got)
        branch = sum_rows(plan, dot(attended, w_o, 0, 0))
        if ahead:
            branch, got = together(branch, next_far())
            far_next.append(got)
        middle = stream + branch
        scale_mlp = norm_scale(middle)
        normed_mlp = (middle * scale_mlp * gain_full[2 + level : 3 + level]).astype(BF)
        normed_mlp_all = gather_rows(plan, normed_mlp)
        w_gu, w_d = w_mlp
        full[level] = (w_qkv, w_o, w_gu, w_d)
        gate_up = dot(normed_mlp_all, w_gu, 1, 1)
        gate, upward = gate_up[:, :width], gate_up[:, width:]
        hidden = (gate * jax.nn.sigmoid(gate) * upward).astype(BF)
        if ahead:
            hidden, got = together(hidden, next_far())
            far_next.append(got)
            own = own_later[level]
            w_attn = with_far(own[: cuts[1]], far_next[0], counts[:2])
            w_attn = all_columns(plan, w_attn, False)
            rest = with_far(own[cuts[1] :], jnp.concatenate(far_next[1:], axis=0), counts[2:])
            rest = all_columns(plan, rest, False)
            later = (rest[: 2 * width], rest[2 * width :])
            full.append((w_attn[: 2 * qkv_rows], w_attn[2 * qkv_rows :], later))
        if level < LAYERS - 1:
            result = middle + sum_rows(plan, dot(hidden, w_d, 1, 0))
        kept.append(
            (
                stream,
                scale_attn,
                normed_all,
                heads,
                out,
                log_total,
                attended,
                middle,
                scale_mlp,
                normed_mlp_all,
                gate_up,
                hidden,
            )
        )
        if level < LAYERS - 1:
            stream = result

    def to_pack(rows, other):
        mine = jnp.where(plan.c == plan.zp, rows, other)
        got = plan.core(jnp.where(plan.c == plan.zp, other, rows))
        count = rows.shape[0]
        near = plan.near(jnp.concatenate([mine, got], axis=0))
        return jnp.concatenate([mine, near[:count], got, near[count:]], axis=0)


    def weight_grads(grad_qkv, grad_wo, grad_wg, grad_wu, grad_wd):
        third = qkv_rows // 3

        def member(i):
            rows = [half[i * third : (i + 1) * third] for half in grad_qkv]
            return jnp.concatenate(rows, axis=0).T

        return (
            member(0),
            member(1),
            member(2),
            jnp.concatenate(grad_wo, axis=0),
            jnp.concatenate(grad_wg, axis=0).T,
            jnp.concatenate(grad_wu, axis=0).T,
            jnp.concatenate(grad_wd, axis=0),
        )

    grads = [None] * LAYERS
    gain_rows = [None] * (2 * LAYERS)
    carried = None
    for level in reversed(range(LAYERS)):
        (
            stream,
            scale_attn,
            normed_all,
            heads,
            out,
            log_total,
            attended,
            middle,
            scale_mlp,
            normed_mlp_all,
            gate_up,
            hidden,
        ) = kept[level]
        w_qkv, w_o, w_gu, w_d = full[level]
        width = 2 * mlp_rows
        if level == LAYERS - 1:
            branch = out_branch
        else:
            branch = gather_rows(plan, grad_stream.astype(BF))
        grad_hidden = dot(branch, w_d, 1, 1)
        gate, upward = gate_up[:, :width], gate_up[:, width:]
        sigma = jax.nn.sigmoid(gate)
        grad_gate = (grad_hidden * upward * sigma * (1.0 + gate * (1.0 - sigma))).astype(BF)
        grad_up = (grad_hidden * gate * sigma).astype(BF)
        grad_gu = jnp.concatenate([grad_gate, grad_up], axis=1)
        partial, grad_gu = together(dot(grad_gu, w_gu, 1, 0), grad_gu)
        grad_normed = sum_rows(plan, partial)
        grad_wd = dot(hidden, branch, 0, 0).astype(BF)
        grad_wgu = dot(grad_gu, normed_mlp_all, 0, 0).astype(BF)
        grad_mlp = jnp.concatenate([grad_wgu, grad_wd], axis=0)
        if level == 0:
            grad_normed, grad_mlp, sum_attn = together(grad_normed, grad_mlp, sum_attn)
        else:
            grad_normed, grad_mlp = together(grad_normed, grad_mlp)
        sum_mlp = columns_sum(plan, grad_mlp, False)
        gain_rows[2 + level], through = norm_back(
            middle, scale_mlp, gain_full[2 + level : 3 + level], grad_normed
        )
        grad_middle = grad_stream + through
        branch = gather_rows(plan, grad_middle.astype(BF))
        if level == 0:
            later_mlp, branch = together(later_mlp, branch)
            mine_mlp, far = far_halves(later_mlp, counts[2:])
            mine_attn, far_attn = far_halves(sum_attn, counts[:2])
            far_a = plan.far(far[:mlp_rows])
        if level == LAYERS - 1:
            partial, branch = together(dot(hidden, w_d, 1, 0), branch)
            last = sum_rows(plan, partial)
        grad_wo = dot(attended, branch, 1, 0).astype(BF)
        grad_attended = dot(w_o, branch, 1, 1).astype(BF)
        grad_attended = to_heads(plan, grad_attended.reshape(4, HEAD, tok_rows))
        if level == 0:
            far_b, far_a = together(far[mlp_rows : 2 * mlp_rows], far_a)
            far_b = plan.far(far_b)
            grad_attended, far_a = together(grad_attended, far_a)
        elif level == LAYERS - 1:
            grad_attended, last = together(grad_attended, last)
            last = from_block_order(plan, (middle + last).astype(BF))
            other = plan.far(last)
        grad_q, grad_k, grad_v = attend_back(
            where_all, first_query, heads, grad_attended, out, log_total
        )
        if level == 0:
            far_c = jnp.concatenate([far_attn, far[2 * mlp_rows :]], axis=0)
            far_c, far_b = together(far_c, far_b)
            far_c = plan.far(far_c)
            grad_q, far_b = together(grad_q, far_b)
        elif level == LAYERS - 1:
            grad_q, other = together(grad_q, other)
            last = to_pack(last, other)
        grad_k = more_keys_sum(plan, grad_k)
        grad_v = more_keys_sum(plan, grad_v)
        if level > 0:
            grad_v = [0.5 * block for block in grad_v]
            if carried is None:
                carried = grad_v
            else:
                carried = [left + right for left, right in zip(carried, grad_v)]
        else:
            grad_v = [left + right for left, right in zip(grad_v, carried)]
        grad_heads = [
            jnp.stack(
                [
                    turn(grad_q[k], cos_all[k], -sine_all[k]).astype(BF),
                    turn(grad_k[k], cos_all[k], -sine_all[k]).astype(BF),
                    grad_v[k].astype(BF),
                ]
            )
            for k in range(4)
        ]
        grad_qkv = from_heads(plan, grad_heads).reshape(2, 2, 3, HEAD, tok_rows)
        grad_qkv = jnp.swapaxes(grad_qkv, 1, 2).reshape(-1, tok_rows)
        if level == 0:
            mine_first, far = far_halves(sum_mlp, counts[2:])
            far_d, far_c = together(far[:mlp_rows], far_c)
            far_d = plan.far(far_d)
            grad_qkv, far_c = together(grad_qkv, far_c)
        elif level == LAYERS - 1:
            grad_qkv, last = together(grad_qkv, last)
            outputs = natural_rows(plan, last)
        grad_wqkv = dot(grad_qkv, normed_all, 1, 0).astype(BF)
        grad_normed = sum_rows(plan, dot(grad_qkv, w_qkv, 0, 0))
        if level == 0:
            far_e = far[mlp_rows:]
            grad_normed, far_d, far_e = together(grad_normed, far_d, far_e)
            cut = qkv_rows + out_rows
            got = jnp.concatenate([far_c[:cut], far_a, far_b, far_c[cut:]], axis=0).astype(F32)
            mine = jnp.concatenate([mine_attn, mine_mlp], axis=0)
            grads[1] = weight_grads(*core_halves(plan, mine + got, counts))
        else:
            grad_normed, later_mlp = together(grad_normed, sum_mlp)
        grad_attn = jnp.concatenate([grad_wqkv, grad_wo], axis=0)
        sum_attn = columns_sum(plan, grad_attn, False)
        gain_rows[level], through = norm_back(
            stream, scale_attn, gain_full[level : level + 1], grad_normed
        )
        grad_stream = grad_middle + through

    rows = from_block_order(plan, grad_stream.astype(BF))
    gain_sum = jnp.concatenate(gain_rows + [jnp.zeros((12, model), F32)], axis=0)
    gain_near = plan.near(gain_sum)
    other, gain_near, far_e = together(plan.far(rows), gain_near, far_e)
    far_e = plan.far(far_e)
    group_rows = tok_rows // plan.ctx
    owner_grid = owner_order[0].reshape(plan.ctx, plan.ctx, group_rows)
    local_rows = (
        lax.dynamic_index_in_dim(owner_grid, plan.x, 1, False) - plan.x * tok_rows
    ).reshape(tok_rows)
    local_rows = local_rows ^ (plan.part * part_rows)
    slots, far_e = together(to_pack(rows, other)[local_rows], far_e)
    grad_tokens = lax.all_to_all(slots, "ctx", split_axis=0, concat_axis=0, tiled=True)

    got = jnp.concatenate([far_d, far_e], axis=0).astype(F32)
    rest = core_halves(plan, mine_first + got, counts[2:])
    gain_sum = columns_sum(plan, gain_sum + gain_near, True)
    mine, far = far_halves(sum_attn, counts[:2])
    far = jnp.concatenate([far, gain_sum.astype(BF)], axis=0)
    far = plan.far(far)
    grad_tokens, far = together(grad_tokens, far)
    grad_tokens = grad_tokens.astype(F32)
    total = jnp.concatenate([mine, gain_sum], axis=0) + far.astype(F32)
    first = core_halves(plan, total, [qkv_rows, out_rows, gain_sum.shape[0]])
    total = first[2][0] + first[2][1]
    grads[0] = weight_grads(first[0], first[1], *rest)

    stacked = [jnp.stack([grads[level][i] for level in range(LAYERS)]) for i in range(7)]
    return (
        outputs,
        grad_tokens,
        total[:2],
        stacked[0],
        stacked[1],
        stacked[2],
        stacked[3],
        total[2:4],
        stacked[4],
        stacked[5],
        stacked[6],
    )


def solution(mesh):
    columns = P(None, ("fsdp", "ctx"), "tp")
    rows = P(None, "tp", ("fsdp", "ctx"))
    gain = P(None, ("fsdp", "ctx"))
    tokens = P(("fsdp", "ctx"), None)
    return jax.shard_map(
        local,
        mesh=mesh,
        in_specs=(
            tokens,
            tokens,
            P("fsdp", None),
            P("fsdp", None),
            gain,
            columns,
            columns,
            columns,
            rows,
            gain,
            columns,
            columns,
            rows,
        ),
        out_specs=(
            tokens,
            tokens,
            gain,
            columns,
            columns,
            columns,
            rows,
            gain,
            columns,
            columns,
            rows,
        ),
        check_vma=False,
    )
```

```python
import functools

import jax
import jax.numpy as jnp
from jax import lax
from jax.experimental import pallas as pl
from jax.experimental.pallas import tpu as pltpu
from jax.sharding import PartitionSpec as P

HEAD = 64
HALF = HEAD // 2
LAYERS = 2
EPS = 1e-05
THETA = 10000.0
NEG = -1e30
BF = jnp.bfloat16
F32 = jnp.float32
IN_VMEM = pl.BlockSpec(memory_space=pltpu.VMEM)
IN_SMEM = pl.BlockSpec(memory_space=pltpu.SMEM)


def dot(left, right, left_dim, right_dim):
    return lax.dot_general(
        left, right, (((left_dim,), (right_dim,)), ((), ())), preferred_element_type=F32
    )


def mm(left, right):
    return jnp.dot(left, right, preferred_element_type=F32)


class Plan:
    def __init__(self):
        self.fsdp = lax.axis_size("fsdp")
        self.ctx = lax.axis_size("ctx")
        self.tp = lax.axis_size("tp")
        self.high = self.fsdp // 2
        f = lax.axis_index("fsdp")
        z = lax.axis_index("tp")
        self.c = f % 2
        self.fh = f // 2
        self.x = lax.axis_index("ctx")
        self.zl = z % 2
        self.zp = z // 2
        self.ci = self.x % 4
        self.part = self.c * 2 + self.zl
        self.peers = self.high * self.ctx

    def core(self, value):
        return lax.ppermute(value, "fsdp", [(i, i ^ 1) for i in range(self.fsdp)])

    def near(self, value):
        return lax.ppermute(value, "tp", [(i, i ^ 1) for i in range(self.tp)])

    def far(self, value):
        return lax.ppermute(value, "tp", [(i, i ^ 2) for i in range(self.tp)])

    def side(self, value, k):
        return lax.ppermute(value, "ctx", [(i, i ^ k) for i in range(self.ctx)])

    def high_fsdp(self, value, k):
        return lax.ppermute(value, "fsdp", [(i, i ^ (2 * k)) for i in range(self.fsdp)])


def flip_list(blocks, index):
    bit = 1
    while bit < len(blocks):
        on = (index & bit) != 0
        blocks = [jnp.where(on, blocks[i ^ bit], blocks[i]) for i in range(len(blocks))]
        bit *= 2
    return blocks


def place(blocks, index, axis):
    width = blocks[0].shape[axis]
    shape = list(blocks[0].shape)
    shape[axis] = width * len(blocks)
    full = jnp.zeros(shape, blocks[0].dtype)
    for i, block in enumerate(blocks):
        full = lax.dynamic_update_slice_in_dim(full, block, (index ^ i) * width, axis)
    return full


def to_block_order(plan, rows):
    width = rows.shape[1] // (2 * plan.peers)
    parts = []
    for h in range(plan.high):
        for x in range(plan.ctx):
            for c in range(2):
                start = ((h * 2 + c) * plan.ctx + x) * width
                parts.append(rows[:, start : start + width])
    return jnp.concatenate(parts, axis=1)


def from_block_order(plan, rows):
    width = rows.shape[1] // (2 * plan.peers)
    parts = []
    for h in range(plan.high):
        for c in range(2):
            for x in range(plan.ctx):
                start = ((h * plan.ctx + x) * 2 + c) * width
                parts.append(rows[:, start : start + width])
    return jnp.concatenate(parts, axis=1)


def gather_rows(plan, rows):
    pair = jnp.concatenate([rows, plan.near(rows)], axis=0)
    return jnp.concatenate([pair, plan.core(pair)], axis=0)


def sum_rows(plan, partial):
    half = partial.shape[0] // 2
    pair = partial[:half] + plan.core(partial[half:].astype(BF)).astype(F32)
    half = half // 2
    return pair[:half] + plan.near(pair[half:].astype(BF)).astype(F32)


def natural_rows(plan, rows):
    count = rows.shape[0] // 4
    parts = [
        lax.dynamic_slice_in_dim(rows, (plan.part ^ i) * count, count, 0) for i in range(4)
    ]
    return jnp.concatenate(parts, axis=0)


def own_columns(plan, halves):
    keep = lax.dynamic_index_in_dim(halves, plan.c, 0, False)
    got = plan.core(lax.dynamic_index_in_dim(halves, 1 - plan.c, 0, False))
    return jnp.where(
        plan.c == 0,
        jnp.concatenate([keep, got], axis=1),
        jnp.concatenate([got, keep], axis=1),
    )


def all_columns(plan, rows, direct):
    if direct and plan.peers == 4:
        return place([rows] + [plan.side(rows, k) for k in range(1, 4)], plan.x, 1)
    full = lax.all_gather(rows, "ctx", axis=1, tiled=True)
    if plan.high > 1:
        parts = [full] + [plan.high_fsdp(full, k) for k in range(1, plan.high)]
        full = place(parts, plan.fh, 1)
    return full


def columns_sum(plan, grad, direct):
    if plan.high > 1:
        width = grad.shape[1] // plan.high
        parts = [
            lax.dynamic_slice_in_dim(grad, (plan.fh ^ k) * width, width, 1)
            for k in range(plan.high)
        ]
        grad = parts[0]
        for k in range(1, plan.high):
            grad = grad + plan.high_fsdp(parts[k], k)
    if direct and plan.ctx == 4:
        width = grad.shape[1] // 4
        parts = [
            lax.dynamic_slice_in_dim(grad, (plan.x ^ k) * width, width, 1) for k in range(4)
        ]
        total = parts[0].astype(F32)
        for k in range(1, 4):
            total = total + plan.side(parts[k], k).astype(F32)
        return total
    return lax.psum_scatter(grad, "ctx", scatter_dimension=1, tiled=True)


def together(value, *others):
    many = isinstance(value, list)
    got = lax.optimization_barrier((*value, *others) if many else (value, *others))
    count = len(value) if many else 1
    first = list(got[:count]) if many else got[0]
    return (first, *got[count:])


def with_far(own, far, counts):
    parts = []
    start = 0
    for rows in counts:
        parts += [own[start : start + rows], far[start : start + rows]]
        start += rows
    return jnp.concatenate(parts, axis=0)


def far_halves(total, counts):
    mine, far = [], []
    start = 0
    for rows in counts:
        mine.append(total[start : start + rows])
        far.append(total[start + rows : start + 2 * rows])
        start += 2 * rows
    return jnp.concatenate(mine, axis=0).astype(F32), jnp.concatenate(far, axis=0).astype(BF)


def core_halves(plan, own, counts):
    width = own.shape[1]
    left, right = own[:, : width // 2], own[:, width // 2 :]
    kept = jnp.where(plan.c == 0, left, right)
    got = plan.core(jnp.where(plan.c == 0, right, left).astype(BF)).astype(F32)
    low = jnp.where(plan.c == 0, kept, got)
    high = jnp.where(plan.c == 0, got, kept)
    out = []
    start = 0
    for rows in counts:
        out.append((low[start : start + rows], high[start : start + rows]))
        start += rows
    return out


def split_hidden(weight):
    return weight.reshape(2, weight.shape[0] // 2, weight.shape[1])


def turn(values, cos_tab, sine_tab):
    first, second = values[..., :HALF, :], values[..., HALF:, :]
    return jnp.concatenate(
        [first * cos_tab - second * sine_tab, second * cos_tab + first * sine_tab], axis=-2
    )


def to_heads(plan, values):
    got = [lax.dynamic_index_in_dim(values, plan.ci, 0, False)]
    for k in range(1, 4):
        got.append(plan.side(lax.dynamic_index_in_dim(values, plan.ci ^ k, 0, False), k))
    return got


def from_heads(plan, blocks):
    got = [blocks[0]] + [plan.side(blocks[k], k) for k in range(1, 4)]
    return place([block[None] for block in got], plan.ci, 0)


def more_keys(plan, blocks):
    full = list(blocks)
    for m in range(1, plan.ctx // 4):
        full += [plan.side(block, 4 * m) for block in blocks]
    return full


def more_keys_sum(plan, blocks):
    total = list(blocks[:4])
    for m in range(1, plan.ctx // 4):
        total = [total[k] + plan.side(blocks[4 * m + k], 4 * m) for k in range(4)]
    return total


def seen(first_row, part, key_block, query_block, size):
    turned = part * (size // 4)
    key = key_block * size + (lax.broadcasted_iota(jnp.int32, (size, 1), 0) ^ turned)
    query = query_block * size + (lax.broadcasted_iota(jnp.int32, (1, size), 1) ^ turned)
    return (key <= query) & (key >= first_row)


def attend_kernel(count, place_ref, first_ref, *refs):
    blocks, (out_ref, low_ref, lse_ref, kt_ref, v_ref, q_ref) = refs[:count], refs[count:]
    size = blocks[0].shape[2]
    x, part = place_ref[0], place_ref[1]
    for k in range(count):
        kt_ref[x ^ k] = blocks[k][1].T
        v_ref[x ^ k] = blocks[k][2]
    for k in range(4):
        q_ref[k] = blocks[k][0] * BF(HEAD ** (-0.5))

    @pl.loop(0, 4)
    def _(k):
        block = x ^ k
        query = q_ref[k]
        first_row = first_ref[k]

        def step(kb, carry):
            peak, total, acc = carry
            s = mm(kt_ref[kb], query)
            s = jnp.where(seen(first_row, part, kb, block, size), s, NEG)
            top = jnp.maximum(peak, jnp.max(s, axis=0, keepdims=True))
            p = jnp.exp(s - top)
            fade = jnp.exp(peak - top)
            total = fade * total + jnp.sum(p, axis=0, keepdims=True)
            return top, total, fade * acc + mm(v_ref[kb], p.astype(BF))

        start = (
            jnp.full((1, size), NEG, F32),
            jnp.zeros((1, size), F32),
            jnp.zeros((HEAD, size), F32),
        )
        peak, total, acc = lax.fori_loop(place_ref[2 + block], block + 1, step, start)
        acc = acc / total
        out_ref[k] = acc
        low_ref[k] = acc.astype(BF)
        lse_ref[k] = peak + jnp.log(total)


def attend(where_all, first_query, blocks):
    count = len(blocks)
    size = blocks[0].shape[2]
    return pl.pallas_call(
        functools.partial(attend_kernel, count),
        out_shape=(
            jax.ShapeDtypeStruct((4, HEAD, size), F32),
            jax.ShapeDtypeStruct((4, HEAD, size), BF),
            jax.ShapeDtypeStruct((4, 1, size), F32),
        ),
        in_specs=[IN_SMEM] + [IN_VMEM] * (1 + count),
        out_specs=(IN_VMEM,) * 3,
        scratch_shapes=[
            pltpu.VMEM((count, size, HEAD), BF),
            pltpu.VMEM((count, HEAD, size), BF),
            pltpu.VMEM((4, HEAD, size), BF),
        ],
        name="attend",
    )(where_all, first_query, *blocks)


def back_kernel(count, place_ref, first_ref, out_ref, lse_ref, *refs):
    blocks, grads = refs[:count], refs[count : count + 4]
    dq_ref, dk_ref, dv_ref, kt_ref, vt_ref, k_ref, dks_ref, dvs_ref = refs[count + 4 : -2]
    q_ref, grad_ref = refs[-2:]
    size = blocks[0].shape[2]
    x, part = place_ref[0], place_ref[1]
    for k in range(count):
        kt_ref[x ^ k] = blocks[k][1].T
        vt_ref[x ^ k] = blocks[k][2].T
        k_ref[x ^ k] = blocks[k][1]
    dks_ref[...] = jnp.zeros_like(dks_ref)
    dvs_ref[...] = jnp.zeros_like(dvs_ref)
    for k in range(4):
        q_ref[k] = blocks[k][0] * BF(HEAD ** (-0.5))
        grad_ref[k] = grads[k][...]

    @pl.loop(0, 4)
    def _(k):
        block = x ^ k
        query = q_ref[k]
        query_t = query.T
        grad = grad_ref[k]
        grad_t = grad.T
        delta = jnp.sum(grad.astype(F32) * out_ref[k], axis=0, keepdims=True)
        lse = lse_ref[k]
        first_row = first_ref[k]

        def step(kb, dq):
            s = mm(kt_ref[kb], query)
            p = jnp.where(seen(first_row, part, kb, block, size), jnp.exp(s - lse), 0.0)
            dp = mm(vt_ref[kb], grad)
            ds = (p * (dp - delta)).astype(BF)
            dvs_ref[kb] += mm(p.astype(BF), grad_t)
            dks_ref[kb] += mm(ds, query_t)
            return dq + mm(k_ref[kb], ds)

        dq = lax.fori_loop(
            place_ref[2 + block], block + 1, step, jnp.zeros((HEAD, size), F32)
        )
        dq_ref[k] = dq * HEAD ** (-0.5)

    for k in range(count):
        dk_ref[k] = dks_ref[x ^ k].T
        dv_ref[k] = dvs_ref[x ^ k].T


def attend_back(where_all, first_query, blocks, grads, out, log_total):
    count = len(blocks)
    size = blocks[0].shape[2]
    return pl.pallas_call(
        functools.partial(back_kernel, count),
        out_shape=(
            jax.ShapeDtypeStruct((4, HEAD, size), F32),
            jax.ShapeDtypeStruct((count, HEAD, size), F32),
            jax.ShapeDtypeStruct((count, HEAD, size), F32),
        ),
        in_specs=[IN_SMEM] + [IN_VMEM] * (3 + count + 4),
        out_specs=(IN_VMEM,) * 3,
        scratch_shapes=[
            pltpu.VMEM((count, size, HEAD), BF),
            pltpu.VMEM((count, size, HEAD), BF),
            pltpu.VMEM((count, HEAD, size), BF),
            pltpu.VMEM((count, size, HEAD), F32),
            pltpu.VMEM((count, size, HEAD), F32),
            pltpu.VMEM((4, HEAD, size), BF),
            pltpu.VMEM((4, HEAD, size), BF),
        ],
        name="attend_back",
    )(where_all, first_query, out, log_total, *blocks, *grads)


def norm_scale(stream):
    return lax.rsqrt(jnp.mean(stream * stream, axis=-1, keepdims=True) + EPS)


def norm_back(stream, scale, gain, grad_normed):
    weighted = grad_normed * gain
    grad_gain = jnp.sum(grad_normed * stream * scale, axis=0, keepdims=True)
    grad_stream = scale * weighted - stream * scale**3 * jnp.mean(
        weighted * stream, axis=1, keepdims=True
    )
    return (grad_gain, grad_stream)


def local(
    tokens,
    out_grad,
    segment_ids,
    owner_order,
    attn_gain,
    w_query,
    w_key,
    w_value,
    w_out,
    mlp_gain,
    w_gate,
    w_up,
    w_down,
):
    plan = Plan()
    tok_rows = tokens.shape[0]
    part_rows = tok_rows // 4
    model = tokens.shape[1]

    gains = jnp.concatenate([attn_gain, mlp_gain], axis=0)
    gains = jnp.concatenate([gains, jnp.zeros((12, gains.shape[1]), BF)], axis=0)
    qkv_rows = 3 * w_query.shape[2] // 2
    out_rows = w_out.shape[1] // 2
    mlp_rows = w_down.shape[1] // 2
    counts = [qkv_rows, out_rows] + [mlp_rows] * 3

    def own_weights(level):
        qkv = [split_hidden(w[level].T) for w in (w_query, w_key, w_value)]
        return [
            jnp.concatenate(qkv, axis=1),
            split_hidden(w_out[level]),
            split_hidden(w_gate[level].T),
            split_hidden(w_up[level].T),
            split_hidden(w_down[level]),
        ]

    groups = own_weights(0)
    own_later = []
    for level in range(1, LAYERS):
        own = own_columns(plan, jnp.concatenate(own_weights(level), axis=1))
        own_later.append(own)
    cut = qkv_rows + out_rows
    pieces = [(cut, cut + mlp_rows), (0, cut)]
    pieces += [(cut + i * mlp_rows, cut + (i + 1) * mlp_rows) for i in (1, 2)]
    def own_rows(array):
        mine = lax.dynamic_slice_in_dim(array, plan.part * part_rows, part_rows, 0)
        got = plan.core(
            lax.dynamic_slice_in_dim(array, (plan.part ^ 2) * part_rows, part_rows, 0)
        )
        return to_block_order(plan, jnp.where(plan.c == plan.zp, mine, got))

    token_rows = own_rows(tokens)
    tokens_all = gather_rows(plan, token_rows).astype(F32)
    stream = token_rows.astype(F32)
    grad_rows = own_rows(out_grad)
    grad_stream = grad_rows.astype(F32)

    own = own_columns(plan, groups[0])
    far_first = plan.far(own)
    own_rest = own_columns(plan, jnp.concatenate(groups[1:], axis=1))
    got = plan.core(gains)
    gain_pair = jnp.where(
        plan.c == 0,
        jnp.concatenate([gains, got], axis=1),
        jnp.concatenate([got, gains], axis=1),
    )
    own_rest, far_first, grad_rows = together(own_rest, far_first, grad_rows)
    out_branch = gather_rows(plan, grad_rows)
    first = jnp.concatenate([own, far_first, gain_pair], axis=0)
    first = all_columns(plan, first, True)
    w_qkv, gain_full = first[: 2 * qkv_rows], first[2 * qkv_rows :].astype(F32)
    last_far = plan.far(own_rest)

    segment = jnp.where(plan.c == plan.zp, segment_ids, plan.core(segment_ids))[0]
    pack = segment.shape[0]
    index_all = jnp.arange(pack, dtype=jnp.int32)
    run_start = jnp.concatenate([jnp.ones((1,), dtype=bool), segment[1:] != segment[:-1]])
    run_first = lax.cummax(jnp.where(run_start, index_all, jnp.zeros_like(index_all)), axis=0)
    where_all = jnp.concatenate(
        [jnp.stack([plan.x, plan.part]).astype(jnp.int32), run_first[::tok_rows] // tok_rows]
    )

    def by_peer(row):
        grid = row.reshape(plan.ctx, 4, part_rows)
        blocks = [lax.dynamic_index_in_dim(grid, plan.x ^ k, 0, False) for k in range(4)]
        grid = jnp.stack(blocks)
        return jnp.concatenate(flip_list([grid[:, i] for i in range(4)], plan.part), axis=1)

    positions = by_peer((index_all - run_first).astype(F32))
    first_query = by_peer(run_first)[:, None, :]
    frequency = THETA ** (-(jnp.arange(HALF, dtype=F32) * 2.0 / HEAD))
    angles = frequency[None, :, None] * positions[:, None, :]
    cos_all, sine_all = jnp.cos(angles), jnp.sin(angles)
    cos_own, sine_own = cos_all[0], sine_all[0]

    full = [(w_qkv, None, None)]
    kept = []
    first_values = None
    for level in range(LAYERS):
        w_qkv, w_o, w_mlp = full[level]
        width = 2 * mlp_rows
        if level == 0:
            scale_all = norm_scale(tokens_all)
            scale_attn = scale_all[:part_rows]
            normed_all = (tokens_all * scale_all * gain_full[:1]).astype(BF)
        else:
            scale_attn = norm_scale(stream)
            normed = (stream * scale_attn * gain_full[level : level + 1]).astype(BF)
            normed_all = gather_rows(plan, normed)
        qkv = dot(w_qkv, normed_all, 1, 1)
        if level + 1 < LAYERS:
            qkv, own_later[level] = together(qkv, own_later[level])
        qkv = qkv.reshape(2, 3, 2, HEAD, tok_rows)
        query = turn(qkv[:, 0], cos_own, sine_own).astype(BF)
        key = turn(qkv[:, 1], cos_own, sine_own).astype(BF)
        if level == 0:
            first_values = qkv[:, 2]
            mixed = first_values
        else:
            mixed = 0.5 * qkv[:, 2] + 0.5 * first_values
        heads = jnp.stack([query, key, mixed.astype(BF)], axis=2)
        heads = more_keys(plan, to_heads(plan, heads.reshape(4, 3, HEAD, tok_rows)))
        ahead = level + 1 < LAYERS
        far_next = []

        def next_far():
            nonlocal last_far
            start, end = pieces[len(far_next)]
            piece = own_later[level][start:end]
            if far_next:
                piece, far_next[-1] = together(piece, far_next[-1])
            else:
                piece, last_far = together(piece, last_far)
            return plan.far(piece)

        if level == 0:
            got = next_far()
            heads, last_far, out_branch, got = together(heads, last_far, out_branch, got)
            far_next.append(got)
            rest = with_far(own_rest, last_far, counts[1:])
            w_o = all_columns(plan, rest[: 2 * out_rows], True)
            rest = all_columns(plan, rest[2 * out_rows :], False)
            w_mlp = (rest[: 2 * width], rest[2 * width :])
        out, out_low, log_total = attend(where_all, first_query, heads)
        if ahead:
            out_low, got, w_o = together(out_low, next_far(), w_o)
            far_next.append(got)
        attended = from_heads(plan, [out_low[k] for k in range(4)])
        attended = attended.reshape(4 * HEAD, tok_rows)
        if ahead:
            attended, got = together(attended, next_far())
            far_next.append(got)
        branch = sum_rows(plan, dot(attended, w_o, 0, 0))
        if ahead:
            branch, got = together(branch, next_far())
            far_next.append(got)
        middle = stream + branch
        scale_mlp = norm_scale(middle)
        normed_mlp = (middle * scale_mlp * gain_full[2 + level : 3 + level]).astype(BF)
        normed_mlp_all = gather_rows(plan, normed_mlp)
        w_gu, w_d = w_mlp
        full[level] = (w_qkv, w_o, w_gu, w_d)
        gate_up = dot(normed_mlp_all, w_gu, 1, 1)
        gate, upward = gate_up[:, :width], gate_up[:, width:]
        hidden = (gate * jax.nn.sigmoid(gate) * upward).astype(BF)
        if ahead:
            own = own_later[level]
            w_attn = with_far(own[:cut], far_next[1], counts[:2])
            w_attn = all_columns(plan, w_attn, False)
            got = jnp.concatenate([far_next[0], far_next[2], far_next[3]], axis=0)
            rest = with_far(own[cut:], got, counts[2:])
            rest = all_columns(plan, rest, False)
            later = (rest[: 2 * width], rest[2 * width :])
            full.append((w_attn[: 2 * qkv_rows], w_attn[2 * qkv_rows :], later))
        if level < LAYERS - 1:
            result = middle + sum_rows(plan, dot(hidden, w_d, 1, 0))
        kept.append(
            (
                stream,
                scale_attn,
                normed_all,
                heads,
                out,
                log_total,
                attended,
                middle,
                scale_mlp,
                normed_mlp_all,
                gate_up,
                hidden,
            )
        )
        if level < LAYERS - 1:
            stream = result

    def to_pack(rows, other):
        mine = jnp.where(plan.c == plan.zp, rows, other)
        got = plan.core(jnp.where(plan.c == plan.zp, other, rows))
        count = rows.shape[0]
        near = plan.near(jnp.concatenate([mine, got], axis=0))
        return jnp.concatenate([mine, near[:count], got, near[count:]], axis=0)


    def weight_grads(grad_qkv, grad_wo, grad_wg, grad_wu, grad_wd):
        third = qkv_rows // 3

        def member(i):
            rows = [half[i * third : (i + 1) * third] for half in grad_qkv]
            return jnp.concatenate(rows, axis=0).T

        return (
            member(0),
            member(1),
            member(2),
            jnp.concatenate(grad_wo, axis=0),
            jnp.concatenate(grad_wg, axis=0).T,
            jnp.concatenate(grad_wu, axis=0).T,
            jnp.concatenate(grad_wd, axis=0),
        )

    grads = [None] * LAYERS
    gain_rows = [None] * (2 * LAYERS)
    carried = None
    for level in reversed(range(LAYERS)):
        (
            stream,
            scale_attn,
            normed_all,
            heads,
            out,
            log_total,
            attended,
            middle,
            scale_mlp,
            normed_mlp_all,
            gate_up,
            hidden,
        ) = kept[level]
        w_qkv, w_o, w_gu, w_d = full[level]
        width = 2 * mlp_rows
        if level == LAYERS - 1:
            branch = out_branch
        else:
            branch = gather_rows(plan, grad_stream.astype(BF))
        grad_hidden = dot(branch, w_d, 1, 1)
        gate, upward = gate_up[:, :width], gate_up[:, width:]
        sigma = jax.nn.sigmoid(gate)
        grad_gate = (grad_hidden * upward * sigma * (1.0 + gate * (1.0 - sigma))).astype(BF)
        grad_up = (grad_hidden * gate * sigma).astype(BF)
        grad_gu = jnp.concatenate([grad_gate, grad_up], axis=1)
        partial, grad_gu = together(dot(grad_gu, w_gu, 1, 0), grad_gu)
        grad_normed = sum_rows(plan, partial)
        grad_wd = dot(hidden, branch, 0, 0).astype(BF)
        grad_wgu = dot(grad_gu, normed_mlp_all, 0, 0).astype(BF)
        grad_mlp = jnp.concatenate([grad_wgu, grad_wd], axis=0)
        if level == 0:
            grad_normed, grad_mlp, sum_attn = together(grad_normed, grad_mlp, sum_attn)
        else:
            grad_normed, grad_mlp = together(grad_normed, grad_mlp)
        sum_mlp = columns_sum(plan, grad_mlp, False)
        gain_rows[2 + level], through = norm_back(
            middle, scale_mlp, gain_full[2 + level : 3 + level], grad_normed
        )
        grad_middle = grad_stream + through
        branch = gather_rows(plan, grad_middle.astype(BF))
        if level == 0:
            later_mlp, branch = together(later_mlp, branch)
            mine_mlp, far = far_halves(later_mlp, counts[2:])
            mine_attn, far_attn = far_halves(sum_attn, counts[:2])
            far_a = plan.far(far[:mlp_rows])
        if level == LAYERS - 1:
            partial, branch = together(dot(hidden, w_d, 1, 0), branch)
            last = sum_rows(plan, partial)
        grad_wo = dot(attended, branch, 1, 0).astype(BF)
        grad_attended = dot(w_o, branch, 1, 1).astype(BF)
        grad_attended = to_heads(plan, grad_attended.reshape(4, HEAD, tok_rows))
        if level == 0:
            far_b, far_a = together(far[mlp_rows : 2 * mlp_rows], far_a)
            far_b = plan.far(far_b)
            grad_attended, far_a = together(grad_attended, far_a)
        elif level == LAYERS - 1:
            grad_attended, last = together(grad_attended, last)
            last = from_block_order(plan, (middle + last).astype(BF))
            other = plan.far(last)
        grad_q, grad_k, grad_v = attend_back(
            where_all, first_query, heads, grad_attended, out, log_total
        )
        if level == 0:
            far_c = jnp.concatenate([far_attn, far[2 * mlp_rows :]], axis=0)
            far_c, far_b = together(far_c, far_b)
            far_c = plan.far(far_c)
            grad_q, far_b = together(grad_q, far_b)
        elif level == LAYERS - 1:
            grad_q, other = together(grad_q, other)
            last = to_pack(last, other)
        grad_k = more_keys_sum(plan, grad_k)
        grad_v = more_keys_sum(plan, grad_v)
        if level > 0:
            grad_v = [0.5 * block for block in grad_v]
            if carried is None:
                carried = grad_v
            else:
                carried = [left + right for left, right in zip(carried, grad_v)]
        else:
            grad_v = [left + right for left, right in zip(grad_v, carried)]
        grad_heads = [
            jnp.stack(
                [
                    turn(grad_q[k], cos_all[k], -sine_all[k]).astype(BF),
                    turn(grad_k[k], cos_all[k], -sine_all[k]).astype(BF),
                    grad_v[k].astype(BF),
                ]
            )
            for k in range(4)
        ]
        grad_qkv = from_heads(plan, grad_heads).reshape(2, 2, 3, HEAD, tok_rows)
        grad_qkv = jnp.swapaxes(grad_qkv, 1, 2).reshape(-1, tok_rows)
        if level == 0:
            grad_qkv, far_c = together(grad_qkv, far_c)
        elif level == LAYERS - 1:
            grad_qkv, last = together(grad_qkv, last)
            outputs = natural_rows(plan, last)
        grad_wqkv = dot(grad_qkv, normed_all, 1, 0).astype(BF)
        partial = dot(grad_qkv, w_qkv, 0, 0)
        if level == 0:
            mine_first, far = far_halves(sum_mlp, counts[2:])
            far_d, partial = together(far[:mlp_rows], partial)
            far_d = plan.far(far_d)
        grad_normed = sum_rows(plan, partial)
        if level == 0:
            far_e = far[mlp_rows:]
            grad_normed, far_d, far_e = together(grad_normed, far_d, far_e)
            cut = qkv_rows + out_rows
            got = jnp.concatenate([far_c[:cut], far_a, far_b, far_c[cut:]], axis=0).astype(F32)
            mine = jnp.concatenate([mine_attn, mine_mlp], axis=0)
            grads[1] = weight_grads(*core_halves(plan, mine + got, counts))
        else:
            grad_normed, later_mlp = together(grad_normed, sum_mlp)
        grad_attn = jnp.concatenate([grad_wqkv, grad_wo], axis=0)
        sum_attn = columns_sum(plan, grad_attn, False)
        gain_rows[level], through = norm_back(
            stream, scale_attn, gain_full[level : level + 1], grad_normed
        )
        grad_stream = grad_middle + through

    rows = from_block_order(plan, grad_stream.astype(BF))
    gain_sum = jnp.concatenate(gain_rows + [jnp.zeros((12, model), F32)], axis=0)
    gain_near = plan.near(gain_sum)
    other, gain_near, far_e = together(plan.far(rows), gain_near, far_e)
    far_e = plan.far(far_e)
    group_rows = tok_rows // plan.ctx
    owner_grid = owner_order[0].reshape(plan.ctx, plan.ctx, group_rows)
    local_rows = (
        lax.dynamic_index_in_dim(owner_grid, plan.x, 1, False) - plan.x * tok_rows
    ).reshape(tok_rows)
    local_rows = local_rows ^ (plan.part * part_rows)
    slots, far_e = together(to_pack(rows, other)[local_rows], far_e)
    grad_tokens = lax.all_to_all(slots, "ctx", split_axis=0, concat_axis=0, tiled=True)

    got = jnp.concatenate([far_d, far_e], axis=0).astype(F32)
    rest = core_halves(plan, mine_first + got, counts[2:])
    gain_sum = columns_sum(plan, gain_sum + gain_near, True)
    mine, far = far_halves(sum_attn, counts[:2])
    far = jnp.concatenate([far, gain_sum.astype(BF)], axis=0)
    far = plan.far(far)
    grad_tokens, far = together(grad_tokens, far)
    grad_tokens = grad_tokens.astype(F32)
    total = jnp.concatenate([mine, gain_sum], axis=0) + far.astype(F32)
    first = core_halves(plan, total, [qkv_rows, out_rows, gain_sum.shape[0]])
    total = first[2][0] + first[2][1]
    grads[0] = weight_grads(first[0], first[1], *rest)

    stacked = [jnp.stack([grads[level][i] for level in range(LAYERS)]) for i in range(7)]
    return (
        outputs,
        grad_tokens,
        total[:2],
        stacked[0],
        stacked[1],
        stacked[2],
        stacked[3],
        total[2:4],
        stacked[4],
        stacked[5],
        stacked[6],
    )


def solution(mesh):
    columns = P(None, ("fsdp", "ctx"), "tp")
    rows = P(None, "tp", ("fsdp", "ctx"))
    gain = P(None, ("fsdp", "ctx"))
    tokens = P(("fsdp", "ctx"), None)
    return jax.shard_map(
        local,
        mesh=mesh,
        in_specs=(
            tokens,
            tokens,
            P("fsdp", None),
            P("fsdp", None),
            gain,
            columns,
            columns,
            columns,
            rows,
            gain,
            columns,
            columns,
            rows,
        ),
        out_specs=(
            tokens,
            tokens,
            gain,
            columns,
            columns,
            columns,
            rows,
            gain,
            columns,
            columns,
            rows,
        ),
        check_vma=False,
    )
```

```python
import functools

import jax
import jax.numpy as jnp
from jax import lax
from jax.experimental import pallas as pl
from jax.experimental.pallas import tpu as pltpu
from jax.sharding import PartitionSpec as P

HEAD = 64
HALF = HEAD // 2
LAYERS = 2
EPS = 1e-05
THETA = 10000.0
NEG = -1e30
BF = jnp.bfloat16
F32 = jnp.float32
IN_VMEM = pl.BlockSpec(memory_space=pltpu.VMEM)
IN_SMEM = pl.BlockSpec(memory_space=pltpu.SMEM)


def dot(left, right, left_dim, right_dim):
    return lax.dot_general(
        left, right, (((left_dim,), (right_dim,)), ((), ())), preferred_element_type=F32
    )


def mm(left, right):
    return jnp.dot(left, right, preferred_element_type=F32)


class Plan:
    def __init__(self):
        self.fsdp = lax.axis_size("fsdp")
        self.ctx = lax.axis_size("ctx")
        self.tp = lax.axis_size("tp")
        self.high = self.fsdp // 2
        f = lax.axis_index("fsdp")
        z = lax.axis_index("tp")
        self.c = f % 2
        self.fh = f // 2
        self.x = lax.axis_index("ctx")
        self.zl = z % 2
        self.zp = z // 2
        self.ci = self.x % 4
        self.part = self.c * 2 + self.zl
        self.peers = self.high * self.ctx

    def core(self, value):
        return lax.ppermute(value, "fsdp", [(i, i ^ 1) for i in range(self.fsdp)])

    def near(self, value):
        return lax.ppermute(value, "tp", [(i, i ^ 1) for i in range(self.tp)])

    def far(self, value):
        return lax.ppermute(value, "tp", [(i, i ^ 2) for i in range(self.tp)])

    def side(self, value, k):
        return lax.ppermute(value, "ctx", [(i, i ^ k) for i in range(self.ctx)])

    def high_fsdp(self, value, k):
        return lax.ppermute(value, "fsdp", [(i, i ^ (2 * k)) for i in range(self.fsdp)])


def flip_list(blocks, index):
    bit = 1
    while bit < len(blocks):
        on = (index & bit) != 0
        blocks = [jnp.where(on, blocks[i ^ bit], blocks[i]) for i in range(len(blocks))]
        bit *= 2
    return blocks


def place(blocks, index, axis):
    width = blocks[0].shape[axis]
    shape = list(blocks[0].shape)
    shape[axis] = width * len(blocks)
    full = jnp.zeros(shape, blocks[0].dtype)
    for i, block in enumerate(blocks):
        full = lax.dynamic_update_slice_in_dim(full, block, (index ^ i) * width, axis)
    return full


def to_block_order(plan, rows):
    width = rows.shape[1] // (2 * plan.peers)
    parts = []
    for h in range(plan.high):
        for x in range(plan.ctx):
            for c in range(2):
                start = ((h * 2 + c) * plan.ctx + x) * width
                parts.append(rows[:, start : start + width])
    return jnp.concatenate(parts, axis=1)


def from_block_order(plan, rows):
    width = rows.shape[1] // (2 * plan.peers)
    parts = []
    for h in range(plan.high):
        for c in range(2):
            for x in range(plan.ctx):
                start = ((h * plan.ctx + x) * 2 + c) * width
                parts.append(rows[:, start : start + width])
    return jnp.concatenate(parts, axis=1)


def gather_rows(plan, rows):
    pair = jnp.concatenate([rows, plan.near(rows)], axis=0)
    return jnp.concatenate([pair, plan.core(pair)], axis=0)


def sum_rows(plan, partial):
    half = partial.shape[0] // 2
    pair = partial[:half] + plan.core(partial[half:].astype(BF)).astype(F32)
    half = half // 2
    return pair[:half] + plan.near(pair[half:].astype(BF)).astype(F32)


def natural_rows(plan, rows):
    count = rows.shape[0] // 4
    parts = [
        lax.dynamic_slice_in_dim(rows, (plan.part ^ i) * count, count, 0) for i in range(4)
    ]
    return jnp.concatenate(parts, axis=0)


def own_columns(plan, halves):
    keep = lax.dynamic_index_in_dim(halves, plan.c, 0, False)
    got = plan.core(lax.dynamic_index_in_dim(halves, 1 - plan.c, 0, False))
    return jnp.where(
        plan.c == 0,
        jnp.concatenate([keep, got], axis=1),
        jnp.concatenate([got, keep], axis=1),
    )


def all_columns(plan, rows, direct):
    if direct and plan.peers == 4:
        return place([rows] + [plan.side(rows, k) for k in range(1, 4)], plan.x, 1)
    full = lax.all_gather(rows, "ctx", axis=1, tiled=True)
    if plan.high > 1:
        parts = [full] + [plan.high_fsdp(full, k) for k in range(1, plan.high)]
        full = place(parts, plan.fh, 1)
    return full


def columns_sum(plan, grad, direct):
    if plan.high > 1:
        width = grad.shape[1] // plan.high
        parts = [
            lax.dynamic_slice_in_dim(grad, (plan.fh ^ k) * width, width, 1)
            for k in range(plan.high)
        ]
        grad = parts[0]
        for k in range(1, plan.high):
            grad = grad + plan.high_fsdp(parts[k], k)
    if direct and plan.ctx == 4:
        width = grad.shape[1] // 4
        parts = [
            lax.dynamic_slice_in_dim(grad, (plan.x ^ k) * width, width, 1) for k in range(4)
        ]
        total = parts[0].astype(F32)
        for k in range(1, 4):
            total = total + plan.side(parts[k], k).astype(F32)
        return total
    return lax.psum_scatter(grad, "ctx", scatter_dimension=1, tiled=True)


def together(value, *others):
    many = isinstance(value, list)
    got = lax.optimization_barrier((*value, *others) if many else (value, *others))
    count = len(value) if many else 1
    first = list(got[:count]) if many else got[0]
    return (first, *got[count:])


def with_far(own, far, counts):
    parts = []
    start = 0
    for rows in counts:
        parts += [own[start : start + rows], far[start : start + rows]]
        start += rows
    return jnp.concatenate(parts, axis=0)


def far_halves(total, counts):
    mine, far = [], []
    start = 0
    for rows in counts:
        mine.append(total[start : start + rows])
        far.append(total[start + rows : start + 2 * rows])
        start += 2 * rows
    return jnp.concatenate(mine, axis=0).astype(F32), jnp.concatenate(far, axis=0).astype(BF)


def core_halves(plan, own, counts):
    width = own.shape[1]
    left, right = own[:, : width // 2], own[:, width // 2 :]
    kept = jnp.where(plan.c == 0, left, right)
    got = plan.core(jnp.where(plan.c == 0, right, left).astype(BF)).astype(F32)
    low = jnp.where(plan.c == 0, kept, got)
    high = jnp.where(plan.c == 0, got, kept)
    out = []
    start = 0
    for rows in counts:
        out.append((low[start : start + rows], high[start : start + rows]))
        start += rows
    return out


def split_hidden(weight):
    return weight.reshape(2, weight.shape[0] // 2, weight.shape[1])


def turn(values, cos_tab, sine_tab):
    first, second = values[..., :HALF, :], values[..., HALF:, :]
    return jnp.concatenate(
        [first * cos_tab - second * sine_tab, second * cos_tab + first * sine_tab], axis=-2
    )


def to_heads(plan, values):
    got = [lax.dynamic_index_in_dim(values, plan.ci, 0, False)]
    for k in range(1, 4):
        got.append(plan.side(lax.dynamic_index_in_dim(values, plan.ci ^ k, 0, False), k))
    return got


def from_heads(plan, blocks):
    got = [blocks[0]] + [plan.side(blocks[k], k) for k in range(1, 4)]
    return place([block[None] for block in got], plan.ci, 0)


def more_keys(plan, blocks):
    full = list(blocks)
    for m in range(1, plan.ctx // 4):
        full += [plan.side(block, 4 * m) for block in blocks]
    return full


def more_keys_sum(plan, blocks):
    total = list(blocks[:4])
    for m in range(1, plan.ctx // 4):
        total = [total[k] + plan.side(blocks[4 * m + k], 4 * m) for k in range(4)]
    return total


def seen(first_row, part, key_block, query_block, size):
    turned = part * (size // 4)
    key = key_block * size + (lax.broadcasted_iota(jnp.int32, (size, 1), 0) ^ turned)
    query = query_block * size + (lax.broadcasted_iota(jnp.int32, (1, size), 1) ^ turned)
    return (key <= query) & (key >= first_row)


def attend_kernel(count, place_ref, first_ref, *refs):
    blocks, (out_ref, low_ref, lse_ref, kt_ref, v_ref) = refs[:count], refs[count:]
    size = blocks[0].shape[2]
    x, part = place_ref[0], place_ref[1]
    for k in range(count):
        kt_ref[x ^ k] = blocks[k][1].T
        v_ref[x ^ k] = blocks[k][2]
    for k in range(4):
        block = x ^ k
        query = blocks[k][0] * BF(HEAD ** (-0.5))
        first_row = first_ref[k]

        def step(kb, carry):
            peak, total, acc = carry
            s = mm(kt_ref[kb], query)
            s = jnp.where(seen(first_row, part, kb, block, size), s, NEG)
            top = jnp.maximum(peak, jnp.max(s, axis=0, keepdims=True))
            p = jnp.exp(s - top)
            fade = jnp.exp(peak - top)
            total = fade * total + jnp.sum(p, axis=0, keepdims=True)
            return top, total, fade * acc + mm(v_ref[kb], p.astype(BF))

        start = (
            jnp.full((1, size), NEG, F32),
            jnp.zeros((1, size), F32),
            jnp.zeros((HEAD, size), F32),
        )
        peak, total, acc = lax.fori_loop(place_ref[2 + block], block + 1, step, start)
        acc = acc / total
        out_ref[k] = acc
        low_ref[k] = acc.astype(BF)
        lse_ref[k] = peak + jnp.log(total)


def attend(where_all, first_query, blocks):
    count = len(blocks)
    size = blocks[0].shape[2]
    return pl.pallas_call(
        functools.partial(attend_kernel, count),
        out_shape=(
            jax.ShapeDtypeStruct((4, HEAD, size), F32),
            jax.ShapeDtypeStruct((4, HEAD, size), BF),
            jax.ShapeDtypeStruct((4, 1, size), F32),
        ),
        in_specs=[IN_SMEM] + [IN_VMEM] * (1 + count),
        out_specs=(IN_VMEM,) * 3,
        scratch_shapes=[
            pltpu.VMEM((count, size, HEAD), BF),
            pltpu.VMEM((count, HEAD, size), BF),
        ],
        name="attend",
    )(where_all, first_query, *blocks)


def back_kernel(count, place_ref, first_ref, out_ref, lse_ref, *refs):
    blocks, grads = refs[:count], refs[count : count + 4]
    dq_ref, dk_ref, dv_ref, kt_ref, vt_ref, k_ref, dks_ref, dvs_ref = refs[count + 4 :]
    size = blocks[0].shape[2]
    x, part = place_ref[0], place_ref[1]
    for k in range(count):
        kt_ref[x ^ k] = blocks[k][1].T
        vt_ref[x ^ k] = blocks[k][2].T
        k_ref[x ^ k] = blocks[k][1]
    dks_ref[...] = jnp.zeros_like(dks_ref)
    dvs_ref[...] = jnp.zeros_like(dvs_ref)
    for k in range(4):
        block = x ^ k
        query = blocks[k][0] * BF(HEAD ** (-0.5))
        query_t = query.T
        grad = grads[k][...]
        grad_t = grad.T
        delta = jnp.sum(grad.astype(F32) * out_ref[k], axis=0, keepdims=True)
        lse = lse_ref[k]
        first_row = first_ref[k]

        def step(kb, dq):
            s = mm(kt_ref[kb], query)
            p = jnp.where(seen(first_row, part, kb, block, size), jnp.exp(s - lse), 0.0)
            dp = mm(vt_ref[kb], grad)
            ds = (p * (dp - delta)).astype(BF)
            dvs_ref[kb] += mm(p.astype(BF), grad_t)
            dks_ref[kb] += mm(ds, query_t)
            return dq + mm(k_ref[kb], ds)

        dq = lax.fori_loop(
            place_ref[2 + block], block + 1, step, jnp.zeros((HEAD, size), F32)
        )
        dq_ref[k] = dq * HEAD ** (-0.5)
    for k in range(count):
        dk_ref[k] = dks_ref[x ^ k].T
        dv_ref[k] = dvs_ref[x ^ k].T


def attend_back(where_all, first_query, blocks, grads, out, log_total):
    count = len(blocks)
    size = blocks[0].shape[2]
    return pl.pallas_call(
        functools.partial(back_kernel, count),
        out_shape=(
            jax.ShapeDtypeStruct((4, HEAD, size), F32),
            jax.ShapeDtypeStruct((count, HEAD, size), F32),
            jax.ShapeDtypeStruct((count, HEAD, size), F32),
        ),
        in_specs=[IN_SMEM] + [IN_VMEM] * (3 + count + 4),
        out_specs=(IN_VMEM,) * 3,
        scratch_shapes=[
            pltpu.VMEM((count, size, HEAD), BF),
            pltpu.VMEM((count, size, HEAD), BF),
            pltpu.VMEM((count, HEAD, size), BF),
            pltpu.VMEM((count, size, HEAD), F32),
            pltpu.VMEM((count, size, HEAD), F32),
        ],
        name="attend_back",
    )(where_all, first_query, out, log_total, *blocks, *grads)


def norm_scale(stream):
    return lax.rsqrt(jnp.mean(stream * stream, axis=-1, keepdims=True) + EPS)


def norm_back(stream, scale, gain, grad_normed):
    weighted = grad_normed * gain
    grad_gain = jnp.sum(grad_normed * stream * scale, axis=0, keepdims=True)
    grad_stream = scale * weighted - stream * scale**3 * jnp.mean(
        weighted * stream, axis=1, keepdims=True
    )
    return (grad_gain, grad_stream)


def local(
    tokens,
    out_grad,
    segment_ids,
    owner_order,
    attn_gain,
    w_query,
    w_key,
    w_value,
    w_out,
    mlp_gain,
    w_gate,
    w_up,
    w_down,
):
    plan = Plan()
    tok_rows = tokens.shape[0]
    part_rows = tok_rows // 4
    model = tokens.shape[1]

    gains = jnp.concatenate([attn_gain, mlp_gain], axis=0)
    gains = jnp.concatenate([gains, jnp.zeros((12, gains.shape[1]), BF)], axis=0)
    qkv_rows = 3 * w_query.shape[2] // 2
    out_rows = w_out.shape[1] // 2
    mlp_rows = w_down.shape[1] // 2
    counts = [qkv_rows, out_rows] + [mlp_rows] * 3

    def own_weights(level):
        qkv = [split_hidden(w[level].T) for w in (w_query, w_key, w_value)]
        return [
            jnp.concatenate(qkv, axis=1),
            split_hidden(w_out[level]),
            split_hidden(w_gate[level].T),
            split_hidden(w_up[level].T),
            split_hidden(w_down[level]),
        ]

    groups = own_weights(0)
    own_later = []
    for level in range(1, LAYERS):
        own = own_columns(plan, jnp.concatenate(own_weights(level), axis=1))
        own_later.append(own)
    cut = qkv_rows + out_rows
    pieces = [(cut, cut + mlp_rows), (0, cut)]
    pieces += [(cut + i * mlp_rows, cut + (i + 1) * mlp_rows) for i in (1, 2)]
    def own_rows(array):
        mine = lax.dynamic_slice_in_dim(array, plan.part * part_rows, part_rows, 0)
        got = plan.core(
            lax.dynamic_slice_in_dim(array, (plan.part ^ 2) * part_rows, part_rows, 0)
        )
        return to_block_order(plan, jnp.where(plan.c == plan.zp, mine, got))

    token_rows = own_rows(tokens)
    tokens_all = gather_rows(plan, token_rows).astype(F32)
    stream = token_rows.astype(F32)
    grad_rows = own_rows(out_grad)
    grad_stream = grad_rows.astype(F32)

    own = own_columns(plan, groups[0])
    far_first = plan.far(own)
    own_rest = own_columns(plan, jnp.concatenate(groups[1:], axis=1))
    got = plan.core(gains)
    gain_pair = jnp.where(
        plan.c == 0,
        jnp.concatenate([gains, got], axis=1),
        jnp.concatenate([got, gains], axis=1),
    )
    own_rest, far_first, grad_rows = together(own_rest, far_first, grad_rows)
    out_branch = gather_rows(plan, grad_rows)
    first = jnp.concatenate([own, far_first, gain_pair], axis=0)
    first = all_columns(plan, first, True)
    w_qkv, gain_full = first[: 2 * qkv_rows], first[2 * qkv_rows :].astype(F32)
    last_far = plan.far(own_rest)

    segment = jnp.where(plan.c == plan.zp, segment_ids, plan.core(segment_ids))[0]
    pack = segment.shape[0]
    index_all = jnp.arange(pack, dtype=jnp.int32)
    run_start = jnp.concatenate([jnp.ones((1,), dtype=bool), segment[1:] != segment[:-1]])
    run_first = lax.cummax(jnp.where(run_start, index_all, jnp.zeros_like(index_all)), axis=0)
    where_all = jnp.concatenate(
        [jnp.stack([plan.x, plan.part]).astype(jnp.int32), run_first[::tok_rows] // tok_rows]
    )

    def by_peer(row):
        grid = row.reshape(plan.ctx, 4, part_rows)
        blocks = [lax.dynamic_index_in_dim(grid, plan.x ^ k, 0, False) for k in range(4)]
        grid = jnp.stack(blocks)
        return jnp.concatenate(flip_list([grid[:, i] for i in range(4)], plan.part), axis=1)

    positions = by_peer((index_all - run_first).astype(F32))
    first_query = by_peer(run_first)[:, None, :]
    frequency = THETA ** (-(jnp.arange(HALF, dtype=F32) * 2.0 / HEAD))
    angles = frequency[None, :, None] * positions[:, None, :]
    cos_all, sine_all = jnp.cos(angles), jnp.sin(angles)
    cos_own, sine_own = cos_all[0], sine_all[0]

    full = [(w_qkv, None, None)]
    kept = []
    first_values = None
    for level in range(LAYERS):
        w_qkv, w_o, w_mlp = full[level]
        width = 2 * mlp_rows
        if level == 0:
            scale_all = norm_scale(tokens_all)
            scale_attn = scale_all[:part_rows]
            normed_all = (tokens_all * scale_all * gain_full[:1]).astype(BF)
        else:
            scale_attn = norm_scale(stream)
            normed = (stream * scale_attn * gain_full[level : level + 1]).astype(BF)
            normed_all = gather_rows(plan, normed)
        qkv = dot(w_qkv, normed_all, 1, 1)
        if level + 1 < LAYERS:
            qkv, own_later[level] = together(qkv, own_later[level])
        qkv = qkv.reshape(2, 3, 2, HEAD, tok_rows)
        query = turn(qkv[:, 0], cos_own, sine_own).astype(BF)
        key = turn(qkv[:, 1], cos_own, sine_own).astype(BF)
        if level == 0:
            first_values = qkv[:, 2]
            mixed = first_values
        else:
            mixed = 0.5 * qkv[:, 2] + 0.5 * first_values
        heads = jnp.stack([query, key, mixed.astype(BF)], axis=2)
        heads = more_keys(plan, to_heads(plan, heads.reshape(4, 3, HEAD, tok_rows)))
        ahead = level + 1 < LAYERS
        far_next = []

        def next_far():
            nonlocal last_far
            start, end = pieces[len(far_next)]
            piece = own_later[level][start:end]
            if far_next:
                piece, far_next[-1] = together(piece, far_next[-1])
            else:
                piece, last_far = together(piece, last_far)
            return plan.far(piece)

        if level == 0:
            got = next_far()
            heads, last_far, out_branch, got = together(heads, last_far, out_branch, got)
            far_next.append(got)
            rest = with_far(own_rest, last_far, counts[1:])
            w_o = all_columns(plan, rest[: 2 * out_rows], True)
            rest = all_columns(plan, rest[2 * out_rows :], False)
            w_mlp = (rest[: 2 * width], rest[2 * width :])
        out, out_low, log_total = attend(where_all, first_query, heads)
        if ahead:
            out_low, got, w_o = together(out_low, next_far(), w_o)
            far_next.append(got)
        attended = from_heads(plan, [out_low[k] for k in range(4)])
        attended = attended.reshape(4 * HEAD, tok_rows)
        if ahead:
            attended, got = together(attended, next_far())
            far_next.append(got)
        branch = sum_rows(plan, dot(attended, w_o, 0, 0))
        if ahead:
            branch, got = together(branch, next_far())
            far_next.append(got)
        middle = stream + branch
        scale_mlp = norm_scale(middle)
        normed_mlp = (middle * scale_mlp * gain_full[2 + level : 3 + level]).astype(BF)
        normed_mlp_all = gather_rows(plan, normed_mlp)
        w_gu, w_d = w_mlp
        full[level] = (w_qkv, w_o, w_gu, w_d)
        gate_up = dot(normed_mlp_all, w_gu, 1, 1)
        gate, upward = gate_up[:, :width], gate_up[:, width:]
        hidden = (gate * jax.nn.sigmoid(gate) * upward).astype(BF)
        if ahead:
            own = own_later[level]
            w_attn = with_far(own[:cut], far_next[1], counts[:2])
            w_attn = all_columns(plan, w_attn, False)
            got = jnp.concatenate([far_next[0], far_next[2], far_next[3]], axis=0)
            rest = with_far(own[cut:], got, counts[2:])
            rest = all_columns(plan, rest, False)
            later = (rest[: 2 * width], rest[2 * width :])
            full.append((w_attn[: 2 * qkv_rows], w_attn[2 * qkv_rows :], later))
        if level < LAYERS - 1:
            result = middle + sum_rows(plan, dot(hidden, w_d, 1, 0))
        kept.append(
            (
                stream,
                scale_attn,
                normed_all,
                heads,
                out,
                log_total,
                attended,
                middle,
                scale_mlp,
                normed_mlp_all,
                gate_up,
                hidden,
            )
        )
        if level < LAYERS - 1:
            stream = result

    def to_pack(rows, other):
        mine = jnp.where(plan.c == plan.zp, rows, other)
        got = plan.core(jnp.where(plan.c == plan.zp, other, rows))
        count = rows.shape[0]
        near = plan.near(jnp.concatenate([mine, got], axis=0))
        return jnp.concatenate([mine, near[:count], got, near[count:]], axis=0)


    def weight_grads(grad_qkv, grad_wo, grad_wg, grad_wu, grad_wd):
        third = qkv_rows // 3

        def member(i):
            rows = [half[i * third : (i + 1) * third] for half in grad_qkv]
            return jnp.concatenate(rows, axis=0).T

        return (
            member(0),
            member(1),
            member(2),
            jnp.concatenate(grad_wo, axis=0),
            jnp.concatenate(grad_wg, axis=0).T,
            jnp.concatenate(grad_wu, axis=0).T,
            jnp.concatenate(grad_wd, axis=0),
        )

    grads = [None] * LAYERS
    gain_rows = [None] * (2 * LAYERS)
    carried = None
    for level in reversed(range(LAYERS)):
        (
            stream,
            scale_attn,
            normed_all,
            heads,
            out,
            log_total,
            attended,
            middle,
            scale_mlp,
            normed_mlp_all,
            gate_up,
            hidden,
        ) = kept[level]
        w_qkv, w_o, w_gu, w_d = full[level]
        width = 2 * mlp_rows
        if level == LAYERS - 1:
            branch = out_branch
        else:
            branch = gather_rows(plan, grad_stream.astype(BF))
        grad_hidden = dot(branch, w_d, 1, 1)
        gate, upward = gate_up[:, :width], gate_up[:, width:]
        sigma = jax.nn.sigmoid(gate)
        grad_gate = (grad_hidden * upward * sigma * (1.0 + gate * (1.0 - sigma))).astype(BF)
        grad_up = (grad_hidden * gate * sigma).astype(BF)
        grad_gu = jnp.concatenate([grad_gate, grad_up], axis=1)
        partial, grad_gu = together(dot(grad_gu, w_gu, 1, 0), grad_gu)
        grad_normed = sum_rows(plan, partial)
        grad_wd = dot(hidden, branch, 0, 0).astype(BF)
        grad_wgu = dot(grad_gu, normed_mlp_all, 0, 0).astype(BF)
        grad_mlp = jnp.concatenate([grad_wgu, grad_wd], axis=0)
        if level == 0:
            grad_normed, grad_mlp, sum_attn = together(grad_normed, grad_mlp, sum_attn)
        else:
            grad_normed, grad_mlp = together(grad_normed, grad_mlp)
        sum_mlp = columns_sum(plan, grad_mlp, False)
        gain_rows[2 + level], through = norm_back(
            middle, scale_mlp, gain_full[2 + level : 3 + level], grad_normed
        )
        grad_middle = grad_stream + through
        branch = gather_rows(plan, grad_middle.astype(BF))
        if level == 0:
            later_mlp, branch = together(later_mlp, branch)
            mine_mlp, far = far_halves(later_mlp, counts[2:])
            mine_attn, far_attn = far_halves(sum_attn, counts[:2])
            far_a = plan.far(far[:mlp_rows])
        if level == LAYERS - 1:
            partial, branch = together(dot(hidden, w_d, 1, 0), branch)
            last = sum_rows(plan, partial)
        grad_wo = dot(attended, branch, 1, 0).astype(BF)
        grad_attended = dot(w_o, branch, 1, 1).astype(BF)
        grad_attended = to_heads(plan, grad_attended.reshape(4, HEAD, tok_rows))
        if level == 0:
            far_b, far_a = together(far[mlp_rows : 2 * mlp_rows], far_a)
            far_b = plan.far(far_b)
            grad_attended, far_a = together(grad_attended, far_a)
        elif level == LAYERS - 1:
            grad_attended, last = together(grad_attended, last)
            last = from_block_order(plan, (middle + last).astype(BF))
            other = plan.far(last)
        grad_q, grad_k, grad_v = attend_back(
            where_all, first_query, heads, grad_attended, out, log_total
        )
        if level == 0:
            far_c = jnp.concatenate([far_attn, far[2 * mlp_rows :]], axis=0)
            far_c, far_b = together(far_c, far_b)
            far_c = plan.far(far_c)
            grad_q, far_b = together(grad_q, far_b)
        elif level == LAYERS - 1:
            grad_q, other = together(grad_q, other)
            last = to_pack(last, other)
        grad_k = more_keys_sum(plan, grad_k)
        grad_v = more_keys_sum(plan, grad_v)
        if level > 0:
            grad_v = [0.5 * block for block in grad_v]
            if carried is None:
                carried = grad_v
            else:
                carried = [left + right for left, right in zip(carried, grad_v)]
        else:
            grad_v = [left + right for left, right in zip(grad_v, carried)]
        grad_heads = [
            jnp.stack(
                [
                    turn(grad_q[k], cos_all[k], -sine_all[k]).astype(BF),
                    turn(grad_k[k], cos_all[k], -sine_all[k]).astype(BF),
                    grad_v[k].astype(BF),
                ]
            )
            for k in range(4)
        ]
        grad_qkv = from_heads(plan, grad_heads).reshape(2, 2, 3, HEAD, tok_rows)
        grad_qkv = jnp.swapaxes(grad_qkv, 1, 2).reshape(-1, tok_rows)
        if level == 0:
            mine_first, far = far_halves(sum_mlp, counts[2:])
            far_d, far_c = together(far[:mlp_rows], far_c)
            far_d = plan.far(far_d)
            grad_qkv, far_c = together(grad_qkv, far_c)
        elif level == LAYERS - 1:
            grad_qkv, last = together(grad_qkv, last)
            outputs = natural_rows(plan, last)
        grad_wqkv = dot(grad_qkv, normed_all, 1, 0).astype(BF)
        grad_normed = sum_rows(plan, dot(grad_qkv, w_qkv, 0, 0))
        if level == 0:
            far_e = far[mlp_rows:]
            grad_normed, far_d, far_e = together(grad_normed, far_d, far_e)
            cut = qkv_rows + out_rows
            got = jnp.concatenate([far_c[:cut], far_a, far_b, far_c[cut:]], axis=0).astype(F32)
            mine = jnp.concatenate([mine_attn, mine_mlp], axis=0)
            grads[1] = weight_grads(*core_halves(plan, mine + got, counts))
        else:
            grad_normed, later_mlp = together(grad_normed, sum_mlp)
        grad_attn = jnp.concatenate([grad_wqkv, grad_wo], axis=0)
        sum_attn = columns_sum(plan, grad_attn, False)
        gain_rows[level], through = norm_back(
            stream, scale_attn, gain_full[level : level + 1], grad_normed
        )
        grad_stream = grad_middle + through

    rows = from_block_order(plan, grad_stream.astype(BF))
    gain_sum = jnp.concatenate(gain_rows + [jnp.zeros((12, model), F32)], axis=0)
    gain_near = plan.near(gain_sum)
    other, gain_near, far_e = together(plan.far(rows), gain_near, far_e)
    far_e = plan.far(far_e)
    group_rows = tok_rows // plan.ctx
    owner_grid = owner_order[0].reshape(plan.ctx, plan.ctx, group_rows)
    local_rows = (
        lax.dynamic_index_in_dim(owner_grid, plan.x, 1, False) - plan.x * tok_rows
    ).reshape(tok_rows)
    local_rows = local_rows ^ (plan.part * part_rows)
    gain_sum = columns_sum(plan, gain_sum + gain_near, True)
    mine, far = far_halves(sum_attn, counts[:2])
    far = jnp.concatenate([far, gain_sum.astype(BF)], axis=0)
    slots, far_e, far = together(to_pack(rows, other)[local_rows], far_e, far)
    far = plan.far(far)
    grad_tokens = lax.all_to_all(slots, "ctx", split_axis=0, concat_axis=0, tiled=True)

    got = jnp.concatenate([far_d, far_e], axis=0).astype(F32)
    rest = core_halves(plan, mine_first + got, counts[2:])
    grad_tokens, far = together(grad_tokens, far)
    grad_tokens = grad_tokens.astype(F32)
    total = jnp.concatenate([mine, gain_sum], axis=0) + far.astype(F32)
    first = core_halves(plan, total, [qkv_rows, out_rows, gain_sum.shape[0]])
    total = first[2][0] + first[2][1]
    grads[0] = weight_grads(first[0], first[1], *rest)

    stacked = [jnp.stack([grads[level][i] for level in range(LAYERS)]) for i in range(7)]
    return (
        outputs,
        grad_tokens,
        total[:2],
        stacked[0],
        stacked[1],
        stacked[2],
        stacked[3],
        total[2:4],
        stacked[4],
        stacked[5],
        stacked[6],
    )


def solution(mesh):
    columns = P(None, ("fsdp", "ctx"), "tp")
    rows = P(None, "tp", ("fsdp", "ctx"))
    gain = P(None, ("fsdp", "ctx"))
    tokens = P(("fsdp", "ctx"), None)
    return jax.shard_map(
        local,
        mesh=mesh,
        in_specs=(
            tokens,
            tokens,
            P("fsdp", None),
            P("fsdp", None),
            gain,
            columns,
            columns,
            columns,
            rows,
            gain,
            columns,
            columns,
            rows,
        ),
        out_specs=(
            tokens,
            tokens,
            gain,
            columns,
            columns,
            columns,
            rows,
            gain,
            columns,
            columns,
            rows,
        ),
        check_vma=False,
    )
```

```python
import functools

import jax
import jax.numpy as jnp
from jax import lax
from jax.experimental import pallas as pl
from jax.experimental.pallas import tpu as pltpu
from jax.sharding import PartitionSpec as P

HEAD = 64
HALF = HEAD // 2
LAYERS = 2
EPS = 1e-05
THETA = 10000.0
NEG = -1e30
BF = jnp.bfloat16
F32 = jnp.float32
IN_VMEM = pl.BlockSpec(memory_space=pltpu.VMEM)
IN_SMEM = pl.BlockSpec(memory_space=pltpu.SMEM)


def dot(left, right, left_dim, right_dim):
    return lax.dot_general(
        left, right, (((left_dim,), (right_dim,)), ((), ())), preferred_element_type=F32
    )


def mm(left, right):
    return jnp.dot(left, right, preferred_element_type=F32)


class Plan:
    def __init__(self):
        self.fsdp = lax.axis_size("fsdp")
        self.ctx = lax.axis_size("ctx")
        self.tp = lax.axis_size("tp")
        self.high = self.fsdp // 2
        f = lax.axis_index("fsdp")
        z = lax.axis_index("tp")
        self.c = f % 2
        self.fh = f // 2
        self.x = lax.axis_index("ctx")
        self.zl = z % 2
        self.zp = z // 2
        self.ci = self.x % 4
        self.part = self.c * 2 + self.zl
        self.peers = self.high * self.ctx

    def core(self, value):
        return lax.ppermute(value, "fsdp", [(i, i ^ 1) for i in range(self.fsdp)])

    def near(self, value):
        return lax.ppermute(value, "tp", [(i, i ^ 1) for i in range(self.tp)])

    def far(self, value):
        return lax.ppermute(value, "tp", [(i, i ^ 2) for i in range(self.tp)])

    def side(self, value, k):
        return lax.ppermute(value, "ctx", [(i, i ^ k) for i in range(self.ctx)])

    def high_fsdp(self, value, k):
        return lax.ppermute(value, "fsdp", [(i, i ^ (2 * k)) for i in range(self.fsdp)])


def flip_list(blocks, index):
    bit = 1
    while bit < len(blocks):
        on = (index & bit) != 0
        blocks = [jnp.where(on, blocks[i ^ bit], blocks[i]) for i in range(len(blocks))]
        bit *= 2
    return blocks


def place(blocks, index, axis):
    width = blocks[0].shape[axis]
    shape = list(blocks[0].shape)
    shape[axis] = width * len(blocks)
    full = jnp.zeros(shape, blocks[0].dtype)
    for i, block in enumerate(blocks):
        full = lax.dynamic_update_slice_in_dim(full, block, (index ^ i) * width, axis)
    return full


def to_block_order(plan, rows):
    width = rows.shape[1] // (2 * plan.peers)
    parts = []
    for h in range(plan.high):
        for x in range(plan.ctx):
            for c in range(2):
                start = ((h * 2 + c) * plan.ctx + x) * width
                parts.append(rows[:, start : start + width])
    return jnp.concatenate(parts, axis=1)


def from_block_order(plan, rows):
    width = rows.shape[1] // (2 * plan.peers)
    parts = []
    for h in range(plan.high):
        for c in range(2):
            for x in range(plan.ctx):
                start = ((h * plan.ctx + x) * 2 + c) * width
                parts.append(rows[:, start : start + width])
    return jnp.concatenate(parts, axis=1)


def gather_rows(plan, rows):
    pair = jnp.concatenate([rows, plan.near(rows)], axis=0)
    return jnp.concatenate([pair, plan.core(pair)], axis=0)


def sum_rows(plan, partial):
    half = partial.shape[0] // 2
    pair = partial[:half] + plan.core(partial[half:].astype(BF)).astype(F32)
    half = half // 2
    return pair[:half] + plan.near(pair[half:].astype(BF)).astype(F32)


def natural_rows(plan, rows):
    count = rows.shape[0] // 4
    parts = [
        lax.dynamic_slice_in_dim(rows, (plan.part ^ i) * count, count, 0) for i in range(4)
    ]
    return jnp.concatenate(parts, axis=0)


def own_columns(plan, halves):
    keep = lax.dynamic_index_in_dim(halves, plan.c, 0, False)
    got = plan.core(lax.dynamic_index_in_dim(halves, 1 - plan.c, 0, False))
    return jnp.where(
        plan.c == 0,
        jnp.concatenate([keep, got], axis=1),
        jnp.concatenate([got, keep], axis=1),
    )


def all_columns(plan, rows, direct):
    if direct and plan.peers == 4:
        return place([rows] + [plan.side(rows, k) for k in range(1, 4)], plan.x, 1)
    full = lax.all_gather(rows, "ctx", axis=1, tiled=True)
    if plan.high > 1:
        parts = [full] + [plan.high_fsdp(full, k) for k in range(1, plan.high)]
        full = place(parts, plan.fh, 1)
    return full


def columns_sum(plan, grad, direct):
    if plan.high > 1:
        width = grad.shape[1] // plan.high
        parts = [
            lax.dynamic_slice_in_dim(grad, (plan.fh ^ k) * width, width, 1)
            for k in range(plan.high)
        ]
        grad = parts[0]
        for k in range(1, plan.high):
            grad = grad + plan.high_fsdp(parts[k], k)
    if direct and plan.ctx == 4:
        width = grad.shape[1] // 4
        parts = [
            lax.dynamic_slice_in_dim(grad, (plan.x ^ k) * width, width, 1) for k in range(4)
        ]
        total = parts[0].astype(F32)
        for k in range(1, 4):
            total = total + plan.side(parts[k], k).astype(F32)
        return total
    return lax.psum_scatter(grad, "ctx", scatter_dimension=1, tiled=True)


def together(value, *others):
    many = isinstance(value, list)
    got = lax.optimization_barrier((*value, *others) if many else (value, *others))
    count = len(value) if many else 1
    first = list(got[:count]) if many else got[0]
    return (first, *got[count:])


def with_far(own, far, counts):
    parts = []
    start = 0
    for rows in counts:
        parts += [own[start : start + rows], far[start : start + rows]]
        start += rows
    return jnp.concatenate(parts, axis=0)


def far_halves(total, counts):
    mine, far = [], []
    start = 0
    for rows in counts:
        mine.append(total[start : start + rows])
        far.append(total[start + rows : start + 2 * rows])
        start += 2 * rows
    return jnp.concatenate(mine, axis=0).astype(F32), jnp.concatenate(far, axis=0).astype(BF)


def core_halves(plan, own, counts):
    width = own.shape[1]
    left, right = own[:, : width // 2], own[:, width // 2 :]
    kept = jnp.where(plan.c == 0, left, right)
    got = plan.core(jnp.where(plan.c == 0, right, left).astype(BF)).astype(F32)
    low = jnp.where(plan.c == 0, kept, got)
    high = jnp.where(plan.c == 0, got, kept)
    out = []
    start = 0
    for rows in counts:
        out.append((low[start : start + rows], high[start : start + rows]))
        start += rows
    return out


def split_hidden(weight):
    return weight.reshape(2, weight.shape[0] // 2, weight.shape[1])


def turn(values, cos_tab, sine_tab):
    first, second = values[..., :HALF, :], values[..., HALF:, :]
    return jnp.concatenate(
        [first * cos_tab - second * sine_tab, second * cos_tab + first * sine_tab], axis=-2
    )


def to_heads(plan, values):
    got = [lax.dynamic_index_in_dim(values, plan.ci, 0, False)]
    for k in range(1, 4):
        got.append(plan.side(lax.dynamic_index_in_dim(values, plan.ci ^ k, 0, False), k))
    return got


def from_heads(plan, blocks):
    got = [blocks[0]] + [plan.side(blocks[k], k) for k in range(1, 4)]
    return place([block[None] for block in got], plan.ci, 0)


def more_keys(plan, blocks):
    full = list(blocks)
    for m in range(1, plan.ctx // 4):
        full += [plan.side(block, 4 * m) for block in blocks]
    return full


def more_keys_sum(plan, blocks):
    total = list(blocks[:4])
    for m in range(1, plan.ctx // 4):
        total = [total[k] + plan.side(blocks[4 * m + k], 4 * m) for k in range(4)]
    return total


def seen(first_row, part, key_block, query_block, size):
    turned = part * (size // 4)
    key = key_block * size + (lax.broadcasted_iota(jnp.int32, (size, 1), 0) ^ turned)
    query = query_block * size + (lax.broadcasted_iota(jnp.int32, (1, size), 1) ^ turned)
    return (key <= query) & (key >= first_row)


def attend_kernel(count, place_ref, first_ref, *refs):
    blocks, (out_ref, low_ref, lse_ref, kt_ref, v_ref, q_ref) = refs[:count], refs[count:]
    size = blocks[0].shape[2]
    x, part = place_ref[0], place_ref[1]
    for k in range(count):
        kt_ref[x ^ k] = blocks[k][1].T
        v_ref[x ^ k] = blocks[k][2]
    for k in range(4):
        q_ref[k] = blocks[k][0] * BF(HEAD ** (-0.5))

    @pl.loop(0, 4)
    def _(k):
        block = x ^ k
        query = q_ref[k]
        first_row = first_ref[k]

        def step(kb, carry):
            peak, total, acc = carry
            s = mm(kt_ref[kb], query)
            s = jnp.where(seen(first_row, part, kb, block, size), s, NEG)
            top = jnp.maximum(peak, jnp.max(s, axis=0, keepdims=True))
            p = jnp.exp(s - top)
            fade = jnp.exp(peak - top)
            total = fade * total + jnp.sum(p, axis=0, keepdims=True)
            return top, total, fade * acc + mm(v_ref[kb], p.astype(BF))

        start = (
            jnp.full((1, size), NEG, F32),
            jnp.zeros((1, size), F32),
            jnp.zeros((HEAD, size), F32),
        )
        peak, total, acc = lax.fori_loop(place_ref[2 + block], block + 1, step, start)
        acc = acc / total
        out_ref[k] = acc
        low_ref[k] = acc.astype(BF)
        lse_ref[k] = peak + jnp.log(total)


def attend(where_all, first_query, blocks):
    count = len(blocks)
    size = blocks[0].shape[2]
    return pl.pallas_call(
        functools.partial(attend_kernel, count),
        out_shape=(
            jax.ShapeDtypeStruct((4, HEAD, size), F32),
            jax.ShapeDtypeStruct((4, HEAD, size), BF),
            jax.ShapeDtypeStruct((4, 1, size), F32),
        ),
        in_specs=[IN_SMEM] + [IN_VMEM] * (1 + count),
        out_specs=(IN_VMEM,) * 3,
        scratch_shapes=[
            pltpu.VMEM((count, size, HEAD), BF),
            pltpu.VMEM((count, HEAD, size), BF),
            pltpu.VMEM((4, HEAD, size), BF),
        ],
        name="attend",
    )(where_all, first_query, *blocks)


def back_kernel(count, place_ref, first_ref, out_ref, lse_ref, *refs):
    blocks, grads = refs[:count], refs[count : count + 4]
    dq_ref, dk_ref, dv_ref, kt_ref, vt_ref, k_ref, dks_ref, dvs_ref = refs[count + 4 : -2]
    q_ref, grad_ref = refs[-2:]
    size = blocks[0].shape[2]
    x, part = place_ref[0], place_ref[1]
    for k in range(count):
        kt_ref[x ^ k] = blocks[k][1].T
        vt_ref[x ^ k] = blocks[k][2].T
        k_ref[x ^ k] = blocks[k][1]
    dks_ref[...] = jnp.zeros_like(dks_ref)
    dvs_ref[...] = jnp.zeros_like(dvs_ref)
    for k in range(4):
        q_ref[k] = blocks[k][0] * BF(HEAD ** (-0.5))
        grad_ref[k] = grads[k][...]

    @pl.loop(0, 4)
    def _(k):
        block = x ^ k
        query = q_ref[k]
        query_t = query.T
        grad = grad_ref[k]
        grad_t = grad.T
        delta = jnp.sum(grad.astype(F32) * out_ref[k], axis=0, keepdims=True)
        lse = lse_ref[k]
        first_row = first_ref[k]

        def step(kb, dq):
            s = mm(kt_ref[kb], query)
            p = jnp.where(seen(first_row, part, kb, block, size), jnp.exp(s - lse), 0.0)
            dp = mm(vt_ref[kb], grad)
            ds = (p * (dp - delta)).astype(BF)
            dvs_ref[kb] += mm(p.astype(BF), grad_t)
            dks_ref[kb] += mm(ds, query_t)
            return dq + mm(k_ref[kb], ds)

        dq = lax.fori_loop(
            place_ref[2 + block], block + 1, step, jnp.zeros((HEAD, size), F32)
        )
        dq_ref[k] = dq * HEAD ** (-0.5)

    for k in range(count):
        dk_ref[k] = dks_ref[x ^ k].T
        dv_ref[k] = dvs_ref[x ^ k].T


def attend_back(where_all, first_query, blocks, grads, out, log_total):
    count = len(blocks)
    size = blocks[0].shape[2]
    return pl.pallas_call(
        functools.partial(back_kernel, count),
        out_shape=(
            jax.ShapeDtypeStruct((4, HEAD, size), F32),
            jax.ShapeDtypeStruct((count, HEAD, size), F32),
            jax.ShapeDtypeStruct((count, HEAD, size), F32),
        ),
        in_specs=[IN_SMEM] + [IN_VMEM] * (3 + count + 4),
        out_specs=(IN_VMEM,) * 3,
        scratch_shapes=[
            pltpu.VMEM((count, size, HEAD), BF),
            pltpu.VMEM((count, size, HEAD), BF),
            pltpu.VMEM((count, HEAD, size), BF),
            pltpu.VMEM((count, size, HEAD), F32),
            pltpu.VMEM((count, size, HEAD), F32),
            pltpu.VMEM((4, HEAD, size), BF),
            pltpu.VMEM((4, HEAD, size), BF),
        ],
        name="attend_back",
    )(where_all, first_query, out, log_total, *blocks, *grads)


def norm_scale(stream):
    return lax.rsqrt(jnp.mean(stream * stream, axis=-1, keepdims=True) + EPS)


def norm_back(stream, scale, gain, grad_normed):
    weighted = grad_normed * gain
    grad_gain = jnp.sum(grad_normed * stream * scale, axis=0, keepdims=True)
    grad_stream = scale * weighted - stream * scale**3 * jnp.mean(
        weighted * stream, axis=1, keepdims=True
    )
    return (grad_gain, grad_stream)


def local(
    tokens,
    out_grad,
    segment_ids,
    owner_order,
    attn_gain,
    w_query,
    w_key,
    w_value,
    w_out,
    mlp_gain,
    w_gate,
    w_up,
    w_down,
):
    plan = Plan()
    tok_rows = tokens.shape[0]
    part_rows = tok_rows // 4
    model = tokens.shape[1]

    gains = jnp.concatenate([attn_gain, mlp_gain], axis=0)
    gains = jnp.concatenate([gains, jnp.zeros((12, gains.shape[1]), BF)], axis=0)
    qkv_rows = 3 * w_query.shape[2] // 2
    out_rows = w_out.shape[1] // 2
    mlp_rows = w_down.shape[1] // 2
    counts = [qkv_rows, out_rows] + [mlp_rows] * 3

    def own_weights(level):
        qkv = [split_hidden(w[level].T) for w in (w_query, w_key, w_value)]
        return [
            jnp.concatenate(qkv, axis=1),
            split_hidden(w_out[level]),
            split_hidden(w_gate[level].T),
            split_hidden(w_up[level].T),
            split_hidden(w_down[level]),
        ]

    groups = own_weights(0)
    own_later = []
    for level in range(1, LAYERS):
        own = own_columns(plan, jnp.concatenate(own_weights(level), axis=1))
        own_later.append(own)
    cut = qkv_rows + out_rows
    pieces = [(cut, cut + mlp_rows), (0, cut)]
    pieces += [(cut + i * mlp_rows, cut + (i + 1) * mlp_rows) for i in (1, 2)]
    def own_rows(array):
        mine = lax.dynamic_slice_in_dim(array, plan.part * part_rows, part_rows, 0)
        got = plan.core(
            lax.dynamic_slice_in_dim(array, (plan.part ^ 2) * part_rows, part_rows, 0)
        )
        return to_block_order(plan, jnp.where(plan.c == plan.zp, mine, got))

    token_rows = own_rows(tokens)
    tokens_all = gather_rows(plan, token_rows).astype(F32)
    stream = token_rows.astype(F32)
    grad_rows = own_rows(out_grad)
    grad_stream = grad_rows.astype(F32)

    own = own_columns(plan, groups[0])
    far_first = plan.far(own)
    own_rest = own_columns(plan, jnp.concatenate(groups[1:], axis=1))
    got = plan.core(gains)
    gain_pair = jnp.where(
        plan.c == 0,
        jnp.concatenate([gains, got], axis=1),
        jnp.concatenate([got, gains], axis=1),
    )
    own_rest, far_first, grad_rows = together(own_rest, far_first, grad_rows)
    out_branch = gather_rows(plan, grad_rows)
    first = jnp.concatenate([own, far_first, gain_pair], axis=0)
    first = all_columns(plan, first, True)
    w_qkv, gain_full = first[: 2 * qkv_rows], first[2 * qkv_rows :].astype(F32)
    last_far = plan.far(own_rest)

    segment = jnp.where(plan.c == plan.zp, segment_ids, plan.core(segment_ids))[0]
    pack = segment.shape[0]
    index_all = jnp.arange(pack, dtype=jnp.int32)
    run_start = jnp.concatenate([jnp.ones((1,), dtype=bool), segment[1:] != segment[:-1]])
    run_first = lax.cummax(jnp.where(run_start, index_all, jnp.zeros_like(index_all)), axis=0)
    where_all = jnp.concatenate(
        [jnp.stack([plan.x, plan.part]).astype(jnp.int32), run_first[::tok_rows] // tok_rows]
    )

    def by_peer(row):
        grid = row.reshape(plan.ctx, 4, part_rows)
        blocks = [lax.dynamic_index_in_dim(grid, plan.x ^ k, 0, False) for k in range(4)]
        grid = jnp.stack(blocks)
        return jnp.concatenate(flip_list([grid[:, i] for i in range(4)], plan.part), axis=1)

    positions = by_peer((index_all - run_first).astype(F32))
    first_query = by_peer(run_first)[:, None, :]
    frequency = THETA ** (-(jnp.arange(HALF, dtype=F32) * 2.0 / HEAD))
    angles = frequency[None, :, None] * positions[:, None, :]
    cos_all, sine_all = jnp.cos(angles), jnp.sin(angles)
    cos_own, sine_own = cos_all[0], sine_all[0]

    full = [(w_qkv, None, None)]
    kept = []
    first_values = None
    for level in range(LAYERS):
        w_qkv, w_o, w_mlp = full[level]
        width = 2 * mlp_rows
        if level == 0:
            scale_all = norm_scale(tokens_all)
            scale_attn = scale_all[:part_rows]
            normed_all = (tokens_all * scale_all * gain_full[:1]).astype(BF)
        else:
            scale_attn = norm_scale(stream)
            normed = (stream * scale_attn * gain_full[level : level + 1]).astype(BF)
            normed_all = gather_rows(plan, normed)
        qkv = dot(w_qkv, normed_all, 1, 1)
        if level + 1 < LAYERS:
            qkv, own_later[level] = together(qkv, own_later[level])
        qkv = qkv.reshape(2, 3, 2, HEAD, tok_rows)
        query = turn(qkv[:, 0], cos_own, sine_own).astype(BF)
        key = turn(qkv[:, 1], cos_own, sine_own).astype(BF)
        if level == 0:
            first_values = qkv[:, 2]
            mixed = first_values
        else:
            mixed = 0.5 * qkv[:, 2] + 0.5 * first_values
        heads = jnp.stack([query, key, mixed.astype(BF)], axis=2)
        heads = more_keys(plan, to_heads(plan, heads.reshape(4, 3, HEAD, tok_rows)))
        ahead = level + 1 < LAYERS
        far_next = []

        def next_far():
            nonlocal last_far
            start, end = pieces[len(far_next)]
            piece = own_later[level][start:end]
            if far_next:
                piece, far_next[-1] = together(piece, far_next[-1])
            else:
                piece, last_far = together(piece, last_far)
            return plan.far(piece)

        if level == 0:
            got = next_far()
            heads, last_far, out_branch, got = together(heads, last_far, out_branch, got)
            far_next.append(got)
            rest = with_far(own_rest, last_far, counts[1:])
            w_o = all_columns(plan, rest[: 2 * out_rows], True)
            rest = all_columns(plan, rest[2 * out_rows :], False)
            w_mlp = (rest[: 2 * width], rest[2 * width :])
        out, out_low, log_total = attend(where_all, first_query, heads)
        if ahead:
            out_low, got, w_o = together(out_low, next_far(), w_o)
            far_next.append(got)
        attended = from_heads(plan, [out_low[k] for k in range(4)])
        attended = attended.reshape(4 * HEAD, tok_rows)
        if ahead:
            attended, got = together(attended, next_far())
            far_next.append(got)
        branch = sum_rows(plan, dot(attended, w_o, 0, 0))
        if ahead:
            branch, got = together(branch, next_far())
            far_next.append(got)
        middle = stream + branch
        scale_mlp = norm_scale(middle)
        normed_mlp = (middle * scale_mlp * gain_full[2 + level : 3 + level]).astype(BF)
        normed_mlp_all = gather_rows(plan, normed_mlp)
        w_gu, w_d = w_mlp
        full[level] = (w_qkv, w_o, w_gu, w_d)
        gate_up = dot(normed_mlp_all, w_gu, 1, 1)
        gate, upward = gate_up[:, :width], gate_up[:, width:]
        hidden = (gate * jax.nn.sigmoid(gate) * upward).astype(BF)
        if ahead:
            own = own_later[level]
            w_attn = with_far(own[:cut], far_next[1], counts[:2])
            w_attn = all_columns(plan, w_attn, False)
            got = jnp.concatenate([far_next[0], far_next[2], far_next[3]], axis=0)
            rest = with_far(own[cut:], got, counts[2:])
            rest = all_columns(plan, rest, False)
            later = (rest[: 2 * width], rest[2 * width :])
            full.append((w_attn[: 2 * qkv_rows], w_attn[2 * qkv_rows :], later))
        if level < LAYERS - 1:
            result = middle + sum_rows(plan, dot(hidden, w_d, 1, 0))
        kept.append(
            (
                stream,
                scale_attn,
                normed_all,
                heads,
                out,
                log_total,
                attended,
                middle,
                scale_mlp,
                normed_mlp_all,
                gate_up,
                hidden,
            )
        )
        if level < LAYERS - 1:
            stream = result

    def to_pack(rows, other):
        mine = jnp.where(plan.c == plan.zp, rows, other)
        got = plan.core(jnp.where(plan.c == plan.zp, other, rows))
        count = rows.shape[0]
        near = plan.near(jnp.concatenate([mine, got], axis=0))
        return jnp.concatenate([mine, near[:count], got, near[count:]], axis=0)


    def weight_grads(grad_qkv, grad_wo, grad_wg, grad_wu, grad_wd):
        third = qkv_rows // 3

        def member(i):
            rows = [half[i * third : (i + 1) * third] for half in grad_qkv]
            return jnp.concatenate(rows, axis=0).T

        return (
            member(0),
            member(1),
            member(2),
            jnp.concatenate(grad_wo, axis=0),
            jnp.concatenate(grad_wg, axis=0).T,
            jnp.concatenate(grad_wu, axis=0).T,
            jnp.concatenate(grad_wd, axis=0),
        )

    grads = [None] * LAYERS
    gain_rows = [None] * (2 * LAYERS)
    carried = None
    for level in reversed(range(LAYERS)):
        (
            stream,
            scale_attn,
            normed_all,
            heads,
            out,
            log_total,
            attended,
            middle,
            scale_mlp,
            normed_mlp_all,
            gate_up,
            hidden,
        ) = kept[level]
        w_qkv, w_o, w_gu, w_d = full[level]
        width = 2 * mlp_rows
        if level == LAYERS - 1:
            branch = out_branch
        else:
            branch = gather_rows(plan, grad_stream.astype(BF))
        grad_hidden = dot(branch, w_d, 1, 1)
        gate, upward = gate_up[:, :width], gate_up[:, width:]
        sigma = jax.nn.sigmoid(gate)
        grad_gate = (grad_hidden * upward * sigma * (1.0 + gate * (1.0 - sigma))).astype(BF)
        grad_up = (grad_hidden * gate * sigma).astype(BF)
        grad_gu = jnp.concatenate([grad_gate, grad_up], axis=1)
        partial, grad_gu = together(dot(grad_gu, w_gu, 1, 0), grad_gu)
        grad_normed = sum_rows(plan, partial)
        grad_wd = dot(hidden, branch, 0, 0).astype(BF)
        grad_wgu = dot(grad_gu, normed_mlp_all, 0, 0).astype(BF)
        grad_mlp = jnp.concatenate([grad_wgu, grad_wd], axis=0)
        if level == 0:
            grad_normed, grad_mlp, sum_attn = together(grad_normed, grad_mlp, sum_attn)
        else:
            grad_normed, grad_mlp = together(grad_normed, grad_mlp)
        sum_mlp = columns_sum(plan, grad_mlp, False)
        gain_rows[2 + level], through = norm_back(
            middle, scale_mlp, gain_full[2 + level : 3 + level], grad_normed
        )
        grad_middle = grad_stream + through
        branch = gather_rows(plan, grad_middle.astype(BF))
        if level == 0:
            later_mlp, branch = together(later_mlp, branch)
            mine_mlp, far = far_halves(later_mlp, counts[2:])
            mine_attn, far_attn = far_halves(sum_attn, counts[:2])
            far_a = plan.far(far[:mlp_rows])
        if level == LAYERS - 1:
            partial, branch = together(dot(hidden, w_d, 1, 0), branch)
            last = sum_rows(plan, partial)
        grad_wo = dot(attended, branch, 1, 0).astype(BF)
        grad_attended = dot(w_o, branch, 1, 1).astype(BF)
        grad_attended = to_heads(plan, grad_attended.reshape(4, HEAD, tok_rows))
        if level == 0:
            far_b, far_a = together(far[mlp_rows : 2 * mlp_rows], far_a)
            far_b = plan.far(far_b)
            grad_attended, far_a = together(grad_attended, far_a)
        elif level == LAYERS - 1:
            grad_attended, last = together(grad_attended, last)
            last = from_block_order(plan, (middle + last).astype(BF))
            other = plan.far(last)
        grad_q, grad_k, grad_v = attend_back(
            where_all, first_query, heads, grad_attended, out, log_total
        )
        if level == 0:
            far_c = jnp.concatenate([far_attn, far[2 * mlp_rows :]], axis=0)
            far_c, far_b = together(far_c, far_b)
            far_c = plan.far(far_c)
            grad_q, far_b = together(grad_q, far_b)
        elif level == LAYERS - 1:
            grad_q, other = together(grad_q, other)
            last = to_pack(last, other)
        grad_k = more_keys_sum(plan, grad_k)
        grad_v = more_keys_sum(plan, grad_v)
        if level > 0:
            grad_v = [0.5 * block for block in grad_v]
            if carried is None:
                carried = grad_v
            else:
                carried = [left + right for left, right in zip(carried, grad_v)]
        else:
            grad_v = [left + right for left, right in zip(grad_v, carried)]
        grad_heads = [
            jnp.stack(
                [
                    turn(grad_q[k], cos_all[k], -sine_all[k]).astype(BF),
                    turn(grad_k[k], cos_all[k], -sine_all[k]).astype(BF),
                    grad_v[k].astype(BF),
                ]
            )
            for k in range(4)
        ]
        grad_qkv = from_heads(plan, grad_heads).reshape(2, 2, 3, HEAD, tok_rows)
        grad_qkv = jnp.swapaxes(grad_qkv, 1, 2).reshape(-1, tok_rows)
        if level == 0:
            mine_first, far = far_halves(sum_mlp, counts[2:])
            far_d, far_c = together(far[:mlp_rows], far_c)
            far_d = plan.far(far_d)
            grad_qkv, far_c = together(grad_qkv, far_c)
        elif level == LAYERS - 1:
            grad_qkv, last = together(grad_qkv, last)
            outputs = natural_rows(plan, last)
        grad_wqkv = dot(grad_qkv, normed_all, 1, 0).astype(BF)
        grad_normed = sum_rows(plan, dot(grad_qkv, w_qkv, 0, 0))
        if level == 0:
            far_e = far[mlp_rows:]
            grad_normed, far_d, far_e = together(grad_normed, far_d, far_e)
            cut = qkv_rows + out_rows
            got = jnp.concatenate([far_c[:cut], far_a, far_b, far_c[cut:]], axis=0).astype(F32)
            mine = jnp.concatenate([mine_attn, mine_mlp], axis=0)
            grads[1] = weight_grads(*core_halves(plan, mine + got, counts))
        else:
            grad_normed, later_mlp = together(grad_normed, sum_mlp)
        grad_attn = jnp.concatenate([grad_wqkv, grad_wo], axis=0)
        sum_attn = columns_sum(plan, grad_attn, False)
        gain_rows[level], through = norm_back(
            stream, scale_attn, gain_full[level : level + 1], grad_normed
        )
        grad_stream = grad_middle + through

    rows = from_block_order(plan, grad_stream.astype(BF))
    gain_sum = jnp.concatenate(gain_rows + [jnp.zeros((12, model), F32)], axis=0)
    gain_near = plan.near(gain_sum)
    other, gain_near, far_e = together(plan.far(rows), gain_near, far_e)
    far_e = plan.far(far_e)
    group_rows = tok_rows // plan.ctx
    owner_grid = owner_order[0].reshape(plan.ctx, plan.ctx, group_rows)
    local_rows = (
        lax.dynamic_index_in_dim(owner_grid, plan.x, 1, False) - plan.x * tok_rows
    ).reshape(tok_rows)
    local_rows = local_rows ^ (plan.part * part_rows)
    gain_sum = columns_sum(plan, gain_sum + gain_near, True)
    mine, far = far_halves(sum_attn, counts[:2])
    far = jnp.concatenate([far, gain_sum.astype(BF)], axis=0)
    block, far_e, far = together(to_pack(rows, other), far_e, far)
    far = plan.far(far)
    slots = block[local_rows]
    grad_tokens = lax.all_to_all(slots, "ctx", split_axis=0, concat_axis=0, tiled=True)

    got = jnp.concatenate([far_d, far_e], axis=0).astype(F32)
    rest = core_halves(plan, mine_first + got, counts[2:])
    grad_tokens, far = together(grad_tokens, far)
    grad_tokens = grad_tokens.astype(F32)
    total = jnp.concatenate([mine, gain_sum], axis=0) + far.astype(F32)
    first = core_halves(plan, total, [qkv_rows, out_rows, gain_sum.shape[0]])
    total = first[2][0] + first[2][1]
    grads[0] = weight_grads(first[0], first[1], *rest)

    stacked = [jnp.stack([grads[level][i] for level in range(LAYERS)]) for i in range(7)]
    return (
        outputs,
        grad_tokens,
        total[:2],
        stacked[0],
        stacked[1],
        stacked[2],
        stacked[3],
        total[2:4],
        stacked[4],
        stacked[5],
        stacked[6],
    )


def solution(mesh):
    columns = P(None, ("fsdp", "ctx"), "tp")
    rows = P(None, "tp", ("fsdp", "ctx"))
    gain = P(None, ("fsdp", "ctx"))
    tokens = P(("fsdp", "ctx"), None)
    return jax.shard_map(
        local,
        mesh=mesh,
        in_specs=(
            tokens,
            tokens,
            P("fsdp", None),
            P("fsdp", None),
            gain,
            columns,
            columns,
            columns,
            rows,
            gain,
            columns,
            columns,
            rows,
        ),
        out_specs=(
            tokens,
            tokens,
            gain,
            columns,
            columns,
            columns,
            rows,
            gain,
            columns,
            columns,
            rows,
        ),
        check_vma=False,
    )
```

```python
import functools

import jax
import jax.numpy as jnp
from jax import lax
from jax.experimental import pallas as pl
from jax.experimental.pallas import tpu as pltpu
from jax.sharding import PartitionSpec as P

HEAD = 64
HALF = HEAD // 2
LAYERS = 2
EPS = 1e-05
THETA = 10000.0
NEG = -1e30
BF = jnp.bfloat16
F32 = jnp.float32
IN_VMEM = pl.BlockSpec(memory_space=pltpu.VMEM)
IN_SMEM = pl.BlockSpec(memory_space=pltpu.SMEM)


def dot(left, right, left_dim, right_dim):
    return lax.dot_general(
        left, right, (((left_dim,), (right_dim,)), ((), ())), preferred_element_type=F32
    )


def mm(left, right):
    return jnp.dot(left, right, preferred_element_type=F32)


class Plan:
    def __init__(self):
        self.fsdp = lax.axis_size("fsdp")
        self.ctx = lax.axis_size("ctx")
        self.tp = lax.axis_size("tp")
        self.high = self.fsdp // 2
        f = lax.axis_index("fsdp")
        z = lax.axis_index("tp")
        self.c = f % 2
        self.fh = f // 2
        self.x = lax.axis_index("ctx")
        self.zl = z % 2
        self.zp = z // 2
        self.ci = self.x % 4
        self.part = self.c * 2 + self.zl
        self.peers = self.high * self.ctx

    def core(self, value):
        return lax.ppermute(value, "fsdp", [(i, i ^ 1) for i in range(self.fsdp)])

    def near(self, value):
        return lax.ppermute(value, "tp", [(i, i ^ 1) for i in range(self.tp)])

    def far(self, value):
        return lax.ppermute(value, "tp", [(i, i ^ 2) for i in range(self.tp)])

    def side(self, value, k):
        return lax.ppermute(value, "ctx", [(i, i ^ k) for i in range(self.ctx)])

    def high_fsdp(self, value, k):
        return lax.ppermute(value, "fsdp", [(i, i ^ (2 * k)) for i in range(self.fsdp)])


def flip_list(blocks, index):
    bit = 1
    while bit < len(blocks):
        on = (index & bit) != 0
        blocks = [jnp.where(on, blocks[i ^ bit], blocks[i]) for i in range(len(blocks))]
        bit *= 2
    return blocks


def place(blocks, index, axis):
    width = blocks[0].shape[axis]
    shape = list(blocks[0].shape)
    shape[axis] = width * len(blocks)
    full = jnp.zeros(shape, blocks[0].dtype)
    for i, block in enumerate(blocks):
        full = lax.dynamic_update_slice_in_dim(full, block, (index ^ i) * width, axis)
    return full


def to_block_order(plan, rows):
    width = rows.shape[1] // (2 * plan.peers)
    parts = []
    for h in range(plan.high):
        for x in range(plan.ctx):
            for c in range(2):
                start = ((h * 2 + c) * plan.ctx + x) * width
                parts.append(rows[:, start : start + width])
    return jnp.concatenate(parts, axis=1)


def from_block_order(plan, rows):
    width = rows.shape[1] // (2 * plan.peers)
    parts = []
    for h in range(plan.high):
        for c in range(2):
            for x in range(plan.ctx):
                start = ((h * plan.ctx + x) * 2 + c) * width
                parts.append(rows[:, start : start + width])
    return jnp.concatenate(parts, axis=1)


def gather_rows(plan, rows):
    pair = jnp.concatenate([rows, plan.near(rows)], axis=0)
    return jnp.concatenate([pair, plan.core(pair)], axis=0)


def sum_rows(plan, partial):
    half = partial.shape[0] // 2
    pair = partial[:half] + plan.core(partial[half:].astype(BF)).astype(F32)
    half = half // 2
    return pair[:half] + plan.near(pair[half:].astype(BF)).astype(F32)


def natural_rows(plan, rows):
    count = rows.shape[0] // 4
    parts = [
        lax.dynamic_slice_in_dim(rows, (plan.part ^ i) * count, count, 0) for i in range(4)
    ]
    return jnp.concatenate(parts, axis=0)


def own_columns(plan, halves):
    keep = lax.dynamic_index_in_dim(halves, plan.c, 0, False)
    got = plan.core(lax.dynamic_index_in_dim(halves, 1 - plan.c, 0, False))
    return jnp.where(
        plan.c == 0,
        jnp.concatenate([keep, got], axis=1),
        jnp.concatenate([got, keep], axis=1),
    )


def all_columns(plan, rows, direct):
    if direct and plan.peers == 4:
        return place([rows] + [plan.side(rows, k) for k in range(1, 4)], plan.x, 1)
    full = lax.all_gather(rows, "ctx", axis=1, tiled=True)
    if plan.high > 1:
        parts = [full] + [plan.high_fsdp(full, k) for k in range(1, plan.high)]
        full = place(parts, plan.fh, 1)
    return full


def columns_sum(plan, grad, direct):
    if plan.high > 1:
        width = grad.shape[1] // plan.high
        parts = [
            lax.dynamic_slice_in_dim(grad, (plan.fh ^ k) * width, width, 1)
            for k in range(plan.high)
        ]
        grad = parts[0]
        for k in range(1, plan.high):
            grad = grad + plan.high_fsdp(parts[k], k)
    if direct and plan.ctx == 4:
        width = grad.shape[1] // 4
        parts = [
            lax.dynamic_slice_in_dim(grad, (plan.x ^ k) * width, width, 1) for k in range(4)
        ]
        total = parts[0].astype(F32)
        for k in range(1, 4):
            total = total + plan.side(parts[k], k).astype(F32)
        return total
    return lax.psum_scatter(grad, "ctx", scatter_dimension=1, tiled=True)


def together(value, *others):
    many = isinstance(value, list)
    got = lax.optimization_barrier((*value, *others) if many else (value, *others))
    count = len(value) if many else 1
    first = list(got[:count]) if many else got[0]
    return (first, *got[count:])


def with_far(own, far, counts):
    parts = []
    start = 0
    for rows in counts:
        parts += [own[start : start + rows], far[start : start + rows]]
        start += rows
    return jnp.concatenate(parts, axis=0)


def far_halves(total, counts):
    mine, far = [], []
    start = 0
    for rows in counts:
        mine.append(total[start : start + rows])
        far.append(total[start + rows : start + 2 * rows])
        start += 2 * rows
    return jnp.concatenate(mine, axis=0).astype(F32), jnp.concatenate(far, axis=0).astype(BF)


def core_halves(plan, own, counts):
    width = own.shape[1]
    left, right = own[:, : width // 2], own[:, width // 2 :]
    kept = jnp.where(plan.c == 0, left, right)
    got = plan.core(jnp.where(plan.c == 0, right, left).astype(BF)).astype(F32)
    low = jnp.where(plan.c == 0, kept, got)
    high = jnp.where(plan.c == 0, got, kept)
    out = []
    start = 0
    for rows in counts:
        out.append((low[start : start + rows], high[start : start + rows]))
        start += rows
    return out


def split_hidden(weight):
    return weight.reshape(2, weight.shape[0] // 2, weight.shape[1])


def turn(values, cos_tab, sine_tab):
    first, second = values[..., :HALF, :], values[..., HALF:, :]
    return jnp.concatenate(
        [first * cos_tab - second * sine_tab, second * cos_tab + first * sine_tab], axis=-2
    )


def to_heads(plan, values):
    got = [lax.dynamic_index_in_dim(values, plan.ci, 0, False)]
    for k in range(1, 4):
        got.append(plan.side(lax.dynamic_index_in_dim(values, plan.ci ^ k, 0, False), k))
    return got


def from_heads(plan, blocks):
    got = [blocks[0]] + [plan.side(blocks[k], k) for k in range(1, 4)]
    return place([block[None] for block in got], plan.ci, 0)


def more_keys(plan, blocks):
    full = list(blocks)
    for m in range(1, plan.ctx // 4):
        full += [plan.side(block, 4 * m) for block in blocks]
    return full


def more_keys_sum(plan, blocks):
    total = list(blocks[:4])
    for m in range(1, plan.ctx // 4):
        total = [total[k] + plan.side(blocks[4 * m + k], 4 * m) for k in range(4)]
    return total


def seen(first_row, part, key_block, query_block, size):
    turned = part * (size // 4)
    key = key_block * size + (lax.broadcasted_iota(jnp.int32, (size, 1), 0) ^ turned)
    query = query_block * size + (lax.broadcasted_iota(jnp.int32, (1, size), 1) ^ turned)
    return (key <= query) & (key >= first_row)


def attend_kernel(count, place_ref, first_ref, *refs):
    blocks, (out_ref, low_ref, lse_ref, kt_ref, v_ref) = refs[:count], refs[count:]
    size = blocks[0].shape[2]
    x, part = place_ref[0], place_ref[1]
    for k in range(count):
        kt_ref[x ^ k] = blocks[k][1].T
        v_ref[x ^ k] = blocks[k][2]
    for k in range(4):
        block = x ^ k
        query = blocks[k][0] * BF(HEAD ** (-0.5))
        first_row = first_ref[k]

        def step(kb, carry):
            peak, total, acc = carry
            s = mm(kt_ref[kb], query)
            s = jnp.where(seen(first_row, part, kb, block, size), s, NEG)
            top = jnp.maximum(peak, jnp.max(s, axis=0, keepdims=True))
            p = jnp.exp(s - top)
            fade = jnp.exp(peak - top)
            total = fade * total + jnp.sum(p, axis=0, keepdims=True)
            return top, total, fade * acc + mm(v_ref[kb], p.astype(BF))

        start = (
            jnp.full((1, size), NEG, F32),
            jnp.zeros((1, size), F32),
            jnp.zeros((HEAD, size), F32),
        )
        peak, total, acc = lax.fori_loop(place_ref[2 + block], block + 1, step, start)
        acc = acc / total
        out_ref[k] = acc
        low_ref[k] = acc.astype(BF)
        lse_ref[k] = peak + jnp.log(total)


def attend(where_all, first_query, blocks):
    count = len(blocks)
    size = blocks[0].shape[2]
    return pl.pallas_call(
        functools.partial(attend_kernel, count),
        out_shape=(
            jax.ShapeDtypeStruct((4, HEAD, size), F32),
            jax.ShapeDtypeStruct((4, HEAD, size), BF),
            jax.ShapeDtypeStruct((4, 1, size), F32),
        ),
        in_specs=[IN_SMEM] + [IN_VMEM] * (1 + count),
        out_specs=(IN_VMEM,) * 3,
        scratch_shapes=[
            pltpu.VMEM((count, size, HEAD), BF),
            pltpu.VMEM((count, HEAD, size), BF),
        ],
        name="attend",
    )(where_all, first_query, *blocks)


def back_kernel(count, place_ref, first_ref, out_ref, lse_ref, *refs):
    blocks, grads = refs[:count], refs[count : count + 4]
    dq_ref, dk_ref, dv_ref, kt_ref, vt_ref, k_ref, dks_ref, dvs_ref = refs[count + 4 :]
    size = blocks[0].shape[2]
    x, part = place_ref[0], place_ref[1]
    for k in range(count):
        kt_ref[x ^ k] = blocks[k][1].T
        vt_ref[x ^ k] = blocks[k][2].T
        k_ref[x ^ k] = blocks[k][1]
    dks_ref[...] = jnp.zeros_like(dks_ref)
    dvs_ref[...] = jnp.zeros_like(dvs_ref)
    for k in range(4):
        block = x ^ k
        query = blocks[k][0] * BF(HEAD ** (-0.5))
        query_t = query.T
        grad = grads[k][...]
        grad_t = grad.T
        delta = jnp.sum(grad.astype(F32) * out_ref[k], axis=0, keepdims=True)
        lse = lse_ref[k]
        first_row = first_ref[k]

        def step(kb, dq):
            s = mm(kt_ref[kb], query)
            p = jnp.where(seen(first_row, part, kb, block, size), jnp.exp(s - lse), 0.0)
            dp = mm(vt_ref[kb], grad)
            ds = (p * (dp - delta)).astype(BF)
            dvs_ref[kb] += mm(p.astype(BF), grad_t)
            dks_ref[kb] += mm(ds, query_t)
            return dq + mm(k_ref[kb], ds)

        dq = lax.fori_loop(
            place_ref[2 + block], block + 1, step, jnp.zeros((HEAD, size), F32)
        )
        dq_ref[k] = dq * HEAD ** (-0.5)
    for k in range(count):
        dk_ref[k] = dks_ref[x ^ k].T
        dv_ref[k] = dvs_ref[x ^ k].T


def attend_back(where_all, first_query, blocks, grads, out, log_total):
    count = len(blocks)
    size = blocks[0].shape[2]
    return pl.pallas_call(
        functools.partial(back_kernel, count),
        out_shape=(
            jax.ShapeDtypeStruct((4, HEAD, size), F32),
            jax.ShapeDtypeStruct((count, HEAD, size), F32),
            jax.ShapeDtypeStruct((count, HEAD, size), F32),
        ),
        in_specs=[IN_SMEM] + [IN_VMEM] * (3 + count + 4),
        out_specs=(IN_VMEM,) * 3,
        scratch_shapes=[
            pltpu.VMEM((count, size, HEAD), BF),
            pltpu.VMEM((count, size, HEAD), BF),
            pltpu.VMEM((count, HEAD, size), BF),
            pltpu.VMEM((count, size, HEAD), F32),
            pltpu.VMEM((count, size, HEAD), F32),
        ],
        name="attend_back",
    )(where_all, first_query, out, log_total, *blocks, *grads)


def norm_scale(stream):
    return lax.rsqrt(jnp.mean(stream * stream, axis=-1, keepdims=True) + EPS)


def norm_back(stream, scale, gain, grad_normed):
    weighted = grad_normed * gain
    grad_gain = jnp.sum(grad_normed * stream * scale, axis=0, keepdims=True)
    grad_stream = scale * weighted - stream * scale**3 * jnp.mean(
        weighted * stream, axis=1, keepdims=True
    )
    return (grad_gain, grad_stream)


def local(
    tokens,
    out_grad,
    segment_ids,
    owner_order,
    attn_gain,
    w_query,
    w_key,
    w_value,
    w_out,
    mlp_gain,
    w_gate,
    w_up,
    w_down,
):
    plan = Plan()
    tok_rows = tokens.shape[0]
    part_rows = tok_rows // 4
    model = tokens.shape[1]

    gains = jnp.concatenate([attn_gain, mlp_gain], axis=0)
    gains = jnp.concatenate([gains, jnp.zeros((12, gains.shape[1]), BF)], axis=0)
    qkv_rows = 3 * w_query.shape[2] // 2
    out_rows = w_out.shape[1] // 2
    mlp_rows = w_down.shape[1] // 2
    counts = [qkv_rows, out_rows] + [mlp_rows] * 3

    def own_weights(level):
        qkv = [split_hidden(w[level].T) for w in (w_query, w_key, w_value)]
        return [
            jnp.concatenate(qkv, axis=1),
            split_hidden(w_out[level]),
            split_hidden(w_gate[level].T),
            split_hidden(w_up[level].T),
            split_hidden(w_down[level]),
        ]

    groups = own_weights(0)
    own_later = []
    for level in range(1, LAYERS):
        own = own_columns(plan, jnp.concatenate(own_weights(level), axis=1))
        own_later.append(own)
    cut = qkv_rows + out_rows
    pieces = [(cut, cut + mlp_rows), (0, cut)]
    pieces += [(cut + i * mlp_rows, cut + (i + 1) * mlp_rows) for i in (1, 2)]
    def own_rows(array):
        mine = lax.dynamic_slice_in_dim(array, plan.part * part_rows, part_rows, 0)
        got = plan.core(
            lax.dynamic_slice_in_dim(array, (plan.part ^ 2) * part_rows, part_rows, 0)
        )
        return to_block_order(plan, jnp.where(plan.c == plan.zp, mine, got))

    token_rows = own_rows(tokens)
    tokens_all = gather_rows(plan, token_rows).astype(F32)
    stream = token_rows.astype(F32)
    grad_rows = own_rows(out_grad)
    grad_stream = grad_rows.astype(F32)

    own = own_columns(plan, groups[0])
    far_first = plan.far(own)
    own_rest = own_columns(plan, jnp.concatenate(groups[1:], axis=1))
    got = plan.core(gains)
    gain_pair = jnp.where(
        plan.c == 0,
        jnp.concatenate([gains, got], axis=1),
        jnp.concatenate([got, gains], axis=1),
    )
    own_rest, far_first = together(own_rest, far_first)
    first = jnp.concatenate([own, far_first, gain_pair], axis=0)
    first = all_columns(plan, first, True)
    w_qkv, gain_full = first[: 2 * qkv_rows], first[2 * qkv_rows :].astype(F32)
    last_far = plan.far(own_rest)

    segment = jnp.where(plan.c == plan.zp, segment_ids, plan.core(segment_ids))[0]
    pack = segment.shape[0]
    index_all = jnp.arange(pack, dtype=jnp.int32)
    run_start = jnp.concatenate([jnp.ones((1,), dtype=bool), segment[1:] != segment[:-1]])
    run_first = lax.cummax(jnp.where(run_start, index_all, jnp.zeros_like(index_all)), axis=0)
    where_all = jnp.concatenate(
        [jnp.stack([plan.x, plan.part]).astype(jnp.int32), run_first[::tok_rows] // tok_rows]
    )

    def by_peer(row):
        grid = row.reshape(plan.ctx, 4, part_rows)
        blocks = [lax.dynamic_index_in_dim(grid, plan.x ^ k, 0, False) for k in range(4)]
        grid = jnp.stack(blocks)
        return jnp.concatenate(flip_list([grid[:, i] for i in range(4)], plan.part), axis=1)

    positions = by_peer((index_all - run_first).astype(F32))
    first_query = by_peer(run_first)[:, None, :]
    frequency = THETA ** (-(jnp.arange(HALF, dtype=F32) * 2.0 / HEAD))
    angles = frequency[None, :, None] * positions[:, None, :]
    cos_all, sine_all = jnp.cos(angles), jnp.sin(angles)
    cos_own, sine_own = cos_all[0], sine_all[0]

    full = [(w_qkv, None, None)]
    kept = []
    first_values = None
    for level in range(LAYERS):
        w_qkv, w_o, w_mlp = full[level]
        width = 2 * mlp_rows
        if level == 0:
            scale_all = norm_scale(tokens_all)
            scale_attn = scale_all[:part_rows]
            normed_all = (tokens_all * scale_all * gain_full[:1]).astype(BF)
        else:
            scale_attn = norm_scale(stream)
            normed = (stream * scale_attn * gain_full[level : level + 1]).astype(BF)
            normed_all = gather_rows(plan, normed)
        qkv = dot(w_qkv, normed_all, 1, 1)
        if level + 1 < LAYERS:
            qkv, own_later[level], grad_rows = together(qkv, own_later[level], grad_rows)
            out_branch = gather_rows(plan, grad_rows)
        qkv = qkv.reshape(2, 3, 2, HEAD, tok_rows)
        query = turn(qkv[:, 0], cos_own, sine_own).astype(BF)
        key = turn(qkv[:, 1], cos_own, sine_own).astype(BF)
        if level == 0:
            first_values = qkv[:, 2]
            mixed = first_values
        else:
            mixed = 0.5 * qkv[:, 2] + 0.5 * first_values
        heads = jnp.stack([query, key, mixed.astype(BF)], axis=2)
        heads = more_keys(plan, to_heads(plan, heads.reshape(4, 3, HEAD, tok_rows)))
        ahead = level + 1 < LAYERS
        far_next = []

        def next_far():
            nonlocal last_far
            start, end = pieces[len(far_next)]
            piece = own_later[level][start:end]
            if far_next:
                piece, far_next[-1] = together(piece, far_next[-1])
            else:
                piece, last_far = together(piece, last_far)
            return plan.far(piece)

        if level == 0:
            got = next_far()
            heads, last_far, out_branch, got = together(heads, last_far, out_branch, got)
            far_next.append(got)
            rest = with_far(own_rest, last_far, counts[1:])
            w_o = all_columns(plan, rest[: 2 * out_rows], True)
            rest = all_columns(plan, rest[2 * out_rows :], False)
            w_mlp = (rest[: 2 * width], rest[2 * width :])
        out, out_low, log_total = attend(where_all, first_query, heads)
        if ahead:
            out_low, got, w_o = together(out_low, next_far(), w_o)
            far_next.append(got)
        attended = from_heads(plan, [out_low[k] for k in range(4)])
        attended = attended.reshape(4 * HEAD, tok_rows)
        if ahead:
            attended, got = together(attended, next_far())
            far_next.append(got)
        branch = sum_rows(plan, dot(attended, w_o, 0, 0))
        if ahead:
            branch, got = together(branch, next_far())
            far_next.append(got)
        middle = stream + branch
        scale_mlp = norm_scale(middle)
        normed_mlp = (middle * scale_mlp * gain_full[2 + level : 3 + level]).astype(BF)
        normed_mlp_all = gather_rows(plan, normed_mlp)
        w_gu, w_d = w_mlp
        full[level] = (w_qkv, w_o, w_gu, w_d)
        gate_up = dot(normed_mlp_all, w_gu, 1, 1)
        gate, upward = gate_up[:, :width], gate_up[:, width:]
        hidden = (gate * jax.nn.sigmoid(gate) * upward).astype(BF)
        if ahead:
            own = own_later[level]
            w_attn = with_far(own[:cut], far_next[1], counts[:2])
            w_attn = all_columns(plan, w_attn, False)
            got = jnp.concatenate([far_next[0], far_next[2], far_next[3]], axis=0)
            rest = with_far(own[cut:], got, counts[2:])
            rest = all_columns(plan, rest, False)
            later = (rest[: 2 * width], rest[2 * width :])
            full.append((w_attn[: 2 * qkv_rows], w_attn[2 * qkv_rows :], later))
        if level < LAYERS - 1:
            result = middle + sum_rows(plan, dot(hidden, w_d, 1, 0))
        kept.append(
            (
                stream,
                scale_attn,
                normed_all,
                heads,
                out,
                log_total,
                attended,
                middle,
                scale_mlp,
                normed_mlp_all,
                gate_up,
                hidden,
            )
        )
        if level < LAYERS - 1:
            stream = result

    def to_pack(rows, other):
        mine = jnp.where(plan.c == plan.zp, rows, other)
        got = plan.core(jnp.where(plan.c == plan.zp, other, rows))
        count = rows.shape[0]
        near = plan.near(jnp.concatenate([mine, got], axis=0))
        return jnp.concatenate([mine, near[:count], got, near[count:]], axis=0)


    def weight_grads(grad_qkv, grad_wo, grad_wg, grad_wu, grad_wd):
        third = qkv_rows // 3

        def member(i):
            rows = [half[i * third : (i + 1) * third] for half in grad_qkv]
            return jnp.concatenate(rows, axis=0).T

        return (
            member(0),
            member(1),
            member(2),
            jnp.concatenate(grad_wo, axis=0),
            jnp.concatenate(grad_wg, axis=0).T,
            jnp.concatenate(grad_wu, axis=0).T,
            jnp.concatenate(grad_wd, axis=0),
        )

    grads = [None] * LAYERS
    gain_rows = [None] * (2 * LAYERS)
    carried = None
    for level in reversed(range(LAYERS)):
        (
            stream,
            scale_attn,
            normed_all,
            heads,
            out,
            log_total,
            attended,
            middle,
            scale_mlp,
            normed_mlp_all,
            gate_up,
            hidden,
        ) = kept[level]
        w_qkv, w_o, w_gu, w_d = full[level]
        width = 2 * mlp_rows
        if level == LAYERS - 1:
            branch = out_branch
        else:
            branch = gather_rows(plan, grad_stream.astype(BF))
        grad_hidden = dot(branch, w_d, 1, 1)
        gate, upward = gate_up[:, :width], gate_up[:, width:]
        sigma = jax.nn.sigmoid(gate)
        grad_gate = (grad_hidden * upward * sigma * (1.0 + gate * (1.0 - sigma))).astype(BF)
        grad_up = (grad_hidden * gate * sigma).astype(BF)
        grad_gu = jnp.concatenate([grad_gate, grad_up], axis=1)
        partial, grad_gu = together(dot(grad_gu, w_gu, 1, 0), grad_gu)
        grad_normed = sum_rows(plan, partial)
        grad_wd = dot(hidden, branch, 0, 0).astype(BF)
        grad_wgu = dot(grad_gu, normed_mlp_all, 0, 0).astype(BF)
        grad_mlp = jnp.concatenate([grad_wgu, grad_wd], axis=0)
        if level == 0:
            grad_normed, grad_mlp, sum_attn = together(grad_normed, grad_mlp, sum_attn)
        else:
            grad_normed, grad_mlp = together(grad_normed, grad_mlp)
        sum_mlp = columns_sum(plan, grad_mlp, False)
        gain_rows[2 + level], through = norm_back(
            middle, scale_mlp, gain_full[2 + level : 3 + level], grad_normed
        )
        grad_middle = grad_stream + through
        branch = gather_rows(plan, grad_middle.astype(BF))
        if level == 0:
            later_mlp, branch = together(later_mlp, branch)
            mine_mlp, far = far_halves(later_mlp, counts[2:])
            mine_attn, far_attn = far_halves(sum_attn, counts[:2])
            far_a = plan.far(far[:mlp_rows])
        if level == LAYERS - 1:
            partial, branch = together(dot(hidden, w_d, 1, 0), branch)
            last = sum_rows(plan, partial)
        grad_wo = dot(attended, branch, 1, 0).astype(BF)
        grad_attended = dot(w_o, branch, 1, 1).astype(BF)
        grad_attended = to_heads(plan, grad_attended.reshape(4, HEAD, tok_rows))
        if level == 0:
            far_b, far_a = together(far[mlp_rows : 2 * mlp_rows], far_a)
            far_b = plan.far(far_b)
            grad_attended, far_a = together(grad_attended, far_a)
        elif level == LAYERS - 1:
            grad_attended, last = together(grad_attended, last)
            last = from_block_order(plan, (middle + last).astype(BF))
            other = plan.far(last)
        grad_q, grad_k, grad_v = attend_back(
            where_all, first_query, heads, grad_attended, out, log_total
        )
        if level == 0:
            far_c = jnp.concatenate([far_attn, far[2 * mlp_rows :]], axis=0)
            far_c, far_b = together(far_c, far_b)
            far_c = plan.far(far_c)
            grad_q, far_b = together(grad_q, far_b)
        elif level == LAYERS - 1:
            grad_q, other = together(grad_q, other)
            last = to_pack(last, other)
        grad_k = more_keys_sum(plan, grad_k)
        grad_v = more_keys_sum(plan, grad_v)
        if level > 0:
            grad_v = [0.5 * block for block in grad_v]
            if carried is None:
                carried = grad_v
            else:
                carried = [left + right for left, right in zip(carried, grad_v)]
        else:
            grad_v = [left + right for left, right in zip(grad_v, carried)]
        grad_heads = [
            jnp.stack(
                [
                    turn(grad_q[k], cos_all[k], -sine_all[k]).astype(BF),
                    turn(grad_k[k], cos_all[k], -sine_all[k]).astype(BF),
                    grad_v[k].astype(BF),
                ]
            )
            for k in range(4)
        ]
        grad_qkv = from_heads(plan, grad_heads).reshape(2, 2, 3, HEAD, tok_rows)
        grad_qkv = jnp.swapaxes(grad_qkv, 1, 2).reshape(-1, tok_rows)
        if level == 0:
            mine_first, far = far_halves(sum_mlp, counts[2:])
            far_d, far_c = together(far[:mlp_rows], far_c)
            far_d = plan.far(far_d)
            grad_qkv, far_c = together(grad_qkv, far_c)
        elif level == LAYERS - 1:
            grad_qkv, last = together(grad_qkv, last)
            outputs = natural_rows(plan, last)
        grad_wqkv = dot(grad_qkv, normed_all, 1, 0).astype(BF)
        grad_normed = sum_rows(plan, dot(grad_qkv, w_qkv, 0, 0))
        if level == 0:
            far_e = far[mlp_rows:]
            grad_normed, far_d, far_e = together(grad_normed, far_d, far_e)
            cut = qkv_rows + out_rows
            got = jnp.concatenate([far_c[:cut], far_a, far_b, far_c[cut:]], axis=0).astype(F32)
            mine = jnp.concatenate([mine_attn, mine_mlp], axis=0)
            grads[1] = weight_grads(*core_halves(plan, mine + got, counts))
        else:
            grad_normed, later_mlp = together(grad_normed, sum_mlp)
        grad_attn = jnp.concatenate([grad_wqkv, grad_wo], axis=0)
        sum_attn = columns_sum(plan, grad_attn, False)
        gain_rows[level], through = norm_back(
            stream, scale_attn, gain_full[level : level + 1], grad_normed
        )
        grad_stream = grad_middle + through

    rows = from_block_order(plan, grad_stream.astype(BF))
    gain_sum = jnp.concatenate(gain_rows + [jnp.zeros((12, model), F32)], axis=0)
    gain_near = plan.near(gain_sum)
    other, gain_near, far_e = together(plan.far(rows), gain_near, far_e)
    far_e = plan.far(far_e)
    group_rows = tok_rows // plan.ctx
    owner_grid = owner_order[0].reshape(plan.ctx, plan.ctx, group_rows)
    local_rows = (
        lax.dynamic_index_in_dim(owner_grid, plan.x, 1, False) - plan.x * tok_rows
    ).reshape(tok_rows)
    local_rows = local_rows ^ (plan.part * part_rows)
    gain_sum = columns_sum(plan, gain_sum + gain_near, True)
    mine, far = far_halves(sum_attn, counts[:2])
    far = jnp.concatenate([far, gain_sum.astype(BF)], axis=0)
    slots, far_e, far = together(to_pack(rows, other)[local_rows], far_e, far)
    far = plan.far(far)
    grad_tokens = lax.all_to_all(slots, "ctx", split_axis=0, concat_axis=0, tiled=True)

    got = jnp.concatenate([far_d, far_e], axis=0).astype(F32)
    rest = core_halves(plan, mine_first + got, counts[2:])
    grad_tokens, far = together(grad_tokens, far)
    grad_tokens = grad_tokens.astype(F32)
    total = jnp.concatenate([mine, gain_sum], axis=0) + far.astype(F32)
    first = core_halves(plan, total, [qkv_rows, out_rows, gain_sum.shape[0]])
    total = first[2][0] + first[2][1]
    grads[0] = weight_grads(first[0], first[1], *rest)

    stacked = [jnp.stack([grads[level][i] for level in range(LAYERS)]) for i in range(7)]
    return (
        outputs,
        grad_tokens,
        total[:2],
        stacked[0],
        stacked[1],
        stacked[2],
        stacked[3],
        total[2:4],
        stacked[4],
        stacked[5],
        stacked[6],
    )


def solution(mesh):
    columns = P(None, ("fsdp", "ctx"), "tp")
    rows = P(None, "tp", ("fsdp", "ctx"))
    gain = P(None, ("fsdp", "ctx"))
    tokens = P(("fsdp", "ctx"), None)
    return jax.shard_map(
        local,
        mesh=mesh,
        in_specs=(
            tokens,
            tokens,
            P("fsdp", None),
            P("fsdp", None),
            gain,
            columns,
            columns,
            columns,
            rows,
            gain,
            columns,
            columns,
            rows,
        ),
        out_specs=(
            tokens,
            tokens,
            gain,
            columns,
            columns,
            columns,
            rows,
            gain,
            columns,
            columns,
            rows,
        ),
        check_vma=False,
    )
```
